32 devices in a mesh: dp: 8 (over z, x), seq: 4 (over y, core).
Axes of the slice: x: 2, y: 2, z: 4, core: 2. Of those that a mesh axis runs over, the one named last changes fastest.
Arguments:
- layer_in: bfloat16 [8192, 2048], P(('dp', 'seq')), may hold values from -6 to 6
- out_grad: bfloat16 [8192, 2048], P(('dp', 'seq')), may hold values from -6 to 6
- seq_start: int32 [8, 4], P('dp'), may hold values from 0 to 1, as said below
- norm1_gain: bfloat16 [2048], P(('dp', 'seq')), may hold values from 0.25 to 1.75
- norm1_shift: bfloat16 [2048], P(('dp', 'seq')), may hold values from -3 to 3
- proj_in: bfloat16 [2048, 12288], P(('dp', 'seq')), may hold values from -0.125 to 0.125
- proj_out: bfloat16 [4096, 2048], P(('dp', 'seq')), may hold values from -0.125 to 0.125
- norm2_gain: bfloat16 [2048], P(('dp', 'seq')), may hold values from 0.25 to 1.75
- norm2_shift: bfloat16 [2048], P(('dp', 'seq')), may hold values from -3 to 3
- ffn_up: bfloat16 [2048, 4096], P(('dp', 'seq')), may hold values from -0.125 to 0.125
- ffn_down: bfloat16 [4096, 2048], P(('dp', 'seq')), may hold values from -0.125 to 0.125
Outputs:
- layer_out: bfloat16 [8192, 2048], P(('dp', 'seq'))
- in_grad: bfloat16 [8192, 2048], P(('dp', 'seq'))
- norm1_gain_grad: float32 [2048], P(('dp', 'seq'))
- norm1_shift_grad: float32 [2048], P(('dp', 'seq'))
- proj_in_grad: float32 [2048, 12288], P(('dp', 'seq'))
- proj_out_grad: float32 [4096, 2048], P(('dp', 'seq'))
- norm2_gain_grad: float32 [2048], P(('dp', 'seq'))
- norm2_shift_grad: float32 [2048], P(('dp', 'seq'))
- ffn_up_grad: float32 [2048, 4096], P(('dp', 'seq'))
- ffn_down_grad: float32 [4096, 2048], P(('dp', 'seq'))
The draws below stay inside these ranges and needn't reach their ends.
Inputs may be any that keep to these rules, and one draw needn't show every extreme that they name: `seq_start`: each group's first block is 1, and a 1 stands only at even block indices, so every sequence covers an even number of blocks of 256 tokens.
All inputs are finite; a program needn't handle non-finite values.
Results may differ from the reference program's by a relative error of at most 0.014.
The reference program's roundings to bfloat16 on the way count: a program that leaves them out, or rounds other values in their place, can miss the bound.
Values may be sent and summed in bfloat16 or wider, within the bound.
No kernel may reach another device: no remote copies, remote signals or barrier semaphores. Data moves between devices by JAX's collectives and lax.ppermute only.
A program may use at most 336 MiB of HBM per device.

```python
import jax
import jax.numpy as jnp
from jax import lax

D = 2048
HEADS = 8
VD = 4096
FF = 4096
TOK_DEV = 256
DK = 256
DV = 512
QKVG = 12288
GROUPS = 8
BLOCKS = 4
TOKENS = 8192


def draw_seq_start(key, part):
    random_bits = jax.random.randint(jax.random.fold_in(key, 17), (GROUPS, BLOCKS), 0, 2)
    column = jnp.arange(BLOCKS)[None, :]
    even_flag = jnp.where(column % 2 == 0, random_bits, 0)
    result = jnp.where(column == 0, 1, even_flag)
    return result.astype(jnp.int32)


def with_spikes(array, own_key, source, target, parts, factor):
    def block_of(dim):
        return (jnp.arange(array.shape[dim]) // (array.shape[dim] // parts)).reshape((-1,) + (1,) * (array.ndim - 1 - dim))

    near = jax.random.permutation(own_key, parts)[block_of(target)]
    far = (block_of(target) + parts // 2) % parts
    return jnp.where((block_of(source) == near) | (block_of(source) == far), factor * array, array)


def level_of(own_key, shape, pieces, least, largest):
    factor_of = 1.0
    for position, shards_of in pieces:
        steps = jax.random.uniform(jax.random.fold_in(jax.random.fold_in(own_key, 6), position), (shards_of,), jnp.float32, least / len(pieces), largest / len(pieces))
        factor_of = factor_of * jnp.repeat(jnp.exp(steps), shape[position] // shards_of).reshape((-1,) + (1,) * (len(shape) - 1 - position))
    return factor_of


def gaussian(rng, extent, scale, most, pieces=(), kind=jnp.bfloat16):
    drawn = jax.random.normal(rng, extent, jnp.float32) * scale
    if len(pieces) > 0:
        drawn = level_of(rng, extent, pieces, -0.22, 0.18) * drawn
    return jnp.clip(drawn, min=-most, max=most).astype(kind)


def bell_draw_with(key, shape, scale, limit, cuts, heavy, kind=jnp.bfloat16):
    array = scale * jax.random.normal(key, shape, jnp.float32)
    if cuts:
        array = array * level_of(key, shape, cuts, -0.22, 0.18)
    return jnp.clip(with_spikes(array, jax.random.fold_in(key, 3), *heavy), -limit, limit).astype(kind)


def setup_inputs(seed: int = 0) -> dict:
    splits = jax.random.split(jax.random.key(seed), 12)
    return {
        "layer_in": bell_draw_with(splits[0], (TOKENS, D), 1.0, 6.0, ((0, 32),), (0, 1, 32, 2.75)),
        "out_grad": bell_draw_with(splits[1], (TOKENS, D), 1.0, 6.0, ((0, 32),), (0, 1, 32, 2.75)),
        "seq_start": draw_seq_start(jax.random.fold_in(splits[11], 71), 0),
        "norm1_gain": jnp.clip(1.0 + 0.15 * jax.random.normal(splits[3], (D,), jnp.float32), 0.25, 1.75).astype(jnp.bfloat16),
        "norm1_shift": gaussian(splits[4], (D,), 0.5, 3.0, ((0, 32),)),
        "proj_in": gaussian(splits[5], (D, QKVG), D ** -0.5, 0.125, ((0, 32),)),
        "proj_out": gaussian(splits[6], (VD, D), (VD // 2) ** -0.5, 0.125, ((0, 32),)),
        "norm2_gain": jnp.clip(1.0 + 0.15 * jax.random.normal(splits[7], (D,), jnp.float32), 0.25, 1.75).astype(jnp.bfloat16),
        "norm2_shift": gaussian(splits[8], (D,), 0.5, 3.0, ((0, 32),)),
        "ffn_up": gaussian(splits[9], (D, FF), D ** -0.5, 0.125, ((0, 32),)),
        "ffn_down": gaussian(splits[10], (FF, D), (FF // 2) ** -0.5, 0.125, ((0, 32),)),
    }


@jax.custom_vjp
def low(v):
    return lax.optimization_barrier(v.astype(jnp.bfloat16)).astype(jnp.float32)

@jax.custom_vjp
def low_back(v):
    return v

def low_keep(v):
    return (low(v), None)

def low_pass(kept, grad):
    return (grad,)

def back_keep(v):
    return (v, None)

def back_low(kept, grad):
    return (low(grad),)
low.defvjp(low_keep, low_pass)
low_back.defvjp(back_keep, back_low)

def layer_norm(rows, row_gain, row_shift):
    average = lax.optimization_barrier(jnp.mean(rows, axis=-1, keepdims=True))
    centred = rows - average
    spread = lax.optimization_barrier(jnp.mean(centred * centred, axis=-1, keepdims=True))
    return centred * lax.rsqrt(spread + 1e-05) * row_gain + row_shift

def gate_norm(gate_pre, retained):
    average = lax.optimization_barrier(jnp.mean(retained, axis=-1, keepdims=True))
    centred = retained - average
    spread = jnp.maximum(lax.optimization_barrier(jnp.mean(centred * centred, axis=-1, keepdims=True)), 0.25)
    normed = centred * lax.rsqrt(spread + 1e-05)
    swish = gate_pre * jax.nn.sigmoid(gate_pre)
    return swish * normed.reshape(gate_pre.shape)

def rotate(heads_in, cosine, sine):
    half_width = heads_in.shape[-1] // 2
    first = heads_in[..., :half_width]
    second = heads_in[..., half_width:]
    return jnp.concatenate([first * cosine - second * sine, first * sine + second * cosine], axis=-1)

def rotary_tables(positions, head_width):
    half_width = head_width // 2
    factor = jnp.power(10000.0, -jnp.arange(half_width, dtype=jnp.float32) / (half_width - 1))
    angles = positions.astype(jnp.float32)[:, None] * factor[None, :]
    return (jnp.cos(angles)[:, None, :], jnp.sin(angles)[:, None, :])

def decay_logs(count):
    return jnp.log(1.0 - jnp.exp2(-5.0 - jnp.arange(count, dtype=jnp.float32)))

def causal_decay(steps_here, log_decay):
    distance = steps_here[:, None] - steps_here[None, :]
    lower = distance[None] >= 0.0
    safe_distance = jnp.where(lower, distance[None], 0.0)
    return jnp.where(lower, jnp.exp(safe_distance * log_decay[:, None, None]), 0.0)

def high_dot(left, right):
    return jnp.dot(left, right, precision=lax.Precision.HIGHEST, preferred_element_type=jnp.float32)

def retention(queries, keys, values, starts):
    highest = lax.Precision.HIGHEST
    steps_here = jnp.arange(TOK_DEV, dtype=jnp.float32)
    log_decay = decay_logs(HEADS)
    decay_query = jnp.exp((steps_here + 1.0)[:, None] * log_decay[None, :])
    decay_key = jnp.exp((TOK_DEV - 1.0 - steps_here)[:, None] * log_decay[None, :])
    decay_mask = causal_decay(steps_here, log_decay)
    query_five = queries.reshape(GROUPS, BLOCKS, TOK_DEV, HEADS, DK)
    key_five = keys.reshape(GROUPS, BLOCKS, TOK_DEV, HEADS, DK)
    value_five = values.reshape(GROUPS, BLOCKS, TOK_DEV, HEADS, DV)
    query_decay = low(query_five * decay_query[:, :, None])
    key_decay = low(key_five * decay_key[:, :, None])
    raw_scores = low_back(jnp.einsum('gsihd,gsjhd->gshij', query_five, key_five, precision=highest))
    scores = low(raw_scores * decay_mask)
    intra = jnp.einsum('gshij,gsjhe->gsihe', scores, value_five, precision=highest)
    local_state = low_back(jnp.einsum('gsjhd,gsjhe->gshde', key_decay, value_five, precision=highest))
    keep_state = 1.0 - starts.astype(jnp.float32)
    block_decay = jnp.exp(TOK_DEV * log_decay)
    local_moved = jnp.moveaxis(local_state, 1, 0)

    def advance(carry, items):
        keep_col, local_col = items
        state_in = keep_col[:, None, None, None] * carry
        return (block_decay[None, :, None, None] * state_in + local_col, state_in)
    start_carry = jnp.zeros_like(local_moved[0])
    _, states = lax.scan(advance, start_carry, (keep_state.T.astype(local_moved.dtype), local_moved))
    states = jnp.moveaxis(states, 0, 1)
    inter = jnp.einsum('gsihd,gshde->gsihe', query_decay, low(states), precision=highest)
    return (intra + inter).reshape(GROUPS * BLOCKS * TOK_DEV, HEADS, DV)

def forward(rows, gain_one, shift_one, proj_in, proj_out, gain_two, shift_two, ffn_up, ffn_down, starts):
    tok_total = rows.shape[0]
    hidden_one = low(layer_norm(rows, gain_one, shift_one))
    projected = high_dot(hidden_one, proj_in)
    query_pre = low_back(projected[:, :D]).reshape(tok_total, HEADS, DK)
    key_pre = low_back(projected[:, D:2 * D]).reshape(tok_total, HEADS, DK)
    value_pre = low_back(projected[:, 2 * D:2 * D + VD])
    gate_pre = low_back(projected[:, 2 * D + VD:])
    positions = jnp.arange(tok_total, dtype=jnp.int32) % jnp.int32(BLOCKS * TOK_DEV)
    cosine, sine = rotary_tables(positions, DK)
    queries = low(rotate(query_pre, cosine, sine))
    keys = low(rotate(key_pre, cosine, sine) * DK ** (-0.5))
    values = low(value_pre).reshape(tok_total, HEADS, DV)
    retained = low_back(retention(queries, keys, values, starts))
    mixed = low(gate_norm(gate_pre, retained))
    middle = rows + low_back(high_dot(mixed, proj_out))
    hidden_two = low(layer_norm(middle, gain_two, shift_two))
    up_pre = low_back(high_dot(hidden_two, ffn_up))
    active = low(jax.nn.gelu(up_pre, approximate=False))
    return middle + low_back(high_dot(active, ffn_down))

def reference(layer_in, out_grad, seq_start, norm1_gain, norm1_shift, proj_in, proj_out, norm2_gain, norm2_shift, ffn_up, ffn_down):
    params = [layer_in, norm1_gain, norm1_shift, proj_in, proj_out, norm2_gain, norm2_shift, ffn_up, ffn_down]
    params = [item.astype(jnp.float32) for item in params]

    def whole(*items):
        return forward(*items, seq_start)
    result, pullback = jax.vjp(whole, *params)
    grads = pullback(out_grad.astype(jnp.float32))
    return (result.astype(jnp.bfloat16), grads[0].astype(jnp.bfloat16), grads[1], grads[2], grads[3], grads[4], grads[5], grads[6], grads[7], grads[8])
```

```python
import jax
import jax.numpy as jnp
from jax import lax
from jax.sharding import PartitionSpec as P

D = 2048
HEADS = 8
VD = 4096
DK = 256
DV = 512
BOTH = ("dp", "seq")
f32 = jnp.float32
bf16 = jnp.bfloat16


def layer_norm(rows, row_gain, row_shift):
    average = jnp.mean(rows, axis=-1, keepdims=True)
    centred = rows - average
    spread = jnp.mean(centred * centred, axis=-1, keepdims=True)
    return centred * lax.rsqrt(spread + 1e-05) * row_gain + row_shift


def gate_norm(gate_pre, retained):
    average = jnp.mean(retained, axis=-1, keepdims=True)
    centred = retained - average
    spread = jnp.maximum(jnp.mean(centred * centred, axis=-1, keepdims=True), 0.25)
    normed = centred * lax.rsqrt(spread + 1e-05)
    swish = gate_pre * jax.nn.sigmoid(gate_pre)
    return swish * normed


def gelu_exact(values):
    return jax.nn.gelu(values, approximate=False)


def rotate(heads_in, cosine, sine):
    half_width = heads_in.shape[-1] // 2
    first = heads_in[..., :half_width]
    second = heads_in[..., half_width:]
    return jnp.concatenate(
        [first * cosine - second * sine, first * sine + second * cosine], axis=-1
    )


def dot(a, b, dims):
    return lax.dot_general(a, b, (dims, ((), ())), preferred_element_type=f32)


def seq_bits(size):
    return [1 << b for b in range(size.bit_length() - 1)]


def swap_seq(x, bit):
    size = lax.axis_size("seq")
    return lax.ppermute(x, "seq", [(i, i ^ bit) for i in range(size)])


def gather_seq(x):
    size, me = lax.axis_size("seq"), lax.axis_index("seq")
    held = x[None]
    for bit in reversed(seq_bits(size)):
        other = swap_seq(held, bit)
        upper = (me & bit) != 0
        held = jnp.where(upper, jnp.stack([other, held]), jnp.stack([held, other]))
        held = held.reshape((-1,) + x.shape) if bit == size // 2 else held
        if bit != size // 2:
            held = jnp.swapaxes(held, 0, 1).reshape((-1,) + x.shape)
    return held


def scatter_seq(x):
    size, me = lax.axis_size("seq"), lax.axis_index("seq")
    held = x
    for bit in seq_bits(size):
        pairs = held.reshape((held.shape[0] // 2, 2) + held.shape[1:])
        mine = jnp.where((me & bit) != 0, 1, 0)
        keep = lax.dynamic_index_in_dim(pairs, mine, 1, False)
        give = lax.dynamic_index_in_dim(pairs, 1 - mine, 1, False)
        held = keep.astype(f32) + swap_seq(give.astype(bf16), bit).astype(f32)
    return held[0]


def exchange_seq(x):
    return lax.all_to_all(x, "seq", 0, 0)


def gather_dp(x):
    return lax.all_gather(x, "dp", axis=0, tiled=True)


def scatter_dp(x):
    return lax.psum_scatter(x.astype(bf16), "dp", scatter_dimension=0, tiled=True)


def local(
    layer_in,
    out_grad,
    seq_start,
    norm1_gain,
    norm1_shift,
    proj_in,
    proj_out,
    norm2_gain,
    norm2_shift,
    ffn_up,
    ffn_down,
):
    S, G = lax.axis_size("seq"), lax.axis_size("dp")
    me = lax.axis_index("seq")
    T = layer_in.shape[0]
    TG = S * T
    H = HEADS // S
    QW, VW = H * DK, H * DV
    FR = ffn_down.shape[0]
    FW = G * FR

    norms = lax.all_gather(
        jnp.stack([norm1_gain, norm1_shift, norm2_gain, norm2_shift]), BOTH, axis=1, tiled=True
    ).astype(f32)
    gain_one, shift_one, gain_two, shift_two = norms

    rows_in = proj_in.shape[0]
    pieces = []
    start = 0
    for width in (QW, QW, VW, VW):
        part = proj_in[:, start : start + S * width]
        pieces.append(part.reshape(rows_in, S, width))
        start += S * width
    w_in = jnp.concatenate(pieces, axis=2).transpose(1, 0, 2)
    w_in = exchange_seq(w_in).reshape(S * rows_in, 2 * QW + 2 * VW)
    w_in = gather_dp(w_in)
    w_out = lax.ppermute(
        proj_out, BOTH, [(j * G + t, t * S + j) for j in range(S) for t in range(G)]
    )
    w_out = gather_dp(w_out)
    rows_up = ffn_up.shape[0]
    w_up = ffn_up.reshape(rows_up, G, S, FR).transpose(2, 0, 1, 3).reshape(S, rows_up, FW)
    w_up = gather_dp(exchange_seq(w_up).reshape(S * rows_up, FW))
    w_down = gather_dp(ffn_down)

    rows_full = layer_in.astype(f32)
    normed_one, norm1_back = jax.vjp(layer_norm, rows_full, gain_one, shift_one)
    hidden_one = gather_seq(normed_one.astype(bf16)).reshape(TG, D)
    cot = gather_seq(out_grad).reshape(TG, D)

    projected = dot(hidden_one, w_in, ((1,), (0,)))
    q_pre = projected[:, :QW].reshape(S, T, H, DK)
    k_pre = projected[:, QW : 2 * QW].reshape(S, T, H, DK)
    values = projected[:, 2 * QW : 2 * QW + VW].astype(bf16).reshape(S, T, H, DV)
    gate_pre = projected[:, 2 * QW + VW :].reshape(S, T, H, DV)

    half = DK // 2
    factor = jnp.power(10000.0, -jnp.arange(half, dtype=f32) / (half - 1))
    angles = jnp.arange(TG, dtype=f32)[:, None] * factor[None, :]
    cosine = jnp.cos(angles).reshape(S, T, 1, half)
    sine = jnp.sin(angles).reshape(S, T, 1, half)
    key_scale = DK ** (-0.5)
    queries = rotate(q_pre, cosine, sine).astype(bf16)
    keys = (rotate(k_pre, cosine, sine) * key_scale).astype(bf16)

    log_all = jnp.log(1.0 - jnp.exp2(-5.0 - jnp.arange(HEADS, dtype=f32)))
    log_decay = lax.dynamic_slice_in_dim(log_all, me * H, H)
    steps = jnp.arange(T, dtype=f32)
    decay_query = jnp.exp((steps + 1.0)[:, None] * log_decay[None, :])
    decay_key = jnp.exp((T - 1.0 - steps)[:, None] * log_decay[None, :])
    distance = steps[:, None] - steps[None, :]
    lower = distance[None] >= 0.0
    safe = jnp.where(lower, distance[None], 0.0)
    mask = jnp.where(lower, jnp.exp(safe * log_decay[:, None, None]), 0.0)
    block_decay = jnp.exp(T * log_decay)[:, None, None]
    keep = 1.0 - seq_start[0].astype(f32)

    query_decay = (queries.astype(f32) * decay_query[None, :, :, None]).astype(bf16)
    key_decay = (keys.astype(f32) * decay_key[None, :, :, None]).astype(bf16)

    def ein(spec, a, b):
        return jnp.einsum(spec, a, b, preferred_element_type=f32)

    raw = ein("bihd,bjhd->bhij", queries, keys)
    scores = (raw * mask[None]).astype(bf16)
    local_state = ein("bjhd,bjhe->bhde", key_decay, values)
    carry = jnp.zeros_like(local_state[0])
    states = []
    for b in range(S):
        state = keep[b] * carry
        states.append(state.astype(bf16))
        carry = block_decay * state + local_state[b]
    state_in = jnp.stack(states)
    retained = ein("bhij,bjhe->bihe", scores, values) + ein("bihd,bhde->bihe", query_decay, state_in)
    gated, gate_back = jax.vjp(gate_norm, gate_pre, retained)
    mixed = gated.astype(bf16).reshape(TG, VW)

    attn = scatter_seq(dot(mixed, w_out, ((1,), (0,))).reshape(S, T, D))
    middle = rows_full + attn
    normed_two, norm2_back = jax.vjp(layer_norm, middle, gain_two, shift_two)
    hidden_two = gather_seq(normed_two.astype(bf16)).reshape(TG, D)
    up_pre = dot(hidden_two, w_up, ((1,), (0,)))
    active_full, gelu_back = jax.vjp(gelu_exact, up_pre)
    active = active_full.astype(bf16)
    down = scatter_seq(dot(active, w_down, ((1,), (0,))).reshape(S, T, D))
    layer_out = (middle + down).astype(bf16)

    down_grad = scatter_dp(dot(active, cot, ((0,), (0,)))).astype(f32)
    grad_active = dot(cot, w_down, ((1,), (1,)))
    grad_up = gelu_back(grad_active)[0].astype(bf16)
    up_grad = scatter_dp(dot(hidden_two, grad_up, ((0,), (0,))))
    up_grad = exchange_seq(up_grad.reshape(S, rows_up, FW)).reshape(S, rows_up, G, FR)
    up_grad = up_grad.transpose(1, 2, 0, 3).reshape(rows_up, G * S * FR).astype(f32)
    grad_hidden_two = scatter_seq(dot(grad_up, w_up, ((1,), (1,))).reshape(S, T, D))
    grad_mid_part, gain_two_grad, shift_two_grad = norm2_back(grad_hidden_two)
    grad_middle = out_grad.astype(f32) + grad_mid_part

    grad_attn = gather_seq(grad_middle.astype(bf16)).reshape(TG, D)
    out_term = scatter_dp(dot(mixed, grad_attn, ((0,), (0,))))
    out_grad_w = lax.ppermute(
        out_term, BOTH, [(t * S + j, j * G + t) for j in range(S) for t in range(G)]
    ).astype(f32)
    grad_mixed = dot(grad_attn, w_out, ((1,), (1,))).reshape(S, T, H, DV)
    grad_gate, grad_ret = gate_back(grad_mixed)
    grad_gate = grad_gate.astype(bf16)
    grad_ret = grad_ret.astype(bf16)
    grad_qdecay = ein("bihe,bhde->bihd", grad_ret, state_in)
    state_grad = ein("bihd,bihe->bhde", query_decay, grad_ret)
    grad_scores = ein("bihe,bjhe->bhij", grad_ret, values)
    grad_raw = (grad_scores * mask[None]).astype(bf16)
    later = jnp.zeros_like(state_grad[0])
    laters = [None] * S
    for b in reversed(range(S)):
        laters[b] = later.astype(bf16)
        later = keep[b] * (state_grad[b] + block_decay * later)
    grad_local = jnp.stack(laters)
    grad_query = (
        ein("bhij,bjhd->bihd", grad_raw, keys) + grad_qdecay * decay_query[None, :, :, None]
    )
    grad_key = (
        ein("bhij,bihd->bjhd", grad_raw, queries)
        + ein("bjhe,bhde->bjhd", values, grad_local) * decay_key[None, :, :, None]
    )
    grad_value = ein("bhij,bihe->bjhe", scores, grad_ret) + ein(
        "bjhd,bhde->bjhe", key_decay, grad_local
    )
    grad_qpre = rotate(grad_query, cosine, -sine).astype(bf16).reshape(TG, QW)
    grad_kpre = rotate(grad_key * key_scale, cosine, -sine).astype(bf16).reshape(TG, QW)
    grad_projected = jnp.concatenate(
        [grad_qpre, grad_kpre, grad_value.astype(bf16).reshape(TG, VW), grad_gate.reshape(TG, VW)],
        axis=1,
    )
    in_term = scatter_dp(dot(hidden_one, grad_projected, ((0,), (0,))))
    in_term = exchange_seq(in_term.reshape(S, rows_in, 2 * QW + 2 * VW))
    cols = []
    start = 0
    for width in (QW, QW, VW, VW):
        part = in_term[:, :, start : start + width]
        cols.append(part.transpose(1, 0, 2).reshape(rows_in, S * width))
        start += width
    in_grad_w = jnp.concatenate(cols, axis=1).astype(f32)
    grad_hidden_one = scatter_seq(dot(grad_projected, w_in, ((1,), (1,))).reshape(S, T, D))
    grad_in_part, gain_one_grad, shift_one_grad = norm1_back(grad_hidden_one)
    in_grad = (grad_middle + grad_in_part).astype(bf16)
    norm_grads = lax.psum_scatter(
        jnp.stack([gain_one_grad, shift_one_grad, gain_two_grad, shift_two_grad]),
        BOTH,
        scatter_dimension=1,
        tiled=True,
    )
    return (
        layer_out,
        in_grad,
        norm_grads[0],
        norm_grads[1],
        in_grad_w,
        out_grad_w,
        norm_grads[2],
        norm_grads[3],
        up_grad,
        down_grad,
    )


def solution(mesh):
    rows, vector = P(BOTH, None), P(BOTH)
    in_specs = (rows, rows, P("dp", None), vector, vector, rows, rows, vector, vector, rows, rows)
    out_specs = (rows, rows, vector, vector, rows, rows, vector, vector, rows, rows)
    return jax.shard_map(local, mesh=mesh, in_specs=in_specs, out_specs=out_specs, check_vma=False)
```

```python
import functools

import jax
import jax.numpy as jnp
from jax import lax
from jax.experimental import pallas as pl
from jax.experimental.pallas import tpu as pltpu
from jax.sharding import PartitionSpec as P

D = 2048
HEADS = 8
VD = 4096
DK = 256
DV = 512
HALF = DK // 2
BOTH = ("dp", "seq")
f32 = jnp.float32
bf16 = jnp.bfloat16
ANY = pl.BlockSpec(memory_space=pl.ANY)
VMEM = pl.BlockSpec(memory_space=pltpu.VMEM)
LIMIT = 58 << 20
DEPTH = 4


def dot(a, b, dims):
    return lax.dot_general(a, b, (dims, ((), ())), preferred_element_type=f32)


def call(body, info, ins, outs, scratch=(), grid=(), in_specs=None, out_specs=None, name=None, cost=None, after=()):
    many = isinstance(outs, (list, tuple))
    n_in, n_after = len(ins), len(after)
    ins, after = list(ins), list(after)

    def inner(at, *refs):
        body(at, *refs[:n_in], *refs[n_in + n_after :])

    spec = pltpu.PrefetchScalarGridSpec(
        num_scalar_prefetch=1,
        grid=grid,
        in_specs=list(in_specs or [ANY] * n_in) + [ANY] * n_after,
        out_specs=out_specs or ([ANY] * len(outs) if many else ANY),
        scratch_shapes=list(scratch),
    )
    moved = sum(x.size * x.dtype.itemsize for x in (*ins, *(outs if many else [outs])))
    return pl.pallas_call(
        inner,
        out_shape=outs,
        grid_spec=spec,
        name=name,
        cost_estimate=pl.CostEstimate(
            flops=cost or 0, bytes_accessed=int(moved), transcendentals=0
        ),
        compiler_params=pltpu.CompilerParams(vmem_limit_bytes=LIMIT),
    )(info, *ins, *after)


def tie(x, *after):
    return pl.pallas_call(
        lambda *refs: None,
        out_shape=like(x.shape, x.dtype),
        in_specs=[ANY] * (1 + len(after)),
        out_specs=ANY,
        input_output_aliases={0: 0},
        name="tie",
    )(x, *after)


def like(shape, dtype):
    return jax.ShapeDtypeStruct(shape, dtype)


def seq_gaps(size):
    return [1 << b for b in range(size.bit_length() - 1)]


def swap_seq(x, gap):
    size = lax.axis_size("seq")
    return lax.ppermute(x, "seq", [(i, i ^ gap) for i in range(size)])


class Loads:
    def __init__(self, sems):
        self.sems, self.count, self.groups = sems, 0, {}

    def add(self, group, source, target):
        copy = pltpu.make_async_copy(source, target, self.sems.at[self.count])
        self.groups.setdefault(group, []).append(copy)
        self.count += 1
        copy.start()

    def wait(self, group):
        for copy in self.groups.pop(group, []):
            copy.wait()


def block_row(at, gap, rows):
    return pl.multiple_of((at[0] ^ gap) * rows, rows)


def gather_seq(x, *after):
    held = {0: x}
    for gap in reversed(seq_gaps(lax.axis_size("seq"))):
        new = {g ^ gap: swap_seq(part, gap) for g, part in list(held.items())}
        if after and gap == lax.axis_size("seq") // 2:
            new = {g: tie(part, *after) for g, part in new.items()}
        held.update(new)
    return held


ROWS = 128


def plain(body, ins, outs, grid, in_specs, out_specs, name, after=()):
    n_in = len(ins)

    def inner(*refs):
        body(*refs[:n_in], *refs[n_in + len(after) :])

    return pl.pallas_call(
        inner,
        out_shape=outs,
        grid=grid,
        in_specs=[*in_specs, *[ANY] * len(after)],
        out_specs=out_specs,
        name=name,
        compiler_params=pltpu.CompilerParams(vmem_limit_bytes=LIMIT),
    )(*ins, *after)


def tile_of(rows, cols):
    return pl.BlockSpec((rows, cols), lambda i: (i, 0))


def add_up(parts, dtype, after=()):
    T, C = parts[0].shape

    def body(*refs):
        total = refs[0][...].astype(f32)
        for ref in refs[1:-1]:
            total = total + ref[...].astype(f32)
        refs[-1][...] = total.astype(dtype)

    return plain(
        body,
        parts,
        like((T, C), dtype),
        (T // ROWS,),
        [tile_of(ROWS, C)] * len(parts),
        tile_of(ROWS, C),
        "add_up",
        after,
    )


def swap_odd(parts, got):
    for gap in sorted((gap for gap in parts if gap & 1), reverse=True):
        got.setdefault(gap ^ 1, []).append(swap_seq(parts[gap], 1))


def scatter_seq(parts, got, after=()):
    size = lax.axis_size("seq")
    sent = parts[0]
    bit = 2
    while bit < size:
        for gap in [gap for gap in reversed(range(size)) if gap & bit and gap % bit == 0]:
            sent = add_up([parts[gap], *got[gap]], bf16, after)
            got.setdefault(gap ^ bit, []).append(swap_seq(sent, bit))
        bit *= 2
    return [parts[0], *got[0]], sent


def norm_forward(rows, gain, shift, more=(), after=()):
    T, C = rows.shape
    wide = len(more) > 0

    def body(rows_ref, gain_ref, shift_ref, *refs):
        outs = refs[-2:] if wide else refs[-1:]
        total = rows_ref[...].astype(f32)
        for ref in refs[: len(more)]:
            total = total + ref[...].astype(f32)
        if wide:
            outs[0][...] = total
        centred = total - jnp.mean(total, axis=-1, keepdims=True)
        spread = jnp.mean(centred * centred, axis=-1, keepdims=True)
        normed = centred * lax.rsqrt(spread + 1e-05) * gain_ref[...] + shift_ref[...]
        outs[-1][...] = normed.astype(bf16)

    vector = pl.BlockSpec((1, C), lambda i: (0, 0))
    outs = ([like((T, C), f32)] if wide else []) + [like((T, C), bf16)]
    return plain(
        body,
        [rows, gain, shift, *more],
        outs,
        (T // ROWS,),
        [tile_of(ROWS, C), vector, vector] + [tile_of(ROWS, C)] * len(more),
        [tile_of(ROWS, C)] * len(outs),
        "norm_forward",
        after,
    )


def norm_backward(rows, gain, base, parts, dtypes, after=()):
    T, C = rows.shape
    n = len(parts)

    def body(rows_ref, gain_ref, base_ref, *refs):
        grad = refs[0][...].astype(f32)
        for ref in refs[1:n]:
            grad = grad + ref[...].astype(f32)
        total = rows_ref[...].astype(f32)
        centred = total - jnp.mean(total, axis=-1, keepdims=True)
        inverse = lax.rsqrt(jnp.mean(centred * centred, axis=-1, keepdims=True) + 1e-05)
        normed = centred * inverse
        inner = grad * gain_ref[...]
        pull = inner - jnp.mean(inner, axis=-1, keepdims=True)
        pull = pull - normed * jnp.mean(inner * normed, axis=-1, keepdims=True)
        result = base_ref[...].astype(f32) + inverse * pull
        for out in refs[n:-1]:
            out[...] = result.astype(out.dtype)
        sums = refs[-1]

        @pl.when(pl.program_id(0) == 0)
        def _():
            sums[...] = jnp.zeros_like(sums)

        sums[0:1, :] += jnp.sum(grad * normed, axis=0, keepdims=True)
        sums[1:2, :] += jnp.sum(grad, axis=0, keepdims=True)

    vector = pl.BlockSpec((1, C), lambda i: (0, 0))
    outs = [like((T, C), t) for t in dtypes] + [like((8, C), f32)]
    return plain(
        body,
        [rows, gain, base, *parts],
        outs,
        (T // ROWS,),
        [tile_of(ROWS, C), vector, tile_of(ROWS, C)] + [tile_of(ROWS, C)] * n,
        [tile_of(ROWS, C)] * len(dtypes) + [pl.BlockSpec((8, C), lambda i: (0, 0))],
        "norm_backward",
        after,
    )


def swap_all(x, gap):
    size = lax.axis_size("dp") * lax.axis_size("seq")
    return lax.ppermute(x, BOTH, [(i, i ^ gap) for i in range(size)])


def flat_index():
    return lax.axis_index("dp") * lax.axis_size("seq") + lax.axis_index("seq")


def gather_all(x):
    S, G = lax.axis_size("seq"), lax.axis_size("dp")
    me = flat_index()
    held = x[None, None]
    middle = None
    for gap in [S * g for g in seq_gaps(G)] + seq_gaps(S):
        axis = 0 if gap >= S else 1
        other = swap_all(held, gap)
        held = jnp.where(
            (me & gap) != 0,
            jnp.concatenate([other, held], axis=axis),
            jnp.concatenate([held, other], axis=axis),
        )
        if gap == S * G // 2:
            middle = held
    return held.reshape((G * S,) + x.shape), middle


def scatter_all(x, afters):
    me = flat_index()
    held = x
    for n, gap in enumerate(reversed(seq_gaps(x.shape[0]))):
        half = held.shape[0] // 2
        upper = (me & gap) != 0
        keep = jnp.where(upper, held[half:], held[:half])
        give = jnp.where(upper, held[:half], held[half:])
        got = swap_all(give, gap)
        if n < len(afters):
            got = tie(got, *afters[n])
        held = keep + got
    return held[0]


def cycle(size):
    depth = DEPTH
    width = size // depth
    walk = [(0, x) for x in range(width)]
    for turn, x in enumerate(reversed(range(width))):
        column = [(z, x) for z in range(1, depth)]
        walk += column if turn % 2 == 0 else column[::-1]
    return [z * width + x for z, x in walk]


def ring_moves(size):
    walk = cycle(size)
    ahead = [(walk[i], walk[(i + 1) % size]) for i in range(size)]
    return ahead, [(b, a) for a, b in ahead]


def shard_place(t, size):
    return (t % DEPTH) * (size // DEPTH) + t // DEPTH


def make_info():
    size = lax.axis_size("dp")
    walk = cycle(size)
    table = [[walk[(walk.index(i) - k) % size] for k in range(size)] for i in range(size)]
    shard = {shard_place(t, size): t for t in range(size)}
    table = [row + [shard[i] for i in row] for row in table]
    row = lax.dynamic_index_in_dim(jnp.array(table, jnp.int32), lax.axis_index("dp"), 0, False)
    return jnp.concatenate([lax.axis_index("seq").astype(jnp.int32)[None], row])


class Gather:
    def __init__(self, x):
        self.size = lax.axis_size("dp")
        self.ahead, self.back = ring_moves(self.size)
        self.got = {0: x}
        self.hop = 0

    def step(self):
        size, half = self.size, self.got[0].shape[0] // 2
        self.hop += 1
        k = self.hop
        a, b = self.got[k - 1], self.got[(size - k + 1) % size]
        if k == size // 2:
            a, b = a[:half], b[half:]
        self.sent = (a, b)
        a, b = lax.ppermute(a, "dp", self.ahead), lax.ppermute(b, "dp", self.back)
        if k == size // 2:
            self.halves = (a, b)
        else:
            self.got[k], self.got[size - k] = a, b
        self.last = (a, b)
        return self


def unfold(ref, row, rows, fold, width, start, r0, n):
    views = []
    for c in range(fold):
        lo, hi = max(r0, c * rows), min(r0 + n, (c + 1) * rows)
        if lo < hi:
            views.append((lo - r0, hi - lo, ref.at[pl.ds(row + lo - c * rows, hi - lo), pl.ds(c * width, width)]))
    return views


def piece_views(refs, kinds, places, r0, n, rows):
    out = []
    column = 0
    places = places if isinstance(places, list) else [places] * len(refs)
    for ref, kind, place in zip(refs, kinds, places):
        if kind == 1:
            start = pl.multiple_of(place * rows + r0, n)
            out.append((0, n, column, ref.shape[1], ref.at[pl.ds(start, n)]))
            column += ref.shape[1]
        else:
            width, short = ref.shape[1] // kind, rows // kind
            row = pl.multiple_of(place * short, short)
            for at, count, view in unfold(ref, row, short, kind, width, 0, r0, n):
                out.append((at, count, column, width, view))
            column += width
    return out


class Weight:
    def __init__(self, ring, kind=1, first=0, width=None, shards=False):
        while ring.hop < ring.size // 2:
            ring.step()
        self.kind, self.first, self.shards, self.size = kind, first, shards, ring.size
        self.rows, cols = ring.got[0].shape
        width = width or cols
        half, middle = self.rows // 2, ring.size // 2
        self.parts = [(k, 0, self.rows, x) for k, x in ring.got.items()]
        self.parts += [(middle, 0, half, ring.halves[0]), (middle, half, half, ring.halves[1])]
        self.shape = (self.size * self.rows // kind, width * kind)
        self.arrays = [x for _, _, _, x in self.parts]
        self.copies = len(self.parts) * kind

    def load(self, loads, group, at, refs, target):
        for (k, r0, n, _), ref in zip(self.parts, refs):
            place = at[1 + k + (self.size if self.shards else 0)]
            for row, count, column, width, view in piece_views([target], [self.kind], place, r0, n, self.rows):
                source = ref.at[pl.ds(row, count), pl.ds(self.first + column, width)]
                loads.add(group, source, view)


def tokens_times(info, held, weight, cols, across, name, after=()):
    gaps = list(held)
    S, (T, K) = len(gaps), held[0].shape
    n_w, n_out = len(weight.arrays), len(cols)

    def body(at, *refs):
        pieces, w_refs, outs = refs[:S], refs[S : S + n_w], refs[S + n_w : S + n_w + n_out]
        x, w, *stages, sems = refs[S + n_w + n_out :]
        loads = Loads(sems)
        weight.load(loads, "w", at, w_refs, w)
        for n, piece in enumerate(pieces):
            loads.add(n, piece, x.at[n])
        loads.wait("w")
        for n, gap in enumerate(gaps):
            loads.wait(n)
            for (first, width, dtype), out, stage in zip(cols, outs, stages):
                if across:
                    result = dot(x[n], w[first : first + width, :], ((1,), (1,)))
                else:
                    result = dot(x[n], w[:, first : first + width], ((1,), (0,)))
                stage[n] = result.astype(dtype)
                loads.add("out", stage.at[n], out.at[pl.ds(block_row(at, gap, T), T)])
        loads.wait("out")

    return call(
        body,
        info,
        [*held.values(), *weight.arrays],
        [like((S * T, width), dtype) for _, width, dtype in cols],
        [pltpu.VMEM((S, T, K), bf16), pltpu.VMEM(weight.shape, bf16)]
        + [pltpu.VMEM((S, T, width), dtype) for _, width, dtype in cols]
        + [pltpu.SemaphoreType.DMA((S + weight.copies + S * n_out,))],
        name=name,
        after=after,
        cost=2 * S * T * K * sum(width for _, width, _ in cols),
    )


def partial_rows(info, terms, gaps, name, after=()):
    arrays, picks = [], []
    for x, weight, _ in terms:
        mine = [x[gap] for gap in gaps] if isinstance(x, dict) else [x]
        picks.append((len(arrays), len(mine), isinstance(x, dict)))
        arrays += [*mine, *weight.arrays]
    first = terms[0][0]
    T = first[gaps[0]].shape[0] if isinstance(first, dict) else first.shape[0] // lax.axis_size("seq")
    widths = [weight.shape[1 if across else 0] for _, weight, across in terms]
    n_term, n_gap = len(terms), len(gaps)

    def body(at, *refs):
        ins, outs = refs[: len(arrays)], refs[len(arrays) : len(arrays) + n_gap]
        scratch = refs[len(arrays) + n_gap :]
        xs, ws, stages, sems = scratch[:n_term], scratch[n_term : 2 * n_term], scratch[2 * n_term : -1], scratch[-1]
        loads = Loads(sems)
        for (x, weight, across), (start, count, by_gap), x_ref, w_ref in zip(terms, picks, xs, ws):
            for n, gap in enumerate(gaps):
                if by_gap:
                    source = ins[start + n]
                else:
                    source = ins[start].at[pl.ds(block_row(at, gap, T), T)]
                loads.add("x", source, x_ref.at[n])
            weight.load(loads, "w", at, ins[start + count : start + count + len(weight.arrays)], w_ref)
        loads.wait("x")
        loads.wait("w")
        for n in range(n_gap):
            half = D // 2
            for c in range(2):
                total = None
                for (_, _, across), x_ref, w_ref in zip(terms, xs, ws):
                    cut = slice(c * half, (c + 1) * half)
                    if across:
                        part = dot(x_ref[n], w_ref[cut, :], ((1,), (1,)))
                    else:
                        part = dot(x_ref[n], w_ref[:, cut], ((1,), (0,)))
                    total = part if total is None else total + part
                stages[n][:, c * half : (c + 1) * half] = total.astype(stages[n].dtype)
            loads.add("out", stages[n], outs[n])
        loads.wait("out")

    dtypes = [bf16 if gap & 1 else f32 for gap in gaps]
    outs = call(
        body,
        info,
        arrays,
        [like((T, D), dtype) for dtype in dtypes],
        [pltpu.VMEM((n_gap, T, width), bf16) for width in widths]
        + [pltpu.VMEM(weight.shape, bf16) for _, weight, _ in terms]
        + [pltpu.VMEM((T, D), dtype) for dtype in dtypes]
        + [pltpu.SemaphoreType.DMA((sum(w.copies for _, w, _ in terms) + (n_term + 1) * n_gap,))],
        name=name,
        after=after,
        cost=2 * n_gap * T * D * sum(widths),
    )
    return dict(zip(gaps, outs))


def feed_forward(info, hidden, cot, up, down, gaps, after=()):
    n_gap = len(gaps)
    T = hidden[0].shape[0]
    FW = up.shape[1]
    n_up, n_down = len(up.arrays), len(down.arrays)
    arrays = [*(hidden[gap] for gap in gaps), *(cot[gap] for gap in gaps), *up.arrays, *down.arrays]

    def body(at, *refs):
        ins, outs = refs[: len(arrays)], refs[len(arrays) : len(arrays) + 3 * n_gap]
        x, g, w_up, w_down, acts, grads, *stages, sems = refs[len(arrays) + 3 * n_gap :]
        loads = Loads(sems)
        up.load(loads, "up", at, ins[2 * n_gap : 2 * n_gap + n_up], w_up)
        for n in range(n_gap):
            loads.add(("x", n), ins[n], x.at[n])
        down.load(loads, "down", at, ins[2 * n_gap + n_up :], w_down)
        for n in range(n_gap):
            loads.add(("g", n), ins[n_gap + n], g.at[n])
        loads.wait("up")
        for n in range(n_gap):
            loads.wait(("x", n))
            pre = dot(x[n], w_up[...], ((1,), (0,)))
            below = 0.5 * (1.0 + lax.erf(pre * 0.5**0.5))
            acts[n] = (pre * below).astype(bf16)
            loads.add("out", acts.at[n], outs[n])
            slope = below + pre * jnp.exp(-0.5 * pre * pre) * (0.5 / jnp.pi) ** 0.5
            if n == 0:
                loads.wait("down")
            loads.wait(("g", n))
            grads[n] = (dot(g[n], w_down[...], ((1,), (1,))) * slope).astype(bf16)
            loads.add("out", grads.at[n], outs[n_gap + n])
            half = D // 2
            for c in range(2):
                cut = slice(c * half, (c + 1) * half)
                stages[n][:, cut] = dot(grads[n], w_up[cut, :], ((1,), (1,))).astype(stages[n].dtype)
            loads.add("out", stages[n], outs[2 * n_gap + n])
        loads.wait("out")

    dtypes = [bf16 if gap & 1 else f32 for gap in gaps]
    outs = call(
        body,
        info,
        arrays,
        [like((T, FW), bf16)] * (2 * n_gap) + [like((T, D), dtype) for dtype in dtypes],
        [pltpu.VMEM((n_gap, T, D), bf16)] * 2
        + [pltpu.VMEM(up.shape, bf16), pltpu.VMEM(down.shape, bf16)]
        + [pltpu.VMEM((n_gap, T, FW), bf16)] * 2
        + [pltpu.VMEM((T, D), dtype) for dtype in dtypes]
        + [pltpu.SemaphoreType.DMA((up.copies + down.copies + 5 * n_gap,))],
        name="feed_forward",
        after=after,
        cost=6 * n_gap * T * D * FW,
    )
    return [dict(zip(gaps, outs[n * n_gap : (n + 1) * n_gap])) for n in range(3)]


class Term:
    def __init__(self, x, y, kind=1, shards=False, ordered=True):
        self.x, self.y, self.kind, self.shards, self.ordered = x, y, kind, shards, ordered
        some = x[0] if isinstance(x, dict) else x
        other = y[0] if isinstance(y, dict) else y
        self.tokens = some.shape[0] * (len(x) if isinstance(x, dict) else 1)
        self.columns = some.shape[1] // lax.axis_size("dp")
        self.rows, self.width = self.columns * kind, other.shape[1] // kind
        self.wide = other.shape[1]
        self.xs = list(x.values()) if isinstance(x, dict) else [x]
        self.ys = list(y.values()) if isinstance(y, dict) else [y]
        self.whole = self.columns % 128 != 0
        if self.whole:
            product = dot(self.rows_of(x), self.rows_of(y), ((0,), (0,)))
            self.xs, self.ys = [product.astype(bf16)], []

    def rows_of(self, held):
        if not isinstance(held, dict):
            return held
        rows = held[0].shape[0]
        out = jnp.zeros((len(held) * rows, held[0].shape[1]), bf16)
        for gap, part in held.items():
            start = (lax.axis_index("seq") ^ gap if self.ordered else gap) * rows
            out = lax.dynamic_update_slice_in_dim(out, part, start, 0)
        return out

    def spread(self, at, which, refs, target, cols=None):
        held = self.x if which == "x" else self.y
        for gap, ref in zip(held if isinstance(held, dict) else [None], refs):
            source = ref if cols is None else ref.at[:, cols]
            if gap is None:
                yield source, target
                continue
            rows = ref.shape[0]
            start = block_row(at, gap, rows) if self.ordered else gap * rows
            yield source, target.at[pl.ds(start, rows)]


class Scatter:
    def __init__(self, info, terms, name):
        self.info, self.terms, self.name = info, terms, name
        self.size = lax.axis_size("dp")
        self.ahead, self.back = ring_moves(self.size)
        self.rows = terms[0].rows
        self.cols = sum(term.width for term in terms)
        self.hop = 0
        self.last = ()

    def pieces(self, which, got, write, outs, after=()):
        terms, n_got, n_out, n_w = self.terms, len(got), len(outs), len(which)
        arrays = [a for term in terms for a in (*term.xs, *term.ys)]

        def body(at, *refs):
            ins, recvs = refs[: len(arrays)], refs[len(arrays) : len(arrays) + n_got]
            results = refs[len(arrays) + n_got : len(arrays) + n_got + n_out]
            scratch, sems = refs[len(arrays) + n_got + n_out : -1], refs[-1]
            held = scratch[:n_got]
            buffers = scratch[n_got:]
            loads = Loads(sems)
            start = 0
            for i, term in enumerate(terms):
                x_refs = ins[start : start + len(term.xs)]
                y_refs = ins[start + len(term.xs) : start + len(term.xs) + len(term.ys)]
                start += len(term.xs) + len(term.ys)
                y_buf, *x_bufs = buffers[i * (1 + n_w) : (i + 1) * (1 + n_w)]
                for n, k in enumerate(which):
                    place = at[1 + k + (self.size if term.shards else 0)]
                    cols = pl.ds(pl.multiple_of(place * term.columns, term.columns), term.columns)
                    if term.whole:
                        loads.add((i, n), x_refs[0].at[cols], x_bufs[n])
                        continue
                    for source, target in term.spread(at, "x", x_refs, x_bufs[n], cols):
                        loads.add((i, n), source, target)
                for source, target in term.spread(at, "y", y_refs, y_buf) if y_refs else ():
                    loads.add((i, 0), source, target)
            for source, target in zip(recvs, held):
                loads.add("got", source, target)
            loads.wait("got")
            column = 0
            for i, term in enumerate(terms):
                y_buf, *x_bufs = buffers[i * (1 + n_w) : (i + 1) * (1 + n_w)]
                for n in range(n_w):
                    loads.wait((i, n))
                    for c in range(term.kind):
                        cols = slice(c * term.width, (c + 1) * term.width)
                        if term.whole:
                            values = x_bufs[n][:, cols].astype(f32)
                        else:
                            values = dot(x_bufs[n][...], y_buf[:, cols], ((0,), (0,)))
                        write(n, c * term.columns, term.columns, column, values, held, results)
                column += term.width

        scratch = [pltpu.VMEM(x.shape, x.dtype) for x in got]
        for term in terms:
            scratch += [pltpu.VMEM((8, 128) if term.whole else (term.tokens, term.wide), bf16)]
            shape = (term.columns, term.wide) if term.whole else (term.tokens, term.columns)
            scratch += [pltpu.VMEM(shape, bf16)] * n_w
        copies = n_got + sum(n_w * len(t.xs) + len(t.ys) for t in terms)
        return call(
            body,
            self.info,
            [*arrays, *got],
            outs,
            [*scratch, pltpu.SemaphoreType.DMA((copies,))],
            in_specs=[ANY] * (len(arrays) + n_got),
            out_specs=[VMEM] * n_out,
            name=self.name,
            after=after,
            cost=2 * n_w * sum(t.tokens * t.columns * t.wide for t in terms),
        )

    def step(self, *after):
        m, rows, half = self.size // 2, self.rows, self.rows // 2
        k = m - self.hop
        self.hop += 1

        def write(n, row, count, column, values, got, outs):
            width = values.shape[1]
            for side in range(2) if k == m else [n]:
                for lo, hi in ((0, half), (half, rows)):
                    low, high = max(row, lo), min(row + count, hi)
                    if low >= high or (k == m and lo != side * half):
                        continue
                    part = values[low - row : high - row]
                    cols = slice(column, column + width)
                    if k < m - 1:
                        part = part + got[n][low:high, cols].astype(f32)
                    elif k == m - 1 and lo == n * half:
                        part = part + got[n][low - lo : high - lo, cols].astype(f32)
                    at = lo if k == m else 0
                    outs[side][low - at : high - at, cols] = part.astype(bf16)

        shape = like((half if k == m else rows, self.cols), bf16)
        which = [m] if k == m else [k, self.size - k]
        a, b = self.pieces(which, self.last, write, [shape, shape], after)
        self.sent = (a, b)
        self.last = (lax.ppermute(a, "dp", self.back), lax.ppermute(b, "dp", self.ahead))
        return self

    def own(self, widths, dtypes, after=()):
        while self.hop < self.size // 2:
            self.step()

        def write(n, row, count, column, values, got, outs):
            width = values.shape[1]
            total = values
            for ref in got:
                total = total + ref[row : row + count, column : column + width].astype(f32)
            start = 0
            for out, wide in zip(outs, widths):
                low, high = max(start, column), min(start + wide, column + width)
                if low < high:
                    part = total[:, low - column : high - column]
                    out[row : row + count, low - start : high - start] = part.astype(out.dtype)
                start += wide

        outs = [like((self.rows, w), t) for w, t in zip(widths, dtypes)]
        return self.pieces([0], self.last, write, outs, after)


def split_columns(info, proj_in, ffn_up, proj_out, H, QW, VW, FW):
    size = lax.axis_size("seq")
    rows, G = proj_in.shape[0], lax.axis_size("dp")
    FR = FW // G
    aligned = FR % 128 == 0
    if not aligned:
        ffn_up = ffn_up.reshape(rows, G, size, FR).transpose(0, 2, 1, 3).reshape(rows, size * FW)

    def body(at, w_in, w_up, w_out, *outs):
        outs[-1][...] = w_out[...]
        for gap in range(size):
            who = at[0] ^ gap
            qkv, gate, up = outs[3 * gap : 3 * gap + 3]
            for h in range(H):
                for n in range(2):
                    src = pl.multiple_of(n * D + (who * H + h) * DK, DK)
                    qkv[:, (2 * h + n) * DK : (2 * h + n + 1) * DK] = w_in[:, pl.ds(src, DK)]
            qkv[:, 2 * QW :] = w_in[:, pl.ds(pl.multiple_of(2 * D + who * VW, VW), VW)]
            gate[...] = w_in[:, pl.ds(pl.multiple_of(2 * D + VD + who * VW, VW), VW)]
            if not aligned:
                up[...] = w_up[:, pl.ds(pl.multiple_of(who * FW, FW), FW)]
                continue
            for i in range(G):
                src = pl.multiple_of((i * size + who) * FR, FR)
                up[:, i * FR : (i + 1) * FR] = w_up[:, pl.ds(src, FR)]

    outs = [like((rows, 2 * QW + VW), bf16), like((rows, VW), bf16), like((rows, FW), bf16)] * size
    outs = [*outs, like(proj_out.shape, bf16)]
    return call(
        body,
        info,
        [proj_in, ffn_up, proj_out],
        outs,
        in_specs=[VMEM] * 3,
        out_specs=[VMEM] * len(outs),
        name="split_columns",
    )


def join_pieces(info, parts, extra, fold, after=()):
    size = len(parts)
    rows, width = parts[0].shape
    wide = 0 if extra is None else extra.shape[1] // fold

    def body(at, *refs):
        out = refs[-1]
        for gap in range(size):
            out[pl.ds(pl.multiple_of((at[0] ^ gap) * rows, rows), rows), :width] = refs[gap][...]
        if extra is not None:
            short = size * rows // fold
            for c in range(fold):
                out[c * short : (c + 1) * short, width:] = refs[size][:, c * wide : (c + 1) * wide]

    ins = parts if extra is None else [*parts, extra]
    return call(
        body,
        info,
        ins,
        like((size * rows, width + wide), bf16),
        in_specs=[VMEM] * len(ins),
        out_specs=VMEM,
        name="join_pieces",
        after=after,
    )


def exchange_rows(info, x):
    size = lax.axis_size("seq")
    rows = x.shape[0] // size

    def body(at, src, *outs):
        for gap in range(size):
            outs[gap][...] = src[pl.ds(pl.multiple_of((at[0] ^ gap) * rows, rows), rows), :]

    outs = [like((rows, x.shape[1]), x.dtype)] * size
    parts = call(
        body, info, [x], outs, in_specs=[VMEM], out_specs=[VMEM] * size, name="exchange_rows"
    )
    return [part if gap == 0 else swap_seq(part, gap) for gap, part in enumerate(parts)]


def join_in_columns(info, qkvs, gates, H, QW, VW):
    size = len(qkvs)
    rows = qkvs[0].shape[0]

    def body(at, *refs):
        out = refs[-1]
        for gap in range(size):
            who = at[0] ^ gap
            qkv, gate = refs[gap], refs[size + gap]
            for h in range(H):
                for n in range(2):
                    to = pl.multiple_of(n * D + (who * H + h) * DK, DK)
                    part = qkv[:, (2 * h + n) * DK : (2 * h + n + 1) * DK]
                    out[:, pl.ds(to, DK)] = part.astype(f32)
            out[:, pl.ds(pl.multiple_of(2 * D + who * VW, VW), VW)] = qkv[:, 2 * QW :].astype(f32)
            to = pl.multiple_of(2 * D + VD + who * VW, VW)
            out[:, pl.ds(to, VW)] = gate[...].astype(f32)

    ins = [*qkvs, *gates]
    return call(
        body,
        info,
        ins,
        like((rows, 2 * D + 2 * VD), f32),
        in_specs=[VMEM] * len(ins),
        out_specs=VMEM,
        name="join_in_columns",
    )


def join_up_columns(info, ups, G, after=()):
    size = len(ups)
    rows, FW = ups[0].shape
    FR = FW // G
    aligned = FR % 128 == 0

    def body(at, *refs):
        out = refs[-1]
        for gap in range(size):
            who = at[0] ^ gap
            if not aligned:
                to = pl.multiple_of(who * FW, FW)
                out[:, pl.ds(to, FW)] = refs[gap][...].astype(f32)
                continue
            for i in range(G):
                to = pl.multiple_of((i * size + who) * FR, FR)
                out[:, pl.ds(to, FR)] = refs[gap][:, i * FR : (i + 1) * FR].astype(f32)

    out = call(
        body,
        info,
        ups,
        like((rows, size * FW), f32),
        in_specs=[VMEM] * size,
        out_specs=VMEM,
        name="join_up_columns",
        after=after,
    )
    if aligned:
        return out
    return out.reshape(rows, size, G, FR).transpose(0, 2, 1, 3).reshape(rows, size * FW)


def decays(log_decay, T):
    step = lax.broadcasted_iota(jnp.int32, (T, 1), 0).astype(f32)
    decay_query = jnp.exp((step + 1.0) * log_decay)
    decay_key = jnp.exp((T - 1.0 - step) * log_decay)
    row = lax.broadcasted_iota(jnp.int32, (T, T), 0)
    column = lax.broadcasted_iota(jnp.int32, (T, T), 1)
    gap = (row - column).astype(f32)
    lower = row >= column
    mask = jnp.where(lower, jnp.exp(jnp.where(lower, gap, 0.0) * log_decay), 0.0)
    return decay_query, decay_key, mask


def turn(u, cosine, sine):
    a, c = u[:, :HALF], u[:, HALF:]
    return jnp.concatenate([a * cosine - c * sine, a * sine + c * cosine], axis=1)


def centre(retained):
    average = jnp.mean(retained, axis=-1, keepdims=True)
    centred = retained - average
    spread = jnp.mean(centred * centred, axis=-1, keepdims=True)
    inverse = lax.rsqrt(jnp.maximum(spread, 0.25) + 1e-05)
    return centred, spread, inverse


def retention_forward(info, logs, keep, qk, v, gate, cosine, sine, S, T, H, after=()):
    TG = S * T

    def body(_, logs_ref, keep_ref, qk_ref, v_ref, g_ref, cos_ref, sin_ref, *outs):
        mixed, qk_out, retained_out, state_out, scores_out = outs
        log_decay = logs_ref[pl.program_id(0)]
        decay_query, decay_key, mask = decays(log_decay, T)
        block_decay = jnp.exp(jnp.full((1, 1), T * log_decay, f32))
        carry = jnp.zeros((DK, DV), f32)
        for b in range(S):
            rows = pl.ds(b * T, T)
            co, si = cos_ref[rows], sin_ref[rows]
            q = turn(qk_ref[rows, :DK], co, si).astype(bf16)
            k = (turn(qk_ref[rows, DK:], co, si) * DK ** (-0.5)).astype(bf16)
            qk_out[rows, :DK] = q
            qk_out[rows, DK:] = k
            value = v_ref[rows]
            scores = (dot(q, k, ((1,), (1,))) * mask).astype(bf16)
            scores_out[0, b] = scores
            state = keep_ref[b] * carry
            state_in = state.astype(bf16)
            state_out[0, b] = state_in
            query_decay = (q.astype(f32) * decay_query).astype(bf16)
            key_decay = (k.astype(f32) * decay_key).astype(bf16)
            retained = dot(scores, value, ((1,), (0,))) + dot(query_decay, state_in, ((1,), (0,)))
            retained_out[rows] = retained
            carry = block_decay * state + dot(key_decay, value, ((0,), (0,)))
            centred, _, inverse = centre(retained)
            g = g_ref[rows]
            mixed[rows] = (g * jax.nn.sigmoid(g) * (centred * inverse)).astype(bf16)

    smem = pl.BlockSpec(memory_space=pltpu.SMEM)
    once = lambda width: pl.BlockSpec((TG, width), lambda h, _: (0, 0))
    head = lambda width: pl.BlockSpec((TG, width), lambda h, _: (0, h))
    return call(
        body,
        info,
        [logs, keep, qk, v, gate, cosine, sine],
        [
            like((TG, H * DV), bf16),
            like((TG, 2 * H * DK), bf16),
            like((TG, H * DV), f32),
            like((H, S, DK, DV), bf16),
            like((H, S, T, T), bf16),
        ],
        grid=(H,),
        in_specs=[smem, smem, head(2 * DK), head(DV), head(DV), once(HALF), once(HALF)],
        out_specs=[
            head(DV),
            head(2 * DK),
            head(DV),
            pl.BlockSpec((1, S, DK, DV), lambda h, _: (h, 0, 0, 0)),
            pl.BlockSpec((1, S, T, T), lambda h, _: (h, 0, 0, 0)),
        ],
        name="retention_forward",
        after=after,
        cost=2 * H * S * T * T * (DK + DV) + 4 * H * S * T * DK * DV,
    )


def retention_backward(info, logs, keep, grad_mixed, gate, retained, qk, v, states, scores, cosine, sine, S, T, H, after=()):
    TG = S * T

    def body(_, logs_ref, keep_ref, gm_ref, g_ref, r_ref, qk_ref, v_ref, state_ref, scores_ref, cos_ref, sin_ref, *outs):
        qk_grad, v_grad, g_grad = outs
        log_decay = logs_ref[pl.program_id(0)]
        decay_query, decay_key, mask = decays(log_decay, T)
        block_decay = jnp.exp(jnp.full((1, 1), T * log_decay, f32))
        later = jnp.zeros((DK, DV), f32)
        for b in reversed(range(S)):
            rows = pl.ds(b * T, T)
            gm, g = gm_ref[rows], g_ref[rows]
            centred, spread, inverse = centre(r_ref[rows])
            sig = jax.nn.sigmoid(g)
            swish = g * sig
            normed = centred * inverse
            g_grad[rows] = (gm * normed * (sig + swish * (1.0 - sig))).astype(bf16)
            grad_normed = gm * swish
            passes = jnp.where(spread > 0.25, 1.0, jnp.where(spread == 0.25, 0.5, 0.0))
            pull = jnp.sum(grad_normed * centred, axis=-1, keepdims=True)
            pull = pull * (-inverse * inverse * inverse / DV) * passes
            grad_centred = grad_normed * inverse + pull * centred
            grad_ret = grad_centred - jnp.mean(grad_centred, axis=-1, keepdims=True)
            grad_ret = grad_ret.astype(bf16)
            q, k, value = qk_ref[rows, :DK], qk_ref[rows, DK:], v_ref[rows]
            query_decay = (q.astype(f32) * decay_query).astype(bf16)
            key_decay = (k.astype(f32) * decay_key).astype(bf16)
            grad_raw = (dot(grad_ret, value, ((1,), (1,))) * mask).astype(bf16)
            local = later.astype(bf16)
            grad_q = dot(grad_raw, k, ((1,), (0,)))
            grad_q = grad_q + decay_query * dot(grad_ret, state_ref[0, b], ((1,), (1,)))
            grad_k = dot(grad_raw, q, ((0,), (0,)))
            grad_k = grad_k + decay_key * dot(value, local, ((1,), (1,)))
            grad_v = dot(scores_ref[0, b], grad_ret, ((0,), (0,)))
            grad_v = grad_v + dot(key_decay, local, ((1,), (0,)))
            co, si = cos_ref[rows], -sin_ref[rows]
            qk_grad[rows, :DK] = turn(grad_q, co, si).astype(bf16)
            qk_grad[rows, DK:] = turn(grad_k * DK ** (-0.5), co, si).astype(bf16)
            v_grad[rows] = grad_v.astype(bf16)
            if b > 0:
                here = dot(query_decay, grad_ret, ((0,), (0,)))
                later = keep_ref[b] * (here + block_decay * later)

    smem = pl.BlockSpec(memory_space=pltpu.SMEM)
    once = lambda width: pl.BlockSpec((TG, width), lambda h, _: (0, 0))
    head = lambda width: pl.BlockSpec((TG, width), lambda h, _: (0, h))
    return call(
        body,
        info,
        [logs, keep, grad_mixed, gate, retained, qk, v, states, scores, cosine, sine],
        [like((TG, 2 * H * DK), bf16), like((TG, H * DV), bf16), like((TG, H * DV), bf16)],
        grid=(H,),
        in_specs=[
            smem,
            smem,
            head(DV),
            head(DV),
            head(DV),
            head(2 * DK),
            head(DV),
            pl.BlockSpec((1, S, DK, DV), lambda h, _: (h, 0, 0, 0)),
            pl.BlockSpec((1, S, T, T), lambda h, _: (h, 0, 0, 0)),
            once(HALF),
            once(HALF),
        ],
        out_specs=[head(2 * DK), head(DV), head(DV)],
        name="retention_backward",
        after=after,
        cost=4 * H * S * T * T * (DK + DV) + 8 * H * S * T * DK * DV,
    )


def local(
    layer_in,
    out_grad,
    seq_start,
    norm1_gain,
    norm1_shift,
    proj_in,
    proj_out,
    norm2_gain,
    norm2_shift,
    ffn_up,
    ffn_down,
):
    S, G = lax.axis_size("seq"), lax.axis_size("dp")
    me = lax.axis_index("seq")
    T = layer_in.shape[0]
    TG = S * T
    H = HEADS // S
    QW, VW = H * DK, H * DV
    FW = G * ffn_down.shape[0]
    fold = S // 2
    info = make_info()

    vectors = jnp.stack([norm1_gain, norm1_shift, norm2_gain, norm2_shift])
    norms, norms_dp = gather_all(vectors)
    norms = norms.transpose(1, 0, 2).reshape(4, 1, D).astype(f32)
    gain_one, shift_one, gain_two, shift_two = norms

    to_rank = [(j * G + t, shard_place(t, G) * S + j) for j in range(S) for t in range(G)]
    *parts, out_shard = split_columns(info, proj_in, ffn_up, proj_out, H, QW, VW, FW)
    out_piece = lax.ppermute(out_shard, BOTH, to_rank)

    def exchanged(own, *after):
        return [own[0]] + [
            swap_seq(tie(x, *after) if after else x, gap) for gap, x in enumerate(own) if gap
        ]

    qkv_parts = exchanged(parts[0::3])
    qkv_ring = Gather(join_pieces(info, qkv_parts, None, fold)).step()
    (normed_one,) = norm_forward(layer_in, gain_one, shift_one, (), (qkv_ring.got[0],))
    hidden_one = gather_seq(normed_one)
    early = (*qkv_ring.last, hidden_one[S // 2])
    gate_parts, up_parts = exchanged(parts[1::3], *early), exchanged(parts[2::3], *early)
    qkv_ring.step()
    cot = gather_seq(tie(out_grad, *qkv_ring.last))
    qkv_ring.step().step()
    gate_piece = join_pieces(info, gate_parts, None, fold, qkv_ring.sent)
    gate_ring = Gather(gate_piece).step().step()
    out_ring = Gather(tie(out_piece, *gate_ring.sent)).step()

    factor = jnp.power(10000.0, -jnp.arange(HALF, dtype=f32) / (HALF - 1))
    angles = jnp.arange(TG, dtype=f32)[:, None] * factor[None, :]
    cosine, sine = jnp.cos(angles), jnp.sin(angles)
    log_all = jnp.log(1.0 - jnp.exp2(-5.0 - jnp.arange(HEADS, dtype=f32)))
    logs = lax.dynamic_slice_in_dim(log_all, me * H, H)
    keep = 1.0 - seq_start[0].astype(f32)

    w_qkv = Weight(qkv_ring)
    qk_pre, values = tokens_times(
        info,
        hidden_one,
        w_qkv,
        [(0, 2 * QW, f32), (2 * QW, VW, bf16)],
        False,
        "project_qkv",
        (*gate_ring.sent, *out_ring.sent, cosine, sine, *cot.values()),
    )
    w_qk = Weight(qkv_ring, 1, 0, 2 * QW)
    w_v = Weight(qkv_ring, 1, 2 * QW, VW)
    out_ring.step()
    w_g = Weight(gate_ring)
    ffn_ring = Gather(join_pieces(info, up_parts, ffn_down, fold, out_ring.sent)).step()
    (gate_pre,) = tokens_times(
        info, hidden_one, w_g, [(0, VW, f32)], False, "project_gate", ffn_ring.sent
    )
    mixed, qk, retained, states, scores = retention_forward(
        info, logs, keep, qk_pre, values, gate_pre, cosine, sine, S, T, H, out_ring.step().step().sent
    )
    w_out = Weight(out_ring, shards=True)
    odd, even = [g for g in reversed(range(S)) if g & 1], [g for g in reversed(range(S)) if not g & 1]
    ffn_ring.step()
    attn, attn_got = partial_rows(info, [(mixed, w_out, False)], odd, "attn_odd", ffn_ring.sent), {}
    swap_odd(attn, attn_got)
    attn |= partial_rows(info, [(mixed, w_out, False)], even, "attn_even", (attn[odd[-1]],))
    attn, attn_sent = scatter_seq(attn, attn_got)
    ffn_ring.step()
    middle, normed_two = norm_forward(layer_in, gain_two, shift_two, attn, ffn_ring.sent)
    ffn_ring.step()
    hidden_two = gather_seq(normed_two)
    w_up = Weight(ffn_ring, 1, 0, FW)
    w_down = Weight(ffn_ring, fold, FW, 2 * D // S)
    near, far = [1, 0], list(reversed(range(2, S)))
    active, grad_up, grad_two = feed_forward(info, hidden_two, cot, w_up, w_down, near)
    two_got = {}
    swap_odd(grad_two, two_got)
    more = feed_forward(info, hidden_two, cot, w_up, w_down, far, (grad_two[0],))
    swap_odd(more[2], two_got)
    for whole, extra in zip((active, grad_up, grad_two), more):
        whole |= extra

    grad_two, two_sent = scatter_seq(grad_two, two_got)
    order = sorted(active)
    active, grad_up, cot, hidden_two, hidden_one = (
        {gap: x[gap] for gap in order} for x in (active, grad_up, cot, hidden_two, hidden_one)
    )
    ffn_sum = Scatter(
        info,
        [Term(hidden_two, grad_up, ordered=False), Term(active, cot, fold, ordered=False)],
        "ffn_hop",
    ).step(two_sent)
    down = partial_rows(info, [(active, w_down, False)], odd + even, "down", ffn_sum.sent)
    down_got = {}
    swap_odd(down, down_got)
    grad_middle, grad_attn, two_sums = norm_backward(
        middle, gain_two, out_grad, grad_two, (f32, bf16), (down[0],)
    )

    ffn_sum.step(grad_attn)
    grad_attn = gather_seq(grad_attn, *ffn_sum.sent)
    (grad_mixed,) = tokens_times(info, grad_attn, w_out, [(0, VW, f32)], True, "grad_mixed")
    ffn_sum.step(grad_mixed)
    down, down_sent = scatter_seq(down, down_got, ffn_sum.sent)
    grad_qk, grad_v, grad_g = retention_backward(
        info, logs, keep, grad_mixed, gate_pre, retained, qk, values, states, scores, cosine, sine, S, T, H,
        (*ffn_sum.sent, down_sent),
    )
    gate_sum = Scatter(
        info, [Term(hidden_one, grad_g), Term(mixed, grad_attn, fold, True)], "gate_hop"
    ).step(grad_g)
    ffn_sum.step(*gate_sum.sent)
    qkv_sum = Scatter(info, [Term(hidden_one, grad_qk), Term(hidden_one, grad_v)], "qkv_hop")
    qkv_sum.step(*ffn_sum.sent)
    terms_one = [(grad_g, w_g, True), (grad_v, w_v, True), (grad_qk, w_qk, True)]
    grad_one, one_got = partial_rows(info, terms_one, odd, "grad_one_odd", qkv_sum.sent), {}
    swap_odd(grad_one, one_got)
    gate_sum.step(grad_one[odd[-1]])
    grad_one |= partial_rows(info, terms_one, even, "grad_one_even", gate_sum.sent)
    grad_one, one_sent = scatter_seq(grad_one, one_got)
    qkv_sum.step(one_sent)
    layer_out = add_up([*down, middle], bf16, qkv_sum.sent)
    up_own, down_own = ffn_sum.own((FW, 2 * D // S), (bf16, f32), (layer_out,))
    up_parts = exchange_rows(info, up_own)
    gate_sum.step(up_parts[0])
    in_grad, one_sums = norm_backward(
        layer_in, gain_one, grad_middle, grad_one, (bf16,), gate_sum.sent
    )
    norm_terms = jnp.stack([one_sums[0], one_sums[1], two_sums[0], two_sums[1]])
    down_grad = jnp.concatenate(jnp.split(tie(down_own, in_grad), fold, axis=0), axis=1)
    qkv_sum.step(in_grad)
    gate_sum.step(*qkv_sum.sent)
    up_grad = join_up_columns(info, up_parts, G, gate_sum.sent)
    norm_afters = [qkv_sum.sent]
    qkv_sum.step(up_grad)
    g_own, out_own = gate_sum.own((VW, 2 * D // S), (bf16, bf16), qkv_sum.sent)
    g_parts = exchange_rows(info, g_own)
    out_grad_w = lax.ppermute(out_own, BOTH, [(b, a) for a, b in to_rank])
    norm_grads = scatter_all(
        norm_terms.reshape(4, G * S, -1).transpose(1, 0, 2),
        [*norm_afters, qkv_sum.sent, (g_own,)],
    )
    out_grad_w = jnp.concatenate(jnp.split(out_grad_w, fold, axis=0), axis=1).astype(f32)
    (qkv_own,) = qkv_sum.own((2 * QW + VW,), (bf16,))
    in_grad_w = join_in_columns(info, exchange_rows(info, qkv_own), g_parts, H, QW, VW)
    return (
        layer_out,
        in_grad,
        norm_grads[0],
        norm_grads[1],
        in_grad_w,
        out_grad_w,
        norm_grads[2],
        norm_grads[3],
        up_grad,
        down_grad,
    )


def solution(mesh):
    rows, vector = P(BOTH, None), P(BOTH)
    in_specs = (rows, rows, P("dp", None), vector, vector, rows, rows, vector, vector, rows, rows)
    out_specs = (rows, rows, vector, vector, rows, rows, vector, vector, rows, rows)
    return jax.shard_map(local, mesh=mesh, in_specs=in_specs, out_specs=out_specs, check_vma=False)
```

```python
import functools

import jax
import jax.numpy as jnp
from jax import lax
from jax.experimental import pallas as pl
from jax.experimental.pallas import tpu as pltpu
from jax.sharding import PartitionSpec as P

D = 2048
HEADS = 8
VD = 4096
DK = 256
DV = 512
HALF = DK // 2
BOTH = ("dp", "seq")
f32 = jnp.float32
bf16 = jnp.bfloat16
ANY = pl.BlockSpec(memory_space=pl.ANY)
VMEM = pl.BlockSpec(memory_space=pltpu.VMEM)
LIMIT = 58 << 20
DEPTH = 4


def dot(a, b, dims):
    return lax.dot_general(a, b, (dims, ((), ())), preferred_element_type=f32)


def call(body, info, ins, outs, scratch=(), grid=(), in_specs=None, out_specs=None, name=None, cost=None, after=()):
    many = isinstance(outs, (list, tuple))
    n_in, n_after = len(ins), len(after)
    ins, after = list(ins), list(after)

    def inner(at, *refs):
        body(at, *refs[:n_in], *refs[n_in + n_after :])

    spec = pltpu.PrefetchScalarGridSpec(
        num_scalar_prefetch=1,
        grid=grid,
        in_specs=list(in_specs or [ANY] * n_in) + [ANY] * n_after,
        out_specs=out_specs or ([ANY] * len(outs) if many else ANY),
        scratch_shapes=list(scratch),
    )
    moved = sum(x.size * x.dtype.itemsize for x in (*ins, *(outs if many else [outs])))
    return pl.pallas_call(
        inner,
        out_shape=outs,
        grid_spec=spec,
        name=name,
        cost_estimate=pl.CostEstimate(
            flops=cost or 0, bytes_accessed=int(moved), transcendentals=0
        ),
        compiler_params=pltpu.CompilerParams(vmem_limit_bytes=LIMIT),
    )(info, *ins, *after)


def tie(x, *after):
    return pl.pallas_call(
        lambda *refs: None,
        out_shape=like(x.shape, x.dtype),
        in_specs=[ANY] * (1 + len(after)),
        out_specs=ANY,
        input_output_aliases={0: 0},
        name="tie",
    )(x, *after)


def like(shape, dtype):
    return jax.ShapeDtypeStruct(shape, dtype)


def seq_gaps(size):
    return [1 << b for b in range(size.bit_length() - 1)]


def swap_seq(x, gap):
    size = lax.axis_size("seq")
    return lax.ppermute(x, "seq", [(i, i ^ gap) for i in range(size)])


class Loads:
    def __init__(self, sems):
        self.sems, self.count, self.groups = sems, 0, {}

    def add(self, group, source, target):
        copy = pltpu.make_async_copy(source, target, self.sems.at[self.count])
        self.groups.setdefault(group, []).append(copy)
        self.count += 1
        copy.start()

    def wait(self, group):
        for copy in self.groups.pop(group, []):
            copy.wait()


def block_row(at, gap, rows):
    return pl.multiple_of((at[0] ^ gap) * rows, rows)


def gather_seq(x, *after):
    held = {0: x}
    for gap in reversed(seq_gaps(lax.axis_size("seq"))):
        new = {g ^ gap: swap_seq(part, gap) for g, part in list(held.items())}
        if after and gap == lax.axis_size("seq") // 2:
            new = {g: tie(part, *after) for g, part in new.items()}
        held.update(new)
    return held


def far_blocks(x, *after):
    held = {0: x}
    for gap in reversed(seq_gaps(lax.axis_size("seq"))[1:]):
        held.update({g ^ gap: tie(swap_seq(part, gap), *after) for g, part in list(held.items())})
    del held[0]
    return held | {g ^ 1: swap_seq(part, 1) for g, part in held.items()}


ROWS = 128


def plain(body, ins, outs, grid, in_specs, out_specs, name, after=()):
    n_in = len(ins)

    def inner(*refs):
        body(*refs[:n_in], *refs[n_in + len(after) :])

    return pl.pallas_call(
        inner,
        out_shape=outs,
        grid=grid,
        in_specs=[*in_specs, *[ANY] * len(after)],
        out_specs=out_specs,
        name=name,
        compiler_params=pltpu.CompilerParams(vmem_limit_bytes=LIMIT),
    )(*ins, *after)


def tile_of(rows, cols):
    return pl.BlockSpec((rows, cols), lambda i: (i, 0))


def add_up(parts, dtype, after=()):
    T, C = parts[0].shape

    def body(*refs):
        total = refs[0][...].astype(f32)
        for ref in refs[1:-1]:
            total = total + ref[...].astype(f32)
        refs[-1][...] = total.astype(dtype)

    return plain(
        body,
        parts,
        like((T, C), dtype),
        (T // ROWS,),
        [tile_of(ROWS, C)] * len(parts),
        tile_of(ROWS, C),
        "add_up",
        after,
    )


def swap_odd(parts, got):
    for gap in sorted((gap for gap in parts if gap & 1), reverse=True):
        got.setdefault(gap ^ 1, []).append(swap_seq(parts[gap], 1))


def scatter_seq(parts, got, after=()):
    size = lax.axis_size("seq")
    sent = parts[0]
    bit = 2
    while bit < size:
        for gap in [gap for gap in reversed(range(size)) if gap & bit and gap % bit == 0]:
            sent = add_up([parts[gap], *got[gap]], bf16, after)
            got.setdefault(gap ^ bit, []).append(swap_seq(sent, bit))
        bit *= 2
    return [parts[0], *got[0]], sent


def norm_forward(rows, gain, shift, more=(), after=()):
    T, C = rows.shape
    wide = len(more) > 0

    def body(rows_ref, gain_ref, shift_ref, *refs):
        outs = refs[-2:] if wide else refs[-1:]
        total = rows_ref[...].astype(f32)
        for ref in refs[: len(more)]:
            total = total + ref[...].astype(f32)
        if wide:
            outs[0][...] = total
        centred = total - jnp.mean(total, axis=-1, keepdims=True)
        spread = jnp.mean(centred * centred, axis=-1, keepdims=True)
        normed = centred * lax.rsqrt(spread + 1e-05) * gain_ref[...] + shift_ref[...]
        outs[-1][...] = normed.astype(bf16)

    vector = pl.BlockSpec((1, C), lambda i: (0, 0))
    outs = ([like((T, C), f32)] if wide else []) + [like((T, C), bf16)]
    return plain(
        body,
        [rows, gain, shift, *more],
        outs,
        (T // ROWS,),
        [tile_of(ROWS, C), vector, vector] + [tile_of(ROWS, C)] * len(more),
        [tile_of(ROWS, C)] * len(outs),
        "norm_forward",
        after,
    )


def norm_backward(rows, gain, base, parts, dtypes, after=()):
    T, C = rows.shape
    n = len(parts)

    def body(rows_ref, gain_ref, base_ref, *refs):
        grad = refs[0][...].astype(f32)
        for ref in refs[1:n]:
            grad = grad + ref[...].astype(f32)
        total = rows_ref[...].astype(f32)
        centred = total - jnp.mean(total, axis=-1, keepdims=True)
        inverse = lax.rsqrt(jnp.mean(centred * centred, axis=-1, keepdims=True) + 1e-05)
        normed = centred * inverse
        inner = grad * gain_ref[...]
        pull = inner - jnp.mean(inner, axis=-1, keepdims=True)
        pull = pull - normed * jnp.mean(inner * normed, axis=-1, keepdims=True)
        result = base_ref[...].astype(f32) + inverse * pull
        for out in refs[n:-1]:
            out[...] = result.astype(out.dtype)
        sums = refs[-1]

        @pl.when(pl.program_id(0) == 0)
        def _():
            sums[...] = jnp.zeros_like(sums)

        sums[0:1, :] += jnp.sum(grad * normed, axis=0, keepdims=True)
        sums[1:2, :] += jnp.sum(grad, axis=0, keepdims=True)

    vector = pl.BlockSpec((1, C), lambda i: (0, 0))
    outs = [like((T, C), t) for t in dtypes] + [like((8, C), f32)]
    return plain(
        body,
        [rows, gain, base, *parts],
        outs,
        (T // ROWS,),
        [tile_of(ROWS, C), vector, tile_of(ROWS, C)] + [tile_of(ROWS, C)] * n,
        [tile_of(ROWS, C)] * len(dtypes) + [pl.BlockSpec((8, C), lambda i: (0, 0))],
        "norm_backward",
        after,
    )


def swap_all(x, gap):
    size = lax.axis_size("dp") * lax.axis_size("seq")
    return lax.ppermute(x, BOTH, [(i, i ^ gap) for i in range(size)])


def flat_index():
    return lax.axis_index("dp") * lax.axis_size("seq") + lax.axis_index("seq")


class GatherAll:
    def __init__(self, x):
        S, G = lax.axis_size("seq"), lax.axis_size("dp")
        self.held, self.gaps = x[None, None], [S * g for g in seq_gaps(G)] + seq_gaps(S)

    def step(self, *after):
        gap, *self.gaps = self.gaps
        axis = 0 if gap >= lax.axis_size("seq") else 1
        other = swap_all(self.held, gap)
        if after:
            other = tie(other, *after)
        self.held = jnp.where(
            (flat_index() & gap) != 0,
            jnp.concatenate([other, self.held], axis=axis),
            jnp.concatenate([self.held, other], axis=axis),
        )
        return self


class ScatterAll:
    def __init__(self, x):
        S, G = lax.axis_size("seq"), lax.axis_size("dp")
        self.held, self.gaps = x, seq_gaps(S)[::-1] + [S * g for g in seq_gaps(G)[::-1]]

    def step(self):
        gap, *self.gaps = self.gaps
        axis = 0 if gap >= lax.axis_size("seq") else 1
        low, high = jnp.split(self.held, 2, axis=axis)
        upper = (flat_index() & gap) != 0
        self.held = jnp.where(upper, high, low) + swap_all(jnp.where(upper, low, high), gap)
        return self


def cycle(size):
    depth = DEPTH
    width = size // depth
    walk = [(0, x) for x in range(width)]
    for turn, x in enumerate(reversed(range(width))):
        column = [(z, x) for z in range(1, depth)]
        walk += column if turn % 2 == 0 else column[::-1]
    return [z * width + x for z, x in walk]


def ring_moves(size):
    walk = cycle(size)
    ahead = [(walk[i], walk[(i + 1) % size]) for i in range(size)]
    return ahead, [(b, a) for a, b in ahead]


def shard_place(t, size):
    return (t % DEPTH) * (size // DEPTH) + t // DEPTH


def make_info():
    size = lax.axis_size("dp")
    walk = cycle(size)
    table = [[walk[(walk.index(i) - k) % size] for k in range(size)] for i in range(size)]
    shard = {shard_place(t, size): t for t in range(size)}
    table = [row + [shard[i] for i in row] for row in table]
    row = lax.dynamic_index_in_dim(jnp.array(table, jnp.int32), lax.axis_index("dp"), 0, False)
    return jnp.concatenate([lax.axis_index("seq").astype(jnp.int32)[None], row])


class Gather:
    def __init__(self, x):
        self.size = lax.axis_size("dp")
        self.ahead, self.back = ring_moves(self.size)
        self.got = {0: x}
        self.hop = 0

    def step(self, *after):
        size, half = self.size, self.got[0].shape[0] // 2
        self.hop += 1
        k = self.hop
        if after and k > 1:
            for n in {k - 1, (size - k + 1) % size}:
                self.got[n] = tie(self.got[n], *after)
        a, b = self.got[k - 1], self.got[(size - k + 1) % size]
        if k == size // 2:
            a, b = a[:half], b[half:]
        self.sent = (a, b)
        a, b = lax.ppermute(a, "dp", self.ahead), lax.ppermute(b, "dp", self.back)
        if k == size // 2:
            self.halves = (a, b)
        else:
            self.got[k], self.got[size - k] = a, b
        self.last = (a, b)
        return self


def unfold(ref, row, rows, fold, width, start, r0, n):
    views = []
    for c in range(fold):
        lo, hi = max(r0, c * rows), min(r0 + n, (c + 1) * rows)
        if lo < hi:
            views.append((lo - r0, hi - lo, ref.at[pl.ds(row + lo - c * rows, hi - lo), pl.ds(c * width, width)]))
    return views


def piece_views(refs, kinds, places, r0, n, rows):
    out = []
    column = 0
    places = places if isinstance(places, list) else [places] * len(refs)
    for ref, kind, place in zip(refs, kinds, places):
        if kind == 1:
            start = pl.multiple_of(place * rows + r0, n)
            out.append((0, n, column, ref.shape[1], ref.at[pl.ds(start, n)]))
            column += ref.shape[1]
        else:
            width, short = ref.shape[1] // kind, rows // kind
            row = pl.multiple_of(place * short, short)
            for at, count, view in unfold(ref, row, short, kind, width, 0, r0, n):
                out.append((at, count, column, width, view))
            column += width
    return out


class Weight:
    def __init__(self, ring, kind=1, first=0, width=None, shards=False):
        while ring.hop < ring.size // 2:
            ring.step()
        self.kind, self.first, self.shards, self.size = kind, first, shards, ring.size
        self.rows, cols = ring.got[0].shape
        width = width or cols
        half, middle = self.rows // 2, ring.size // 2
        self.parts = [(k, 0, self.rows, x) for k, x in ring.got.items()]
        self.parts += [(middle, 0, half, ring.halves[0]), (middle, half, half, ring.halves[1])]
        self.shape = (self.size * self.rows // kind, width * kind)
        self.arrays = [x for _, _, _, x in self.parts]
        self.copies = len(self.parts) * kind

    def load(self, loads, group, at, refs, target):
        for (k, r0, n, _), ref in zip(self.parts, refs):
            place = at[1 + k + (self.size if self.shards else 0)]
            for row, count, column, width, view in piece_views([target], [self.kind], place, r0, n, self.rows):
                source = ref.at[pl.ds(row, count), pl.ds(self.first + column, width)]
                loads.add(group, source, view)


def tokens_times(info, held, weight, cols, across, name, after=()):
    gaps = list(held)
    S, (T, K) = len(gaps), held[0].shape
    n_w, n_out = len(weight.arrays), len(cols)

    def body(at, *refs):
        pieces, w_refs, outs = refs[:S], refs[S : S + n_w], refs[S + n_w : S + n_w + n_out]
        x, w, *stages, sems = refs[S + n_w + n_out :]
        loads = Loads(sems)
        weight.load(loads, "w", at, w_refs, w)
        for n, piece in enumerate(pieces):
            loads.add(n // 2, piece, x.at[pl.ds(n * T, T)])
        loads.wait("w")
        for n in range(0, S, 2):
            loads.wait(n // 2)
            rows = pl.ds(n * T, 2 * T)
            for (first, width, dtype), out, stage in zip(cols, outs, stages):
                if across:
                    result = dot(x[rows], w[first : first + width, :], ((1,), (1,)))
                else:
                    result = dot(x[rows], w[:, first : first + width], ((1,), (0,)))
                stage[rows] = result.astype(dtype)
                for m in (n, n + 1):
                    target = out.at[pl.ds(block_row(at, gaps[m], T), T)]
                    loads.add("out", stage.at[pl.ds(m * T, T)], target)
        loads.wait("out")

    return call(
        body,
        info,
        [*held.values(), *weight.arrays],
        [like((S * T, width), dtype) for _, width, dtype in cols],
        [pltpu.VMEM((S * T, K), bf16), pltpu.VMEM(weight.shape, bf16)]
        + [pltpu.VMEM((S * T, width), dtype) for _, width, dtype in cols]
        + [pltpu.SemaphoreType.DMA((S + weight.copies + S * n_out,))],
        name=name,
        after=after,
        cost=2 * S * T * K * sum(width for _, width, _ in cols),
    )


def partial_rows(info, terms, gaps, name, after=(), ordered=False):
    arrays, picks = [], []
    for x, weight, _ in terms:
        mine = [x[gap] for gap in gaps] if isinstance(x, dict) else [x]
        picks.append((len(arrays), len(mine), isinstance(x, dict)))
        arrays += [*mine, *weight.arrays]
    first = terms[0][0]
    T = first[gaps[0]].shape[0] if isinstance(first, dict) else first.shape[0] // lax.axis_size("seq")
    widths = [weight.shape[1 if across else 0] for _, weight, across in terms]
    n_term, n_gap = len(terms), len(gaps)

    def body(at, *refs):
        n_out = 1 if ordered else n_gap
        ins, outs = refs[: len(arrays)], refs[len(arrays) : len(arrays) + n_out]
        scratch = refs[len(arrays) + n_out :]
        xs, ws, stages, sems = scratch[:n_term], scratch[n_term : 2 * n_term], scratch[2 * n_term : -1], scratch[-1]
        loads = Loads(sems)
        for (x, weight, across), (start, count, by_gap), x_ref, w_ref in zip(terms, picks, xs, ws):
            for n, gap in enumerate(gaps):
                if by_gap:
                    source = ins[start + n]
                else:
                    source = ins[start].at[pl.ds(block_row(at, gap, T), T)]
                loads.add("x", source, x_ref.at[pl.ds(n * T, T)])
            weight.load(loads, "w", at, ins[start + count : start + count + len(weight.arrays)], w_ref)
        loads.wait("x")
        loads.wait("w")
        for c in range(4):
            cut = slice(c * (D // 4), (c + 1) * (D // 4))
            total = None
            for (_, _, across), x_ref, w_ref in zip(terms, xs, ws):
                if across:
                    part = dot(x_ref[...], w_ref[cut, :], ((1,), (1,)))
                else:
                    part = dot(x_ref[...], w_ref[:, cut], ((1,), (0,)))
                total = part if total is None else total + part
            for n in range(n_gap):
                stages[n][:, cut] = total[n * T : (n + 1) * T].astype(stages[n].dtype)
        for n, gap in enumerate(gaps):
            target = outs[0].at[pl.ds(block_row(at, gap, T), T)] if ordered else outs[n]
            loads.add("out", stages[n], target)
        loads.wait("out")

    dtypes = [bf16 if gap & 1 or ordered else f32 for gap in gaps]
    outs = call(
        body,
        info,
        arrays,
        [like((n_gap * T, D), bf16)] if ordered else [like((T, D), dtype) for dtype in dtypes],
        [pltpu.VMEM((n_gap * T, width), bf16) for width in widths]
        + [pltpu.VMEM(weight.shape, bf16) for _, weight, _ in terms]
        + [pltpu.VMEM((T, D), dtype) for dtype in dtypes]
        + [pltpu.SemaphoreType.DMA((sum(w.copies for _, w, _ in terms) + (n_term + 1) * n_gap,))],
        name=name,
        after=after,
        cost=2 * n_gap * T * D * sum(widths),
    )
    return outs[0] if ordered else dict(zip(gaps, outs))


def feed_forward(info, hidden, cot, up, down, gaps, after=()):
    n_gap = len(gaps)
    T = hidden[0].shape[0]
    FW = up.shape[1]
    n_up, n_down = len(up.arrays), len(down.arrays)
    arrays = [*(hidden[gap] for gap in gaps), cot, *up.arrays, *down.arrays]

    def body(at, *refs):
        ins, outs = refs[: len(arrays)], refs[len(arrays) : len(arrays) + 3 * n_gap]
        x, g, w_up, w_down, acts, grads, *stages, sems = refs[len(arrays) + 3 * n_gap :]
        loads = Loads(sems)
        up.load(loads, "up", at, ins[n_gap + 1 : n_gap + 1 + n_up], w_up)
        for n in range(n_gap):
            loads.add(("x", n // 2), ins[n], x.at[pl.ds(n * T, T)])
        down.load(loads, "down", at, ins[n_gap + 1 + n_up :], w_down)
        for n, gap in enumerate(gaps):
            source = ins[n_gap].at[pl.ds(block_row(at, gap, T), T)]
            loads.add(("g", n // 2), source, g.at[pl.ds(n * T, T)])
        loads.wait("up")
        for n in range(0, n_gap, 2):
            rows = pl.ds(n * T, 2 * T)
            both = [(m, pl.ds(m * T, T)) for m in (n, n + 1)]
            loads.wait(("x", n // 2))
            pre = dot(x[rows], w_up[...], ((1,), (0,)))
            below = 0.5 * (1.0 + lax.erf(pre * 0.5**0.5))
            acts[rows] = (pre * below).astype(bf16)
            for m, part in both:
                loads.add("out", acts.at[part], outs[m])
            slope = below + pre * jnp.exp(-0.5 * pre * pre) * (0.5 / jnp.pi) ** 0.5
            if n == 0:
                loads.wait("down")
            loads.wait(("g", n // 2))
            grads[rows] = (dot(g[rows], w_down[...], ((1,), (1,))) * slope).astype(bf16)
            for m, part in both:
                loads.add("out", grads.at[part], outs[n_gap + m])
            for c in range(4):
                cut = slice(c * (D // 4), (c + 1) * (D // 4))
                result = dot(grads[rows], w_up[cut, :], ((1,), (1,)))
                for m, part in both:
                    value = result[(m - n) * T : (m - n + 1) * T]
                    stages[m][:, cut] = value.astype(stages[m].dtype)
            for m, part in both:
                loads.add("out", stages[m], outs[2 * n_gap + m])
        loads.wait("out")

    dtypes = [bf16 if gap & 1 else f32 for gap in gaps]
    outs = call(
        body,
        info,
        arrays,
        [like((T, FW), bf16)] * (2 * n_gap) + [like((T, D), dtype) for dtype in dtypes],
        [pltpu.VMEM((n_gap * T, D), bf16)] * 2
        + [pltpu.VMEM(up.shape, bf16), pltpu.VMEM(down.shape, bf16)]
        + [pltpu.VMEM((n_gap * T, FW), bf16)] * 2
        + [pltpu.VMEM((T, D), dtype) for dtype in dtypes]
        + [pltpu.SemaphoreType.DMA((up.copies + down.copies + 5 * n_gap,))],
        name="feed_forward",
        after=after,
        cost=6 * n_gap * T * D * FW,
    )
    return [dict(zip(gaps, outs[n * n_gap : (n + 1) * n_gap])) for n in range(3)]


class Term:
    def __init__(self, x, y, kind=1, shards=False, ordered=True):
        self.x, self.y, self.kind, self.shards, self.ordered = x, y, kind, shards, ordered
        some = x[0] if isinstance(x, dict) else x
        other = y[0] if isinstance(y, dict) else y
        self.tokens = some.shape[0] * (len(x) if isinstance(x, dict) else 1)
        self.columns = some.shape[1] // lax.axis_size("dp")
        self.rows, self.width = self.columns * kind, other.shape[1] // kind
        self.wide = other.shape[1]
        self.xs = list(x.values()) if isinstance(x, dict) else [x]
        self.ys = list(y.values()) if isinstance(y, dict) else [y]
        self.whole = self.columns % 128 != 0
        if self.whole:
            product = dot(self.rows_of(x), self.rows_of(y), ((0,), (0,)))
            self.xs, self.ys = [product.astype(bf16)], []

    def rows_of(self, held):
        if not isinstance(held, dict):
            return held
        rows = held[0].shape[0]
        out = jnp.zeros((len(held) * rows, held[0].shape[1]), bf16)
        for gap, part in held.items():
            start = (lax.axis_index("seq") ^ gap if self.ordered else gap) * rows
            out = lax.dynamic_update_slice_in_dim(out, part, start, 0)
        return out

    def spread(self, at, which, refs, target, cols=None):
        held = self.x if which == "x" else self.y
        for gap, ref in zip(held if isinstance(held, dict) else [None], refs):
            source = ref if cols is None else ref.at[:, cols]
            if gap is None:
                yield source, target
                continue
            rows = ref.shape[0]
            start = block_row(at, gap, rows) if self.ordered else gap * rows
            yield source, target.at[pl.ds(start, rows)]


class Scatter:
    def __init__(self, info, terms, name):
        self.info, self.terms, self.name = info, terms, name
        self.size = lax.axis_size("dp")
        self.ahead, self.back = ring_moves(self.size)
        self.rows = terms[0].rows
        self.cols = sum(term.width for term in terms)
        self.hop = 0
        self.last = ()

    def pieces(self, which, got, write, outs, after=()):
        terms, n_got, n_out, n_w = self.terms, len(got), len(outs), len(which)
        arrays = [a for term in terms for a in (*term.xs, *term.ys)]

        def body(at, *refs):
            ins, recvs = refs[: len(arrays)], refs[len(arrays) : len(arrays) + n_got]
            results = refs[len(arrays) + n_got : len(arrays) + n_got + n_out]
            scratch, sems = refs[len(arrays) + n_got + n_out : -1], refs[-1]
            held = scratch[:n_got]
            buffers = scratch[n_got:]
            loads = Loads(sems)
            start = 0
            for i, term in enumerate(terms):
                x_refs = ins[start : start + len(term.xs)]
                y_refs = ins[start + len(term.xs) : start + len(term.xs) + len(term.ys)]
                start += len(term.xs) + len(term.ys)
                y_buf, x_buf = buffers[2 * i : 2 * i + 2]
                for n, k in enumerate(which):
                    mine = pl.ds(n * term.columns, term.columns)
                    x_part = x_buf.at[mine] if term.whole else x_buf.at[:, mine]
                    place = at[1 + k + (self.size if term.shards else 0)]
                    cols = pl.ds(pl.multiple_of(place * term.columns, term.columns), term.columns)
                    if term.whole:
                        loads.add(i, x_refs[0].at[cols], x_part)
                        continue
                    for source, target in term.spread(at, "x", x_refs, x_part, cols):
                        loads.add(i, source, target)
                for source, target in term.spread(at, "y", y_refs, y_buf) if y_refs else ():
                    loads.add(i, source, target)
            for source, target in zip(recvs, held):
                loads.add("got", source, target)
            loads.wait("got")
            column = 0
            for i, term in enumerate(terms):
                y_buf, x_buf = buffers[2 * i : 2 * i + 2]
                loads.wait(i)
                for c in range(term.kind):
                    cols = slice(c * term.width, (c + 1) * term.width)
                    if term.whole:
                        values = x_buf[:, cols].astype(f32)
                    else:
                        values = dot(x_buf[...], y_buf[:, cols], ((0,), (0,)))
                    for n in range(n_w):
                        piece = values[n * term.columns : (n + 1) * term.columns]
                        write(n, c * term.columns, term.columns, column, piece, held, results)
                column += term.width

        scratch = [pltpu.VMEM(x.shape, x.dtype) for x in got]
        for term in terms:
            scratch += [pltpu.VMEM((8, 128) if term.whole else (term.tokens, term.wide), bf16)]
            many = n_w * term.columns
            scratch += [pltpu.VMEM((many, term.wide) if term.whole else (term.tokens, many), bf16)]
        copies = n_got + sum(n_w * len(t.xs) + len(t.ys) for t in terms)
        return call(
            body,
            self.info,
            [*arrays, *got],
            outs,
            [*scratch, pltpu.SemaphoreType.DMA((copies,))],
            in_specs=[ANY] * (len(arrays) + n_got),
            out_specs=[VMEM] * n_out,
            name=self.name,
            after=after,
            cost=2 * n_w * sum(t.tokens * t.columns * t.wide for t in terms),
        )

    def step(self, *after):
        m, rows, half = self.size // 2, self.rows, self.rows // 2
        k = m - self.hop
        self.hop += 1

        def write(n, row, count, column, values, got, outs):
            width = values.shape[1]
            for side in range(2) if k == m else [n]:
                for lo, hi in ((0, half), (half, rows)):
                    low, high = max(row, lo), min(row + count, hi)
                    if low >= high or (k == m and lo != side * half):
                        continue
                    part = values[low - row : high - row]
                    cols = slice(column, column + width)
                    if k < m - 1:
                        part = part + got[n][low:high, cols].astype(f32)
                    elif k == m - 1 and lo == n * half:
                        part = part + got[n][low - lo : high - lo, cols].astype(f32)
                    at = lo if k == m else 0
                    outs[side][low - at : high - at, cols] = part.astype(bf16)

        shape = like((half if k == m else rows, self.cols), bf16)
        which = [m] if k == m else [k, self.size - k]
        a, b = self.pieces(which, self.last, write, [shape, shape], after)
        self.sent = (a, b)
        self.last = (lax.ppermute(a, "dp", self.back), lax.ppermute(b, "dp", self.ahead))
        return self

    def own(self, widths, dtypes, after=()):
        while self.hop < self.size // 2:
            self.step()

        def write(n, row, count, column, values, got, outs):
            width = values.shape[1]
            total = values
            for ref in got:
                total = total + ref[row : row + count, column : column + width].astype(f32)
            start = 0
            for out, wide in zip(outs, widths):
                low, high = max(start, column), min(start + wide, column + width)
                if low < high:
                    part = total[:, low - column : high - column]
                    out[row : row + count, low - start : high - start] = part.astype(out.dtype)
                start += wide

        outs = [like((self.rows, w), t) for w, t in zip(widths, dtypes)]
        return self.pieces([0], self.last, write, outs, after)


def split_columns(info, proj_in, ffn_up, H, QW, VW, FW):
    size = lax.axis_size("seq")
    rows, G = proj_in.shape[0], lax.axis_size("dp")
    FR = FW // G
    aligned = FR % 128 == 0
    if not aligned:
        ffn_up = ffn_up.reshape(rows, G, size, FR).transpose(0, 2, 1, 3).reshape(rows, size * FW)

    def body(at, w_in, w_up, *outs):
        for gap in range(size):
            who = at[0] ^ gap
            qkv, gate = outs[2 * gap : 2 * gap + 2]
            for h in range(H):
                for n in range(2):
                    src = pl.multiple_of(n * D + (who * H + h) * DK, DK)
                    qkv[:, (2 * h + n) * DK : (2 * h + n + 1) * DK] = w_in[:, pl.ds(src, DK)]
            qkv[:, 2 * QW :] = w_in[:, pl.ds(pl.multiple_of(2 * D + who * VW, VW), VW)]
            gate[:, :VW] = w_in[:, pl.ds(pl.multiple_of(2 * D + VD + who * VW, VW), VW)]
            if not aligned:
                gate[:, VW:] = w_up[:, pl.ds(pl.multiple_of(who * FW, FW), FW)]
                continue
            for i in range(G):
                src = pl.multiple_of((i * size + who) * FR, FR)
                gate[:, VW + i * FR : VW + (i + 1) * FR] = w_up[:, pl.ds(src, FR)]

    outs = [like((rows, 2 * QW + VW), bf16), like((rows, VW + FW), bf16)] * size
    return call(
        body,
        info,
        [proj_in, ffn_up],
        outs,
        in_specs=[VMEM] * 2,
        out_specs=[VMEM] * len(outs),
        name="split_columns",
    )


def join_pieces(info, parts, extra, fold, after=(), first=0, width=None):
    size = len(parts)
    rows, width = parts[0].shape[0], width or parts[0].shape[1]
    wide = 0 if extra is None else extra.shape[1] // fold

    def body(at, *refs):
        out = refs[-1]
        for gap in range(size):
            out[pl.ds(pl.multiple_of((at[0] ^ gap) * rows, rows), rows), :width] = refs[gap][:, first : first + width]
        if extra is not None:
            short = size * rows // fold
            for c in range(fold):
                out[c * short : (c + 1) * short, width:] = refs[size][:, c * wide : (c + 1) * wide]

    ins = parts if extra is None else [*parts, extra]
    return call(
        body,
        info,
        ins,
        like((size * rows, width + wide), bf16),
        in_specs=[VMEM] * len(ins),
        out_specs=VMEM,
        name="join_pieces",
        after=after,
    )


def exchange_rows(info, x):
    size = lax.axis_size("seq")
    rows = x.shape[0] // size

    def body(at, src, *outs):
        for gap in range(size):
            outs[gap][...] = src[pl.ds(pl.multiple_of((at[0] ^ gap) * rows, rows), rows), :]

    outs = [like((rows, x.shape[1]), x.dtype)] * size
    parts = call(
        body, info, [x], outs, in_specs=[VMEM], out_specs=[VMEM] * size, name="exchange_rows"
    )
    return [part if gap == 0 else swap_seq(part, gap) for gap, part in enumerate(parts)]


def join_in_columns(info, qkvs, gates, H, QW, VW, after=()):
    size = len(qkvs)
    rows = qkvs[0].shape[0]

    def body(at, *refs):
        out = refs[-1]
        for gap in range(size):
            who = at[0] ^ gap
            qkv, gate = refs[gap], refs[size + gap]
            for h in range(H):
                for n in range(2):
                    to = pl.multiple_of(n * D + (who * H + h) * DK, DK)
                    part = qkv[:, (2 * h + n) * DK : (2 * h + n + 1) * DK]
                    out[:, pl.ds(to, DK)] = part.astype(f32)
            out[:, pl.ds(pl.multiple_of(2 * D + who * VW, VW), VW)] = qkv[:, 2 * QW :].astype(f32)
            to = pl.multiple_of(2 * D + VD + who * VW, VW)
            out[:, pl.ds(to, VW)] = gate[...].astype(f32)

    ins = [*qkvs, *gates]
    return call(
        body,
        info,
        ins,
        like((rows, 2 * D + 2 * VD), f32),
        in_specs=[VMEM] * len(ins),
        out_specs=VMEM,
        name="join_in_columns",
        after=after,
    )


def join_up_columns(info, ups, G, after=()):
    size = len(ups)
    rows, FW = ups[0].shape
    FR = FW // G
    aligned = FR % 128 == 0

    def body(at, *refs):
        out = refs[-1]
        for gap in range(size):
            who = at[0] ^ gap
            if not aligned:
                to = pl.multiple_of(who * FW, FW)
                out[:, pl.ds(to, FW)] = refs[gap][...].astype(f32)
                continue
            for i in range(G):
                to = pl.multiple_of((i * size + who) * FR, FR)
                out[:, pl.ds(to, FR)] = refs[gap][:, i * FR : (i + 1) * FR].astype(f32)

    out = call(
        body,
        info,
        ups,
        like((rows, size * FW), f32),
        in_specs=[VMEM] * size,
        out_specs=VMEM,
        name="join_up_columns",
        after=after,
    )
    if aligned:
        return out
    return out.reshape(rows, size, G, FR).transpose(0, 2, 1, 3).reshape(rows, size * FW)


def decays(log_decay, T):
    step = lax.broadcasted_iota(jnp.int32, (T, 1), 0).astype(f32)
    decay_query = jnp.exp((step + 1.0) * log_decay)
    decay_key = jnp.exp((T - 1.0 - step) * log_decay)
    row = lax.broadcasted_iota(jnp.int32, (T, T), 0)
    column = lax.broadcasted_iota(jnp.int32, (T, T), 1)
    gap = (row - column).astype(f32)
    lower = row >= column
    mask = jnp.where(lower, jnp.exp(jnp.where(lower, gap, 0.0) * log_decay), 0.0)
    return decay_query, decay_key, mask


def turn(u, cosine, sine):
    a, c = u[:, :HALF], u[:, HALF:]
    return jnp.concatenate([a * cosine - c * sine, a * sine + c * cosine], axis=1)


def centre(retained):
    average = jnp.mean(retained, axis=-1, keepdims=True)
    centred = retained - average
    spread = jnp.mean(centred * centred, axis=-1, keepdims=True)
    inverse = lax.rsqrt(jnp.maximum(spread, 0.25) + 1e-05)
    return centred, spread, inverse


def retention_forward(info, logs, keep, qk, v, gate, cosine, sine, S, T, H, after=()):
    TG = S * T

    def body(_, logs_ref, keep_ref, qk_ref, v_ref, g_ref, cos_ref, sin_ref, *outs):
        mixed, qk_out, retained_out, state_out, scores_out = outs
        log_decay = logs_ref[pl.program_id(0)]
        decay_query, decay_key, mask = decays(log_decay, T)
        block_decay = jnp.exp(jnp.full((1, 1), T * log_decay, f32))
        carry = jnp.zeros((DK, DV), f32)
        for b in range(S):
            rows = pl.ds(b * T, T)
            co, si = cos_ref[rows], sin_ref[rows]
            q = turn(qk_ref[rows, :DK], co, si).astype(bf16)
            k = (turn(qk_ref[rows, DK:], co, si) * DK ** (-0.5)).astype(bf16)
            qk_out[rows, :DK] = q
            qk_out[rows, DK:] = k
            value = v_ref[rows]
            scores = (dot(q, k, ((1,), (1,))) * mask).astype(bf16)
            scores_out[0, b] = scores
            state = keep_ref[b] * carry
            state_in = state.astype(bf16)
            state_out[0, b] = state_in
            query_decay = (q.astype(f32) * decay_query).astype(bf16)
            key_decay = (k.astype(f32) * decay_key).astype(bf16)
            retained = dot(scores, value, ((1,), (0,))) + dot(query_decay, state_in, ((1,), (0,)))
            retained_out[rows] = retained
            carry = block_decay * state + dot(key_decay, value, ((0,), (0,)))
            centred, _, inverse = centre(retained)
            g = g_ref[rows]
            mixed[rows] = (g * jax.nn.sigmoid(g) * (centred * inverse)).astype(bf16)

    smem = pl.BlockSpec(memory_space=pltpu.SMEM)
    once = lambda width: pl.BlockSpec((TG, width), lambda h, _: (0, 0))
    head = lambda width: pl.BlockSpec((TG, width), lambda h, _: (0, h))
    return call(
        body,
        info,
        [logs, keep, qk, v, gate, cosine, sine],
        [
            like((TG, H * DV), bf16),
            like((TG, 2 * H * DK), bf16),
            like((TG, H * DV), f32),
            like((H, S, DK, DV), bf16),
            like((H, S, T, T), bf16),
        ],
        grid=(H,),
        in_specs=[smem, smem, head(2 * DK), head(DV), head(DV), once(HALF), once(HALF)],
        out_specs=[
            head(DV),
            head(2 * DK),
            head(DV),
            pl.BlockSpec((1, S, DK, DV), lambda h, _: (h, 0, 0, 0)),
            pl.BlockSpec((1, S, T, T), lambda h, _: (h, 0, 0, 0)),
        ],
        name="retention_forward",
        after=after,
        cost=2 * H * S * T * T * (DK + DV) + 4 * H * S * T * DK * DV,
    )


def retention_backward(info, logs, keep, grad_mixed, gate, retained, qk, v, states, scores, cosine, sine, S, T, H, after=()):
    TG = S * T

    def body(_, logs_ref, keep_ref, gm_ref, g_ref, r_ref, qk_ref, v_ref, state_ref, scores_ref, cos_ref, sin_ref, *outs):
        qk_grad, v_grad, g_grad = outs
        log_decay = logs_ref[pl.program_id(0)]
        decay_query, decay_key, mask = decays(log_decay, T)
        block_decay = jnp.exp(jnp.full((1, 1), T * log_decay, f32))
        later = jnp.zeros((DK, DV), f32)
        for b in reversed(range(S)):
            rows = pl.ds(b * T, T)
            gm, g = gm_ref[rows], g_ref[rows]
            centred, spread, inverse = centre(r_ref[rows])
            sig = jax.nn.sigmoid(g)
            swish = g * sig
            normed = centred * inverse
            g_grad[rows] = (gm * normed * (sig + swish * (1.0 - sig))).astype(bf16)
            grad_normed = gm * swish
            passes = jnp.where(spread > 0.25, 1.0, jnp.where(spread == 0.25, 0.5, 0.0))
            pull = jnp.sum(grad_normed * centred, axis=-1, keepdims=True)
            pull = pull * (-inverse * inverse * inverse / DV) * passes
            grad_centred = grad_normed * inverse + pull * centred
            grad_ret = grad_centred - jnp.mean(grad_centred, axis=-1, keepdims=True)
            grad_ret = grad_ret.astype(bf16)
            q, k, value = qk_ref[rows, :DK], qk_ref[rows, DK:], v_ref[rows]
            query_decay = (q.astype(f32) * decay_query).astype(bf16)
            key_decay = (k.astype(f32) * decay_key).astype(bf16)
            grad_raw = (dot(grad_ret, value, ((1,), (1,))) * mask).astype(bf16)
            local = later.astype(bf16)
            grad_q = dot(grad_raw, k, ((1,), (0,)))
            grad_q = grad_q + decay_query * dot(grad_ret, state_ref[0, b], ((1,), (1,)))
            grad_k = dot(grad_raw, q, ((0,), (0,)))
            grad_k = grad_k + decay_key * dot(value, local, ((1,), (1,)))
            grad_v = dot(scores_ref[0, b], grad_ret, ((0,), (0,)))
            grad_v = grad_v + dot(key_decay, local, ((1,), (0,)))
            co, si = cos_ref[rows], -sin_ref[rows]
            qk_grad[rows, :DK] = turn(grad_q, co, si).astype(bf16)
            qk_grad[rows, DK:] = turn(grad_k * DK ** (-0.5), co, si).astype(bf16)
            v_grad[rows] = grad_v.astype(bf16)
            if b > 0:
                here = dot(query_decay, grad_ret, ((0,), (0,)))
                later = keep_ref[b] * (here + block_decay * later)

    smem = pl.BlockSpec(memory_space=pltpu.SMEM)
    once = lambda width: pl.BlockSpec((TG, width), lambda h, _: (0, 0))
    head = lambda width: pl.BlockSpec((TG, width), lambda h, _: (0, h))
    return call(
        body,
        info,
        [logs, keep, grad_mixed, gate, retained, qk, v, states, scores, cosine, sine],
        [like((TG, 2 * H * DK), bf16), like((TG, H * DV), bf16), like((TG, H * DV), bf16)],
        grid=(H,),
        in_specs=[
            smem,
            smem,
            head(DV),
            head(DV),
            head(DV),
            head(2 * DK),
            head(DV),
            pl.BlockSpec((1, S, DK, DV), lambda h, _: (h, 0, 0, 0)),
            pl.BlockSpec((1, S, T, T), lambda h, _: (h, 0, 0, 0)),
            once(HALF),
            once(HALF),
        ],
        out_specs=[head(2 * DK), head(DV), head(DV)],
        name="retention_backward",
        after=after,
        cost=4 * H * S * T * T * (DK + DV) + 8 * H * S * T * DK * DV,
    )


def local(
    layer_in,
    out_grad,
    seq_start,
    norm1_gain,
    norm1_shift,
    proj_in,
    proj_out,
    norm2_gain,
    norm2_shift,
    ffn_up,
    ffn_down,
):
    S, G = lax.axis_size("seq"), lax.axis_size("dp")
    me = lax.axis_index("seq")
    T = layer_in.shape[0]
    TG = S * T
    H = HEADS // S
    QW, VW = H * DK, H * DV
    FW = G * ffn_down.shape[0]
    fold = S // 2
    info = make_info()

    to_rank = [(j * G + t, shard_place(t, G) * S + j) for j in range(S) for t in range(G)]
    parts = split_columns(info, proj_in, ffn_up, H, QW, VW, FW)

    vectors = jnp.stack([norm1_gain, norm1_shift, norm2_gain, norm2_shift])
    norms = GatherAll(tie(vectors, parts[0]))
    while norms.gaps:
        norms.step()
    norms = norms.held.transpose(2, 0, 1, 3).reshape(4, 1, D).astype(f32)
    gain_one, shift_one, gain_two, shift_two = norms

    out_piece = lax.ppermute(tie(proj_out, norms), BOTH, to_rank)

    def exchanged(own, *after):
        return [own[0]] + [
            swap_seq(tie(x, *after) if after else x, gap) for gap, x in enumerate(own) if gap
        ]

    qkv_parts = exchanged(parts[0::2])
    qkv_ring = Gather(join_pieces(info, qkv_parts, None, fold, (norms,))).step()
    (normed_one,) = norm_forward(layer_in, gain_one, shift_one, (), (qkv_ring.got[0],))
    hidden_one = gather_seq(normed_one)
    early = (*qkv_ring.last, hidden_one[S // 2])
    qkv_ring.step()
    gate_parts = exchanged(parts[1::2], *early)
    cot = lax.all_gather(tie(out_grad, *early), "seq", axis=0, tiled=True)
    qkv_ring.step().step()
    gate_piece = join_pieces(
        info, gate_parts, None, fold, (*qkv_ring.sent, hidden_one[1], hidden_one[S - 1]), 0, VW
    )
    gate_ring = Gather(gate_piece).step().step(*qkv_ring.last)
    out_ring = Gather(tie(out_piece, *gate_ring.sent)).step()

    factor = jnp.power(10000.0, -jnp.arange(HALF, dtype=f32) / (HALF - 1))
    angles = jnp.arange(TG, dtype=f32)[:, None] * factor[None, :]
    cosine, sine = jnp.cos(angles), jnp.sin(angles)
    log_all = jnp.log(1.0 - jnp.exp2(-5.0 - jnp.arange(HEADS, dtype=f32)))
    logs = lax.dynamic_slice_in_dim(log_all, me * H, H)
    keep = 1.0 - seq_start[0].astype(f32)

    w_qkv = Weight(qkv_ring)
    qk_pre, values = tokens_times(
        info,
        hidden_one,
        w_qkv,
        [(0, 2 * QW, f32), (2 * QW, VW, bf16)],
        False,
        "project_qkv",
        (*gate_ring.sent, *out_ring.sent, cosine, sine),
    )
    w_qk = Weight(qkv_ring, 1, 0, 2 * QW)
    w_v = Weight(qkv_ring, 1, 2 * QW, VW)
    gate_ring.step(qk_pre)
    out_ring.step(qk_pre)
    gate_ring.step()
    out_ring.step()
    w_g = Weight(gate_ring)
    (gate_pre,) = tokens_times(
        info, hidden_one, w_g, [(0, VW, f32)], False, "project_gate", out_ring.sent
    )
    out_ring.step(gate_pre)
    ffn_ring = Gather(join_pieces(info, gate_parts, ffn_down, fold, out_ring.sent, VW, FW)).step()
    mixed, qk, retained, states, scores = retention_forward(
        info, logs, keep, qk_pre, values, gate_pre, cosine, sine, S, T, H,
        (*out_ring.sent, ffn_ring.got[0]),
    )
    w_out = Weight(out_ring, shards=True)
    odd, even = [g for g in reversed(range(S)) if g & 1], [g for g in reversed(range(S)) if not g & 1]
    ffn_ring.step()
    attn, attn_got = partial_rows(info, [(mixed, w_out, False)], odd, "attn_odd", (ffn_ring.got[0],)), {}
    swap_odd(attn, attn_got)
    attn |= partial_rows(info, [(mixed, w_out, False)], even, "attn_even", (attn[odd[-1]],))
    attn, attn_sent = scatter_seq(attn, attn_got)
    ffn_ring.step()
    middle, normed_two = norm_forward(layer_in, gain_two, shift_two, attn, ffn_ring.sent)
    ffn_ring.step()
    w_up = Weight(ffn_ring, 1, 0, FW)
    w_down = Weight(ffn_ring, fold, FW, 2 * D // S)
    near, far = [1, 0], list(reversed(range(2, S)))
    hidden_two = {0: normed_two, 1: swap_seq(normed_two, 1)}
    active, grad_up, grad_two = feed_forward(info, hidden_two, cot, w_up, w_down, near)
    hidden_two |= far_blocks(normed_two)
    two_got = {}
    swap_odd(grad_two, two_got)
    more = feed_forward(info, hidden_two, cot, w_up, w_down, far, (grad_two[0],))
    swap_odd(more[2], two_got)
    for whole, extra in zip((active, grad_up, grad_two), more):
        whole |= extra

    grad_two, two_sent = scatter_seq(grad_two, two_got)
    order = sorted(active)
    active, grad_up, hidden_two, hidden_one = (
        {gap: x[gap] for gap in order} for x in (active, grad_up, hidden_two, hidden_one)
    )
    ffn_sum = Scatter(
        info,
        [Term(hidden_two, grad_up), Term(active, cot, fold)],
        "ffn_hop",
    ).step(two_sent)
    down = partial_rows(
        info, [(active, w_down, False)], odd + even, "down", ffn_sum.sent, True
    )
    grad_middle, grad_attn, two_sums = norm_backward(
        middle, gain_two, out_grad, grad_two, (f32, bf16), (down, *ffn_sum.last)
    )

    ffn_sum.step(grad_attn)
    grad_attn = gather_seq(grad_attn, *ffn_sum.last)
    (grad_mixed,) = tokens_times(info, grad_attn, w_out, [(0, VW, f32)], True, "grad_mixed")
    ffn_sum.step(grad_mixed)
    down = lax.psum_scatter(tie(down, *ffn_sum.sent), "seq", scatter_dimension=0, tiled=True)
    grad_qk, grad_v, grad_g = retention_backward(
        info, logs, keep, grad_mixed, gate_pre, retained, qk, values, states, scores, cosine, sine, S, T, H,
        ffn_sum.sent,
    )
    gate_sum = Scatter(
        info, [Term(hidden_one, grad_g), Term(mixed, grad_attn, fold, True)], "gate_hop"
    ).step(grad_g)
    ffn_sum.step(*gate_sum.sent)
    qkv_sum = Scatter(info, [Term(hidden_one, grad_qk), Term(hidden_one, grad_v)], "qkv_hop")
    qkv_sum.step(*ffn_sum.sent)
    terms_one = [(grad_g, w_g, True), (grad_v, w_v, True), (grad_qk, w_qk, True)]
    grad_one, one_got = partial_rows(info, terms_one, odd, "grad_one_odd", qkv_sum.sent), {}
    swap_odd(grad_one, one_got)
    gate_sum.step(grad_one[odd[-1]])
    grad_one |= partial_rows(info, terms_one, even, "grad_one_even", gate_sum.sent)
    grad_one, one_sent = scatter_seq(grad_one, one_got)
    qkv_sum.step(one_sent)
    up_own, down_own = ffn_sum.own((FW, 2 * D // S), (bf16, f32), qkv_sum.sent)
    up_parts = exchange_rows(info, up_own)
    layer_out = add_up([down, middle], bf16, (up_parts[0],))
    gate_sum.step(layer_out)
    in_grad, one_sums = norm_backward(
        layer_in, gain_one, grad_middle, grad_one, (bf16,), gate_sum.sent
    )
    norm_terms = jnp.stack([one_sums[0], one_sums[1], two_sums[0], two_sums[1]])
    down_grad = jnp.concatenate(jnp.split(tie(down_own, in_grad), fold, axis=0), axis=1)
    qkv_sum.step(in_grad)
    gate_sum.step(*qkv_sum.sent)
    up_grad = join_up_columns(info, up_parts, G, gate_sum.sent)
    norm_sum = ScatterAll(norm_terms.reshape(4, G, S, -1).transpose(1, 2, 0, 3))
    for _ in seq_gaps(S):
        norm_sum.step()
    qkv_sum.step(up_grad, norm_sum.held)
    g_own, out_own = gate_sum.own((VW, 2 * D // S), (bf16, bf16), qkv_sum.sent)
    g_parts = exchange_rows(info, g_own)
    out_grad_w = lax.ppermute(out_own, BOTH, [(b, a) for a, b in to_rank])
    norm_sum.step()
    (qkv_own,) = qkv_sum.own((2 * QW + VW,), (bf16,), (g_parts[0], norm_sum.held))
    qkv_parts = exchange_rows(info, qkv_own)
    norm_sum.held = tie(norm_sum.held, qkv_parts[S // 2])
    while norm_sum.gaps:
        norm_sum.step()
    norm_grads = norm_sum.held[0, 0]
    in_grad_w = join_in_columns(info, qkv_parts, g_parts, H, QW, VW, (out_grad_w,))
    out_grad_w = jnp.concatenate(jnp.split(out_grad_w, fold, axis=0), axis=1).astype(f32)
    return (
        layer_out,
        in_grad,
        norm_grads[0],
        norm_grads[1],
        in_grad_w,
        out_grad_w,
        norm_grads[2],
        norm_grads[3],
        up_grad,
        down_grad,
    )


def solution(mesh):
    rows, vector = P(BOTH, None), P(BOTH)
    in_specs = (rows, rows, P("dp", None), vector, vector, rows, rows, vector, vector, rows, rows)
    out_specs = (rows, rows, vector, vector, rows, rows, vector, vector, rows, rows)
    return jax.shard_map(local, mesh=mesh, in_specs=in_specs, out_specs=out_specs, check_vma=False)
```

```python
import functools

import jax
import jax.numpy as jnp
from jax import lax
from jax.experimental import pallas as pl
from jax.experimental.pallas import tpu as pltpu
from jax.sharding import PartitionSpec as P

D = 2048
HEADS = 8
VD = 4096
DK = 256
DV = 512
HALF = DK // 2
BOTH = ("dp", "seq")
f32 = jnp.float32
bf16 = jnp.bfloat16
ANY = pl.BlockSpec(memory_space=pl.ANY)
VMEM = pl.BlockSpec(memory_space=pltpu.VMEM)
LIMIT = 58 << 20
DEPTH = 4


def dot(a, b, dims):
    return lax.dot_general(a, b, (dims, ((), ())), preferred_element_type=f32)


def call(body, info, ins, outs, scratch=(), grid=(), in_specs=None, out_specs=None, name=None, cost=None, after=()):
    many = isinstance(outs, (list, tuple))
    n_in, n_after = len(ins), len(after)
    ins, after = list(ins), list(after)

    def inner(at, *refs):
        body(at, *refs[:n_in], *refs[n_in + n_after :])

    spec = pltpu.PrefetchScalarGridSpec(
        num_scalar_prefetch=1,
        grid=grid,
        in_specs=list(in_specs or [ANY] * n_in) + [ANY] * n_after,
        out_specs=out_specs or ([ANY] * len(outs) if many else ANY),
        scratch_shapes=list(scratch),
    )
    moved = sum(x.size * x.dtype.itemsize for x in (*ins, *(outs if many else [outs])))
    return pl.pallas_call(
        inner,
        out_shape=outs,
        grid_spec=spec,
        name=name,
        cost_estimate=pl.CostEstimate(
            flops=cost or 0, bytes_accessed=int(moved), transcendentals=0
        ),
        compiler_params=pltpu.CompilerParams(vmem_limit_bytes=LIMIT),
    )(info, *ins, *after)


def tie(x, *after):
    return pl.pallas_call(
        lambda *refs: None,
        out_shape=like(x.shape, x.dtype),
        in_specs=[ANY] * (1 + len(after)),
        out_specs=ANY,
        input_output_aliases={0: 0},
        name="tie",
    )(x, *after)


def like(shape, dtype):
    return jax.ShapeDtypeStruct(shape, dtype)


def seq_gaps(size):
    return [1 << b for b in range(size.bit_length() - 1)]


def swap_seq(x, gap):
    size = lax.axis_size("seq")
    return lax.ppermute(x, "seq", [(i, i ^ gap) for i in range(size)])


class Loads:
    def __init__(self, sems):
        self.sems, self.count, self.groups = sems, 0, {}

    def add(self, group, source, target):
        copy = pltpu.make_async_copy(source, target, self.sems.at[self.count])
        self.groups.setdefault(group, []).append(copy)
        self.count += 1
        copy.start()

    def wait(self, group):
        for copy in self.groups.pop(group, []):
            copy.wait()


def block_row(at, gap, rows):
    return pl.multiple_of((at[0] ^ gap) * rows, rows)


def gather_seq(x, *after):
    held = {0: x}
    for gap in reversed(seq_gaps(lax.axis_size("seq"))):
        new = {g ^ gap: swap_seq(part, gap) for g, part in list(held.items())}
        if after and gap == lax.axis_size("seq") // 2:
            new = {g: tie(part, *after) for g, part in new.items()}
        held.update(new)
    return held


def far_blocks(x, *after):
    held = {0: x}
    for gap in reversed(seq_gaps(lax.axis_size("seq"))[1:]):
        held.update({g ^ gap: tie(swap_seq(part, gap), *after) for g, part in list(held.items())})
    del held[0]
    return held | {g ^ 1: swap_seq(part, 1) for g, part in held.items()}


ROWS = 128


def plain(body, ins, outs, grid, in_specs, out_specs, name, after=()):
    n_in = len(ins)

    def inner(*refs):
        body(*refs[:n_in], *refs[n_in + len(after) :])

    return pl.pallas_call(
        inner,
        out_shape=outs,
        grid=grid,
        in_specs=[*in_specs, *[ANY] * len(after)],
        out_specs=out_specs,
        name=name,
        compiler_params=pltpu.CompilerParams(vmem_limit_bytes=LIMIT),
    )(*ins, *after)


def tile_of(rows, cols):
    return pl.BlockSpec((rows, cols), lambda i: (i, 0))


def add_up(parts, dtype, after=()):
    T, C = parts[0].shape

    def body(*refs):
        total = refs[0][...].astype(f32)
        for ref in refs[1:-1]:
            total = total + ref[...].astype(f32)
        refs[-1][...] = total.astype(dtype)

    return plain(
        body,
        parts,
        like((T, C), dtype),
        (T // ROWS,),
        [tile_of(ROWS, C)] * len(parts),
        tile_of(ROWS, C),
        "add_up",
        after,
    )


def swap_odd(parts, got):
    for gap in sorted((gap for gap in parts if gap & 1), reverse=True):
        got.setdefault(gap ^ 1, []).append(swap_seq(parts[gap], 1))


def scatter_seq(parts, got, after=()):
    size = lax.axis_size("seq")
    sent = parts[0]
    bit = 2
    while bit < size:
        for gap in [gap for gap in reversed(range(size)) if gap & bit and gap % bit == 0]:
            sent = add_up([parts[gap], *got[gap]], bf16, after)
            got.setdefault(gap ^ bit, []).append(swap_seq(sent, bit))
        bit *= 2
    return [parts[0], *got[0]], sent


def norm_forward(rows, gain, shift, more=(), after=()):
    T, C = rows.shape
    wide = len(more) > 0

    def body(rows_ref, gain_ref, shift_ref, *refs):
        outs = refs[-2:] if wide else refs[-1:]
        total = rows_ref[...].astype(f32)
        for ref in refs[: len(more)]:
            total = total + ref[...].astype(f32)
        if wide:
            outs[0][...] = total
        centred = total - jnp.mean(total, axis=-1, keepdims=True)
        spread = jnp.mean(centred * centred, axis=-1, keepdims=True)
        normed = centred * lax.rsqrt(spread + 1e-05) * gain_ref[...] + shift_ref[...]
        outs[-1][...] = normed.astype(bf16)

    vector = pl.BlockSpec((1, C), lambda i: (0, 0))
    outs = ([like((T, C), f32)] if wide else []) + [like((T, C), bf16)]
    return plain(
        body,
        [rows, gain, shift, *more],
        outs,
        (T // ROWS,),
        [tile_of(ROWS, C), vector, vector] + [tile_of(ROWS, C)] * len(more),
        [tile_of(ROWS, C)] * len(outs),
        "norm_forward",
        after,
    )


def norm_backward(rows, gain, base, parts, dtypes, after=()):
    T, C = rows.shape
    n = len(parts)

    def body(rows_ref, gain_ref, base_ref, *refs):
        grad = refs[0][...].astype(f32)
        for ref in refs[1:n]:
            grad = grad + ref[...].astype(f32)
        total = rows_ref[...].astype(f32)
        centred = total - jnp.mean(total, axis=-1, keepdims=True)
        inverse = lax.rsqrt(jnp.mean(centred * centred, axis=-1, keepdims=True) + 1e-05)
        normed = centred * inverse
        inner = grad * gain_ref[...]
        pull = inner - jnp.mean(inner, axis=-1, keepdims=True)
        pull = pull - normed * jnp.mean(inner * normed, axis=-1, keepdims=True)
        result = base_ref[...].astype(f32) + inverse * pull
        for out in refs[n:-1]:
            out[...] = result.astype(out.dtype)
        sums = refs[-1]

        @pl.when(pl.program_id(0) == 0)
        def _():
            sums[...] = jnp.zeros_like(sums)

        sums[0:1, :] += jnp.sum(grad * normed, axis=0, keepdims=True)
        sums[1:2, :] += jnp.sum(grad, axis=0, keepdims=True)

    vector = pl.BlockSpec((1, C), lambda i: (0, 0))
    outs = [like((T, C), t) for t in dtypes] + [like((8, C), f32)]
    return plain(
        body,
        [rows, gain, base, *parts],
        outs,
        (T // ROWS,),
        [tile_of(ROWS, C), vector, tile_of(ROWS, C)] + [tile_of(ROWS, C)] * n,
        [tile_of(ROWS, C)] * len(dtypes) + [pl.BlockSpec((8, C), lambda i: (0, 0))],
        "norm_backward",
        after,
    )


def swap_all(x, gap):
    size = lax.axis_size("dp") * lax.axis_size("seq")
    return lax.ppermute(x, BOTH, [(i, i ^ gap) for i in range(size)])


def flat_index():
    return lax.axis_index("dp") * lax.axis_size("seq") + lax.axis_index("seq")


class GatherAll:
    def __init__(self, x):
        S, G = lax.axis_size("seq"), lax.axis_size("dp")
        self.held, self.gaps = x[None, None], [S * g for g in seq_gaps(G)] + seq_gaps(S)

    def step(self, *after):
        gap, *self.gaps = self.gaps
        axis = 0 if gap >= lax.axis_size("seq") else 1
        other = swap_all(self.held, gap)
        if after:
            other = tie(other, *after)
        self.held = jnp.where(
            (flat_index() & gap) != 0,
            jnp.concatenate([other, self.held], axis=axis),
            jnp.concatenate([self.held, other], axis=axis),
        )
        return self


class ScatterAll:
    def __init__(self, x):
        S, G = lax.axis_size("seq"), lax.axis_size("dp")
        self.held, self.gaps = x, seq_gaps(S)[::-1] + [S * g for g in seq_gaps(G)[::-1]]

    def step(self):
        gap, *self.gaps = self.gaps
        axis = 0 if gap >= lax.axis_size("seq") else 1
        low, high = jnp.split(self.held, 2, axis=axis)
        upper = (flat_index() & gap) != 0
        self.held = jnp.where(upper, high, low) + swap_all(jnp.where(upper, low, high), gap)
        return self


def cycle(size):
    depth = DEPTH
    width = size // depth
    walk = [(0, x) for x in range(width)]
    for turn, x in enumerate(reversed(range(width))):
        column = [(z, x) for z in range(1, depth)]
        walk += column if turn % 2 == 0 else column[::-1]
    return [z * width + x for z, x in walk]


def ring_moves(size):
    walk = cycle(size)
    ahead = [(walk[i], walk[(i + 1) % size]) for i in range(size)]
    return ahead, [(b, a) for a, b in ahead]


def shard_place(t, size):
    return (t % DEPTH) * (size // DEPTH) + t // DEPTH


def make_info():
    size = lax.axis_size("dp")
    walk = cycle(size)
    table = [[walk[(walk.index(i) - k) % size] for k in range(size)] for i in range(size)]
    shard = {shard_place(t, size): t for t in range(size)}
    table = [row + [shard[i] for i in row] for row in table]
    row = lax.dynamic_index_in_dim(jnp.array(table, jnp.int32), lax.axis_index("dp"), 0, False)
    return jnp.concatenate([lax.axis_index("seq").astype(jnp.int32)[None], row])


class Gather:
    def __init__(self, x):
        self.size = lax.axis_size("dp")
        self.ahead, self.back = ring_moves(self.size)
        self.got = {0: x}
        self.hop = 0

    def step(self, *after):
        size, half = self.size, self.got[0].shape[0] // 2
        self.hop += 1
        k = self.hop
        if after and k > 1:
            for n in {k - 1, (size - k + 1) % size}:
                self.got[n] = tie(self.got[n], *after)
        a, b = self.got[k - 1], self.got[(size - k + 1) % size]
        if k == size // 2:
            a, b = a[:half], b[half:]
        self.sent = (a, b)
        a, b = lax.ppermute(a, "dp", self.ahead), lax.ppermute(b, "dp", self.back)
        if k == size // 2:
            self.halves = (a, b)
        else:
            self.got[k], self.got[size - k] = a, b
        self.last = (a, b)
        return self


def unfold(ref, row, rows, fold, width, start, r0, n):
    views = []
    for c in range(fold):
        lo, hi = max(r0, c * rows), min(r0 + n, (c + 1) * rows)
        if lo < hi:
            views.append((lo - r0, hi - lo, ref.at[pl.ds(row + lo - c * rows, hi - lo), pl.ds(c * width, width)]))
    return views


def piece_views(refs, kinds, places, r0, n, rows):
    out = []
    column = 0
    places = places if isinstance(places, list) else [places] * len(refs)
    for ref, kind, place in zip(refs, kinds, places):
        if kind == 1:
            start = pl.multiple_of(place * rows + r0, n)
            out.append((0, n, column, ref.shape[1], ref.at[pl.ds(start, n)]))
            column += ref.shape[1]
        else:
            width, short = ref.shape[1] // kind, rows // kind
            row = pl.multiple_of(place * short, short)
            for at, count, view in unfold(ref, row, short, kind, width, 0, r0, n):
                out.append((at, count, column, width, view))
            column += width
    return out


class Weight:
    def __init__(self, ring, kind=1, first=0, width=None, shards=False):
        while ring.hop < ring.size // 2:
            ring.step()
        self.kind, self.first, self.shards, self.size = kind, first, shards, ring.size
        self.rows, cols = ring.got[0].shape
        width = width or cols
        half, middle = self.rows // 2, ring.size // 2
        self.parts = [(k, 0, self.rows, x) for k, x in ring.got.items()]
        self.parts += [(middle, 0, half, ring.halves[0]), (middle, half, half, ring.halves[1])]
        self.shape = (self.size * self.rows // kind, width * kind)
        self.arrays = [x for _, _, _, x in self.parts]
        self.copies = len(self.parts) * kind

    def load(self, loads, group, at, refs, target):
        for (k, r0, n, _), ref in zip(self.parts, refs):
            place = at[1 + k + (self.size if self.shards else 0)]
            for row, count, column, width, view in piece_views([target], [self.kind], place, r0, n, self.rows):
                source = ref.at[pl.ds(row, count), pl.ds(self.first + column, width)]
                loads.add(group, source, view)


def tokens_times(info, held, weight, cols, across, name, after=()):
    gaps = list(held)
    S, (T, K) = len(gaps), held[0].shape
    n_w, n_out = len(weight.arrays), len(cols)

    def body(at, *refs):
        pieces, w_refs, outs = refs[:S], refs[S : S + n_w], refs[S + n_w : S + n_w + n_out]
        x, w, *stages, sems = refs[S + n_w + n_out :]
        loads = Loads(sems)
        weight.load(loads, "w", at, w_refs, w)
        for n, piece in enumerate(pieces):
            loads.add(n // 2, piece, x.at[pl.ds(n * T, T)])
        loads.wait("w")
        for n in range(0, S, 2):
            loads.wait(n // 2)
            rows = pl.ds(n * T, 2 * T)
            for (first, width, dtype), out, stage in zip(cols, outs, stages):
                if across:
                    result = dot(x[rows], w[first : first + width, :], ((1,), (1,)))
                else:
                    result = dot(x[rows], w[:, first : first + width], ((1,), (0,)))
                stage[rows] = result.astype(dtype)
                for m in (n, n + 1):
                    target = out.at[pl.ds(block_row(at, gaps[m], T), T)]
                    loads.add("out", stage.at[pl.ds(m * T, T)], target)
        loads.wait("out")

    return call(
        body,
        info,
        [*held.values(), *weight.arrays],
        [like((S * T, width), dtype) for _, width, dtype in cols],
        [pltpu.VMEM((S * T, K), bf16), pltpu.VMEM(weight.shape, bf16)]
        + [pltpu.VMEM((S * T, width), dtype) for _, width, dtype in cols]
        + [pltpu.SemaphoreType.DMA((S + weight.copies + S * n_out,))],
        name=name,
        after=after,
        cost=2 * S * T * K * sum(width for _, width, _ in cols),
    )


def partial_rows(info, terms, gaps, name, after=(), ordered=False):
    arrays, picks = [], []
    for x, weight, _ in terms:
        mine = [x[gap] for gap in gaps] if isinstance(x, dict) else [x]
        picks.append((len(arrays), len(mine), isinstance(x, dict)))
        arrays += [*mine, *weight.arrays]
    first = terms[0][0]
    T = first[gaps[0]].shape[0] if isinstance(first, dict) else first.shape[0] // lax.axis_size("seq")
    widths = [weight.shape[1 if across else 0] for _, weight, across in terms]
    n_term, n_gap = len(terms), len(gaps)

    def body(at, *refs):
        n_out = 1 if ordered else n_gap
        ins, outs = refs[: len(arrays)], refs[len(arrays) : len(arrays) + n_out]
        scratch = refs[len(arrays) + n_out :]
        xs, ws, stages, sems = scratch[:n_term], scratch[n_term : 2 * n_term], scratch[2 * n_term : -1], scratch[-1]
        loads = Loads(sems)
        for (x, weight, across), (start, count, by_gap), x_ref, w_ref in zip(terms, picks, xs, ws):
            for n, gap in enumerate(gaps):
                if by_gap:
                    source = ins[start + n]
                else:
                    source = ins[start].at[pl.ds(block_row(at, gap, T), T)]
                loads.add("x", source, x_ref.at[pl.ds(n * T, T)])
            weight.load(loads, "w", at, ins[start + count : start + count + len(weight.arrays)], w_ref)
        loads.wait("x")
        loads.wait("w")
        for c in range(4):
            cut = slice(c * (D // 4), (c + 1) * (D // 4))
            total = None
            for (_, _, across), x_ref, w_ref in zip(terms, xs, ws):
                if across:
                    part = dot(x_ref[...], w_ref[cut, :], ((1,), (1,)))
                else:
                    part = dot(x_ref[...], w_ref[:, cut], ((1,), (0,)))
                total = part if total is None else total + part
            for n in range(n_gap):
                stages[n][:, cut] = total[n * T : (n + 1) * T].astype(stages[n].dtype)
        for n, gap in enumerate(gaps):
            target = outs[0].at[pl.ds(block_row(at, gap, T), T)] if ordered else outs[n]
            loads.add("out", stages[n], target)
        loads.wait("out")

    dtypes = [bf16 if gap & 1 or ordered else f32 for gap in gaps]
    outs = call(
        body,
        info,
        arrays,
        [like((n_gap * T, D), bf16)] if ordered else [like((T, D), dtype) for dtype in dtypes],
        [pltpu.VMEM((n_gap * T, width), bf16) for width in widths]
        + [pltpu.VMEM(weight.shape, bf16) for _, weight, _ in terms]
        + [pltpu.VMEM((T, D), dtype) for dtype in dtypes]
        + [pltpu.SemaphoreType.DMA((sum(w.copies for _, w, _ in terms) + (n_term + 1) * n_gap,))],
        name=name,
        after=after,
        cost=2 * n_gap * T * D * sum(widths),
    )
    return outs[0] if ordered else dict(zip(gaps, outs))


def feed_forward(info, hidden, cot, up, down, gaps, after=()):
    n_gap = len(gaps)
    T = hidden[0].shape[0]
    FW = up.shape[1]
    n_up, n_down = len(up.arrays), len(down.arrays)
    arrays = [*(hidden[gap] for gap in gaps), cot, *up.arrays, *down.arrays]

    def body(at, *refs):
        ins, outs = refs[: len(arrays)], refs[len(arrays) : len(arrays) + 3 * n_gap]
        x, g, w_up, w_down, acts, grads, *stages, sems = refs[len(arrays) + 3 * n_gap :]
        loads = Loads(sems)
        up.load(loads, "up", at, ins[n_gap + 1 : n_gap + 1 + n_up], w_up)
        for n in range(n_gap):
            loads.add(("x", n // 2), ins[n], x.at[pl.ds(n * T, T)])
        down.load(loads, "down", at, ins[n_gap + 1 + n_up :], w_down)
        for n, gap in enumerate(gaps):
            source = ins[n_gap].at[pl.ds(block_row(at, gap, T), T)]
            loads.add(("g", n // 2), source, g.at[pl.ds(n * T, T)])
        loads.wait("up")
        for n in range(0, n_gap, 2):
            rows = pl.ds(n * T, 2 * T)
            both = [(m, pl.ds(m * T, T)) for m in (n, n + 1)]
            loads.wait(("x", n // 2))
            pre = dot(x[rows], w_up[...], ((1,), (0,)))
            below = 0.5 * (1.0 + lax.erf(pre * 0.5**0.5))
            acts[rows] = (pre * below).astype(bf16)
            for m, part in both:
                loads.add("out", acts.at[part], outs[m])
            slope = below + pre * jnp.exp(-0.5 * pre * pre) * (0.5 / jnp.pi) ** 0.5
            if n == 0:
                loads.wait("down")
            loads.wait(("g", n // 2))
            grads[rows] = (dot(g[rows], w_down[...], ((1,), (1,))) * slope).astype(bf16)
            for m, part in both:
                loads.add("out", grads.at[part], outs[n_gap + m])
            for c in range(4):
                cut = slice(c * (D // 4), (c + 1) * (D // 4))
                result = dot(grads[rows], w_up[cut, :], ((1,), (1,)))
                for m, part in both:
                    value = result[(m - n) * T : (m - n + 1) * T]
                    stages[m][:, cut] = value.astype(stages[m].dtype)
            for m, part in both:
                loads.add("out", stages[m], outs[2 * n_gap + m])
        loads.wait("out")

    dtypes = [bf16 if gap & 1 else f32 for gap in gaps]
    outs = call(
        body,
        info,
        arrays,
        [like((T, FW), bf16)] * (2 * n_gap) + [like((T, D), dtype) for dtype in dtypes],
        [pltpu.VMEM((n_gap * T, D), bf16)] * 2
        + [pltpu.VMEM(up.shape, bf16), pltpu.VMEM(down.shape, bf16)]
        + [pltpu.VMEM((n_gap * T, FW), bf16)] * 2
        + [pltpu.VMEM((T, D), dtype) for dtype in dtypes]
        + [pltpu.SemaphoreType.DMA((up.copies + down.copies + 5 * n_gap,))],
        name="feed_forward",
        after=after,
        cost=6 * n_gap * T * D * FW,
    )
    return [dict(zip(gaps, outs[n * n_gap : (n + 1) * n_gap])) for n in range(3)]


class Term:
    def __init__(self, x, y, kind=1, shards=False, ordered=True):
        self.x, self.y, self.kind, self.shards, self.ordered = x, y, kind, shards, ordered
        some = x[0] if isinstance(x, dict) else x
        other = y[0] if isinstance(y, dict) else y
        self.tokens = some.shape[0] * (len(x) if isinstance(x, dict) else 1)
        self.columns = some.shape[1] // lax.axis_size("dp")
        self.rows, self.width = self.columns * kind, other.shape[1] // kind
        self.wide = other.shape[1]
        self.xs = list(x.values()) if isinstance(x, dict) else [x]
        self.ys = list(y.values()) if isinstance(y, dict) else [y]
        self.whole = self.columns % 128 != 0
        if self.whole:
            product = dot(self.rows_of(x), self.rows_of(y), ((0,), (0,)))
            self.xs, self.ys = [product.astype(bf16)], []

    def rows_of(self, held):
        if not isinstance(held, dict):
            return held
        rows = held[0].shape[0]
        out = jnp.zeros((len(held) * rows, held[0].shape[1]), bf16)
        for gap, part in held.items():
            start = (lax.axis_index("seq") ^ gap if self.ordered else gap) * rows
            out = lax.dynamic_update_slice_in_dim(out, part, start, 0)
        return out

    def spread(self, at, which, refs, target, cols=None):
        held = self.x if which == "x" else self.y
        for gap, ref in zip(held if isinstance(held, dict) else [None], refs):
            source = ref if cols is None else ref.at[:, cols]
            if gap is None:
                yield source, target
                continue
            rows = ref.shape[0]
            start = block_row(at, gap, rows) if self.ordered else gap * rows
            yield source, target.at[pl.ds(start, rows)]


class Scatter:
    def __init__(self, info, terms, name):
        self.info, self.terms, self.name = info, terms, name
        self.size = lax.axis_size("dp")
        self.ahead, self.back = ring_moves(self.size)
        self.rows = terms[0].rows
        self.cols = sum(term.width for term in terms)
        self.hop = 0
        self.last = ()

    def pieces(self, which, got, write, outs, after=()):
        terms, n_got, n_out, n_w = self.terms, len(got), len(outs), len(which)
        arrays = [a for term in terms for a in (*term.xs, *term.ys)]

        def body(at, *refs):
            ins, recvs = refs[: len(arrays)], refs[len(arrays) : len(arrays) + n_got]
            results = refs[len(arrays) + n_got : len(arrays) + n_got + n_out]
            scratch, sems = refs[len(arrays) + n_got + n_out : -1], refs[-1]
            held = scratch[:n_got]
            buffers = scratch[n_got:]
            loads = Loads(sems)
            start = 0
            for i, term in enumerate(terms):
                x_refs = ins[start : start + len(term.xs)]
                y_refs = ins[start + len(term.xs) : start + len(term.xs) + len(term.ys)]
                start += len(term.xs) + len(term.ys)
                y_buf, x_buf = buffers[2 * i : 2 * i + 2]
                for n, k in enumerate(which):
                    mine = pl.ds(n * term.columns, term.columns)
                    x_part = x_buf.at[mine] if term.whole else x_buf.at[:, mine]
                    place = at[1 + k + (self.size if term.shards else 0)]
                    cols = pl.ds(pl.multiple_of(place * term.columns, term.columns), term.columns)
                    if term.whole:
                        loads.add(i, x_refs[0].at[cols], x_part)
                        continue
                    for source, target in term.spread(at, "x", x_refs, x_part, cols):
                        loads.add(i, source, target)
                for source, target in term.spread(at, "y", y_refs, y_buf) if y_refs else ():
                    loads.add(i, source, target)
            for source, target in zip(recvs, held):
                loads.add("got", source, target)
            loads.wait("got")
            column = 0
            for i, term in enumerate(terms):
                y_buf, x_buf = buffers[2 * i : 2 * i + 2]
                loads.wait(i)
                for c in range(term.kind):
                    cols = slice(c * term.width, (c + 1) * term.width)
                    if term.whole:
                        values = x_buf[:, cols].astype(f32)
                    else:
                        values = dot(x_buf[...], y_buf[:, cols], ((0,), (0,)))
                    for n in range(n_w):
                        piece = values[n * term.columns : (n + 1) * term.columns]
                        write(n, c * term.columns, term.columns, column, piece, held, results)
                column += term.width

        scratch = [pltpu.VMEM(x.shape, x.dtype) for x in got]
        for term in terms:
            scratch += [pltpu.VMEM((8, 128) if term.whole else (term.tokens, term.wide), bf16)]
            many = n_w * term.columns
            scratch += [pltpu.VMEM((many, term.wide) if term.whole else (term.tokens, many), bf16)]
        copies = n_got + sum(n_w * len(t.xs) + len(t.ys) for t in terms)
        return call(
            body,
            self.info,
            [*arrays, *got],
            outs,
            [*scratch, pltpu.SemaphoreType.DMA((copies,))],
            in_specs=[ANY] * (len(arrays) + n_got),
            out_specs=[VMEM] * n_out,
            name=self.name,
            after=after,
            cost=2 * n_w * sum(t.tokens * t.columns * t.wide for t in terms),
        )

    def step(self, *after):
        m, rows, half = self.size // 2, self.rows, self.rows // 2
        k = m - self.hop
        self.hop += 1

        def write(n, row, count, column, values, got, outs):
            width = values.shape[1]
            for side in range(2) if k == m else [n]:
                for lo, hi in ((0, half), (half, rows)):
                    low, high = max(row, lo), min(row + count, hi)
                    if low >= high or (k == m and lo != side * half):
                        continue
                    part = values[low - row : high - row]
                    cols = slice(column, column + width)
                    if k < m - 1:
                        part = part + got[n][low:high, cols].astype(f32)
                    elif k == m - 1 and lo == n * half:
                        part = part + got[n][low - lo : high - lo, cols].astype(f32)
                    at = lo if k == m else 0
                    outs[side][low - at : high - at, cols] = part.astype(bf16)

        shape = like((half if k == m else rows, self.cols), bf16)
        which = [m] if k == m else [k, self.size - k]
        a, b = self.pieces(which, self.last, write, [shape, shape], after)
        self.sent = (a, b)
        self.last = (lax.ppermute(a, "dp", self.back), lax.ppermute(b, "dp", self.ahead))
        return self

    def own(self, widths, dtypes, after=()):
        while self.hop < self.size // 2:
            self.step()

        def write(n, row, count, column, values, got, outs):
            width = values.shape[1]
            total = values
            for ref in got:
                total = total + ref[row : row + count, column : column + width].astype(f32)
            start = 0
            for out, wide in zip(outs, widths):
                low, high = max(start, column), min(start + wide, column + width)
                if low < high:
                    part = total[:, low - column : high - column]
                    out[row : row + count, low - start : high - start] = part.astype(out.dtype)
                start += wide

        outs = [like((self.rows, w), t) for w, t in zip(widths, dtypes)]
        return self.pieces([0], self.last, write, outs, after)


def split_columns(info, proj_in, ffn_up, H, QW, VW, FW):
    size = lax.axis_size("seq")
    rows, G = proj_in.shape[0], lax.axis_size("dp")
    FR = FW // G
    aligned = FR % 128 == 0
    if not aligned:
        ffn_up = ffn_up.reshape(rows, G, size, FR).transpose(0, 2, 1, 3).reshape(rows, size * FW)

    def body(at, w_in, w_up, *outs):
        for gap in range(size):
            who = at[0] ^ gap
            qkv, gate = outs[2 * gap : 2 * gap + 2]
            for h in range(H):
                for n in range(2):
                    src = pl.multiple_of(n * D + (who * H + h) * DK, DK)
                    qkv[:, (2 * h + n) * DK : (2 * h + n + 1) * DK] = w_in[:, pl.ds(src, DK)]
            qkv[:, 2 * QW :] = w_in[:, pl.ds(pl.multiple_of(2 * D + who * VW, VW), VW)]
            gate[:, :VW] = w_in[:, pl.ds(pl.multiple_of(2 * D + VD + who * VW, VW), VW)]
            if not aligned:
                gate[:, VW:] = w_up[:, pl.ds(pl.multiple_of(who * FW, FW), FW)]
                continue
            for i in range(G):
                src = pl.multiple_of((i * size + who) * FR, FR)
                gate[:, VW + i * FR : VW + (i + 1) * FR] = w_up[:, pl.ds(src, FR)]

    outs = [like((rows, 2 * QW + VW), bf16), like((rows, VW + FW), bf16)] * size
    return call(
        body,
        info,
        [proj_in, ffn_up],
        outs,
        in_specs=[VMEM] * 2,
        out_specs=[VMEM] * len(outs),
        name="split_columns",
    )


def join_pieces(info, parts, extra, fold, after=(), first=0, width=None):
    size = len(parts)
    rows, width = parts[0].shape[0], width or parts[0].shape[1]
    wide = 0 if extra is None else extra.shape[1] // fold

    def body(at, *refs):
        out = refs[-1]
        for gap in range(size):
            out[pl.ds(pl.multiple_of((at[0] ^ gap) * rows, rows), rows), :width] = refs[gap][:, first : first + width]
        if extra is not None:
            short = size * rows // fold
            for c in range(fold):
                out[c * short : (c + 1) * short, width:] = refs[size][:, c * wide : (c + 1) * wide]

    ins = parts if extra is None else [*parts, extra]
    return call(
        body,
        info,
        ins,
        like((size * rows, width + wide), bf16),
        in_specs=[VMEM] * len(ins),
        out_specs=VMEM,
        name="join_pieces",
        after=after,
    )


def exchange_rows(info, x):
    size = lax.axis_size("seq")
    rows = x.shape[0] // size

    def body(at, src, *outs):
        for gap in range(size):
            outs[gap][...] = src[pl.ds(pl.multiple_of((at[0] ^ gap) * rows, rows), rows), :]

    outs = [like((rows, x.shape[1]), x.dtype)] * size
    parts = call(
        body, info, [x], outs, in_specs=[VMEM], out_specs=[VMEM] * size, name="exchange_rows"
    )
    return [part if gap == 0 else swap_seq(part, gap) for gap, part in enumerate(parts)]


def join_in_columns(info, qkvs, gates, H, QW, VW, after=()):
    size = len(qkvs)
    rows = qkvs[0].shape[0]

    def body(at, *refs):
        out = refs[-1]
        for gap in range(size):
            who = at[0] ^ gap
            qkv, gate = refs[gap], refs[size + gap]
            for h in range(H):
                for n in range(2):
                    to = pl.multiple_of(n * D + (who * H + h) * DK, DK)
                    part = qkv[:, (2 * h + n) * DK : (2 * h + n + 1) * DK]
                    out[:, pl.ds(to, DK)] = part.astype(f32)
            out[:, pl.ds(pl.multiple_of(2 * D + who * VW, VW), VW)] = qkv[:, 2 * QW :].astype(f32)
            to = pl.multiple_of(2 * D + VD + who * VW, VW)
            out[:, pl.ds(to, VW)] = gate[...].astype(f32)

    ins = [*qkvs, *gates]
    return call(
        body,
        info,
        ins,
        like((rows, 2 * D + 2 * VD), f32),
        in_specs=[VMEM] * len(ins),
        out_specs=VMEM,
        name="join_in_columns",
        after=after,
    )


def join_up_columns(info, ups, G, after=()):
    size = len(ups)
    rows, FW = ups[0].shape
    FR = FW // G
    aligned = FR % 128 == 0

    def body(at, *refs):
        out = refs[-1]
        for gap in range(size):
            who = at[0] ^ gap
            if not aligned:
                to = pl.multiple_of(who * FW, FW)
                out[:, pl.ds(to, FW)] = refs[gap][...].astype(f32)
                continue
            for i in range(G):
                to = pl.multiple_of((i * size + who) * FR, FR)
                out[:, pl.ds(to, FR)] = refs[gap][:, i * FR : (i + 1) * FR].astype(f32)

    out = call(
        body,
        info,
        ups,
        like((rows, size * FW), f32),
        in_specs=[VMEM] * size,
        out_specs=VMEM,
        name="join_up_columns",
        after=after,
    )
    if aligned:
        return out
    return out.reshape(rows, size, G, FR).transpose(0, 2, 1, 3).reshape(rows, size * FW)


def decays(log_decay, T):
    step = lax.broadcasted_iota(jnp.int32, (T, 1), 0).astype(f32)
    decay_query = jnp.exp((step + 1.0) * log_decay)
    decay_key = jnp.exp((T - 1.0 - step) * log_decay)
    row = lax.broadcasted_iota(jnp.int32, (T, T), 0)
    column = lax.broadcasted_iota(jnp.int32, (T, T), 1)
    gap = (row - column).astype(f32)
    lower = row >= column
    mask = jnp.where(lower, jnp.exp(jnp.where(lower, gap, 0.0) * log_decay), 0.0)
    return decay_query, decay_key, mask


def turn(u, cosine, sine):
    a, c = u[:, :HALF], u[:, HALF:]
    return jnp.concatenate([a * cosine - c * sine, a * sine + c * cosine], axis=1)


def centre(retained):
    average = jnp.mean(retained, axis=-1, keepdims=True)
    centred = retained - average
    spread = jnp.mean(centred * centred, axis=-1, keepdims=True)
    inverse = lax.rsqrt(jnp.maximum(spread, 0.25) + 1e-05)
    return centred, spread, inverse


def retention_forward(info, logs, keep, qk, v, gate, cosine, sine, S, T, H, after=()):
    TG = S * T

    def body(_, logs_ref, keep_ref, qk_ref, v_ref, g_ref, cos_ref, sin_ref, *outs):
        mixed, qk_out, retained_out, state_out, scores_out = outs
        log_decay = logs_ref[pl.program_id(0)]
        decay_query, decay_key, mask = decays(log_decay, T)
        block_decay = jnp.exp(jnp.full((1, 1), T * log_decay, f32))
        carry = jnp.zeros((DK, DV), f32)
        for b in range(S):
            rows = pl.ds(b * T, T)
            co, si = cos_ref[rows], sin_ref[rows]
            q = turn(qk_ref[rows, :DK], co, si).astype(bf16)
            k = (turn(qk_ref[rows, DK:], co, si) * DK ** (-0.5)).astype(bf16)
            qk_out[rows, :DK] = q
            qk_out[rows, DK:] = k
            value = v_ref[rows]
            scores = (dot(q, k, ((1,), (1,))) * mask).astype(bf16)
            scores_out[0, b] = scores
            state = keep_ref[b] * carry
            state_in = state.astype(bf16)
            state_out[0, b] = state_in
            query_decay = (q.astype(f32) * decay_query).astype(bf16)
            key_decay = (k.astype(f32) * decay_key).astype(bf16)
            retained = dot(scores, value, ((1,), (0,))) + dot(query_decay, state_in, ((1,), (0,)))
            retained_out[rows] = retained
            carry = block_decay * state + dot(key_decay, value, ((0,), (0,)))
            centred, _, inverse = centre(retained)
            g = g_ref[rows]
            mixed[rows] = (g * jax.nn.sigmoid(g) * (centred * inverse)).astype(bf16)

    smem = pl.BlockSpec(memory_space=pltpu.SMEM)
    once = lambda width: pl.BlockSpec((TG, width), lambda h, _: (0, 0))
    head = lambda width: pl.BlockSpec((TG, width), lambda h, _: (0, h))
    return call(
        body,
        info,
        [logs, keep, qk, v, gate, cosine, sine],
        [
            like((TG, H * DV), bf16),
            like((TG, 2 * H * DK), bf16),
            like((TG, H * DV), f32),
            like((H, S, DK, DV), bf16),
            like((H, S, T, T), bf16),
        ],
        grid=(H,),
        in_specs=[smem, smem, head(2 * DK), head(DV), head(DV), once(HALF), once(HALF)],
        out_specs=[
            head(DV),
            head(2 * DK),
            head(DV),
            pl.BlockSpec((1, S, DK, DV), lambda h, _: (h, 0, 0, 0)),
            pl.BlockSpec((1, S, T, T), lambda h, _: (h, 0, 0, 0)),
        ],
        name="retention_forward",
        after=after,
        cost=2 * H * S * T * T * (DK + DV) + 4 * H * S * T * DK * DV,
    )


def retention_backward(info, logs, keep, grad_mixed, gate, retained, qk, v, states, scores, cosine, sine, S, T, H, after=()):
    TG = S * T

    def body(_, logs_ref, keep_ref, gm_ref, g_ref, r_ref, qk_ref, v_ref, state_ref, scores_ref, cos_ref, sin_ref, *outs):
        qk_grad, v_grad, g_grad = outs
        log_decay = logs_ref[pl.program_id(0)]
        decay_query, decay_key, mask = decays(log_decay, T)
        block_decay = jnp.exp(jnp.full((1, 1), T * log_decay, f32))
        later = jnp.zeros((DK, DV), f32)
        for b in reversed(range(S)):
            rows = pl.ds(b * T, T)
            gm, g = gm_ref[rows], g_ref[rows]
            centred, spread, inverse = centre(r_ref[rows])
            sig = jax.nn.sigmoid(g)
            swish = g * sig
            normed = centred * inverse
            g_grad[rows] = (gm * normed * (sig + swish * (1.0 - sig))).astype(bf16)
            grad_normed = gm * swish
            passes = jnp.where(spread > 0.25, 1.0, jnp.where(spread == 0.25, 0.5, 0.0))
            pull = jnp.sum(grad_normed * centred, axis=-1, keepdims=True)
            pull = pull * (-inverse * inverse * inverse / DV) * passes
            grad_centred = grad_normed * inverse + pull * centred
            grad_ret = grad_centred - jnp.mean(grad_centred, axis=-1, keepdims=True)
            grad_ret = grad_ret.astype(bf16)
            q, k, value = qk_ref[rows, :DK], qk_ref[rows, DK:], v_ref[rows]
            query_decay = (q.astype(f32) * decay_query).astype(bf16)
            key_decay = (k.astype(f32) * decay_key).astype(bf16)
            grad_raw = (dot(grad_ret, value, ((1,), (1,))) * mask).astype(bf16)
            local = later.astype(bf16)
            grad_q = dot(grad_raw, k, ((1,), (0,)))
            grad_q = grad_q + decay_query * dot(grad_ret, state_ref[0, b], ((1,), (1,)))
            grad_k = dot(grad_raw, q, ((0,), (0,)))
            grad_k = grad_k + decay_key * dot(value, local, ((1,), (1,)))
            grad_v = dot(scores_ref[0, b], grad_ret, ((0,), (0,)))
            grad_v = grad_v + dot(key_decay, local, ((1,), (0,)))
            co, si = cos_ref[rows], -sin_ref[rows]
            qk_grad[rows, :DK] = turn(grad_q, co, si).astype(bf16)
            qk_grad[rows, DK:] = turn(grad_k * DK ** (-0.5), co, si).astype(bf16)
            v_grad[rows] = grad_v.astype(bf16)
            if b > 0:
                here = dot(query_decay, grad_ret, ((0,), (0,)))
                later = keep_ref[b] * (here + block_decay * later)

    smem = pl.BlockSpec(memory_space=pltpu.SMEM)
    once = lambda width: pl.BlockSpec((TG, width), lambda h, _: (0, 0))
    head = lambda width: pl.BlockSpec((TG, width), lambda h, _: (0, h))
    return call(
        body,
        info,
        [logs, keep, grad_mixed, gate, retained, qk, v, states, scores, cosine, sine],
        [like((TG, 2 * H * DK), bf16), like((TG, H * DV), bf16), like((TG, H * DV), bf16)],
        grid=(H,),
        in_specs=[
            smem,
            smem,
            head(DV),
            head(DV),
            head(DV),
            head(2 * DK),
            head(DV),
            pl.BlockSpec((1, S, DK, DV), lambda h, _: (h, 0, 0, 0)),
            pl.BlockSpec((1, S, T, T), lambda h, _: (h, 0, 0, 0)),
            once(HALF),
            once(HALF),
        ],
        out_specs=[head(2 * DK), head(DV), head(DV)],
        name="retention_backward",
        after=after,
        cost=4 * H * S * T * T * (DK + DV) + 8 * H * S * T * DK * DV,
    )


def local(
    layer_in,
    out_grad,
    seq_start,
    norm1_gain,
    norm1_shift,
    proj_in,
    proj_out,
    norm2_gain,
    norm2_shift,
    ffn_up,
    ffn_down,
):
    S, G = lax.axis_size("seq"), lax.axis_size("dp")
    me = lax.axis_index("seq")
    T = layer_in.shape[0]
    TG = S * T
    H = HEADS // S
    QW, VW = H * DK, H * DV
    FW = G * ffn_down.shape[0]
    fold = S // 2
    info = make_info()

    to_rank = [(j * G + t, shard_place(t, G) * S + j) for j in range(S) for t in range(G)]
    parts = split_columns(info, proj_in, ffn_up, H, QW, VW, FW)

    vectors = jnp.stack([norm1_gain, norm1_shift, norm2_gain, norm2_shift])
    norms = GatherAll(tie(vectors, parts[0]))
    while norms.gaps:
        norms.step()
    norms = norms.held.transpose(2, 0, 1, 3).reshape(4, 1, D).astype(f32)
    gain_one, shift_one, gain_two, shift_two = norms

    out_piece = lax.ppermute(tie(proj_out, norms), BOTH, to_rank)

    def exchanged(own, *after):
        return [own[0]] + [
            swap_seq(tie(x, *after) if after else x, gap) for gap, x in enumerate(own) if gap
        ]

    qkv_parts = exchanged(parts[0::2])
    qkv_ring = Gather(join_pieces(info, qkv_parts, None, fold, (norms,))).step()
    (normed_one,) = norm_forward(layer_in, gain_one, shift_one, (), (qkv_ring.got[0],))
    hidden_one = gather_seq(normed_one)
    early = (*qkv_ring.last, hidden_one[S // 2])
    qkv_ring.step()
    gate_parts = exchanged(parts[1::2], *early)
    cot = lax.all_gather(tie(out_grad, *early), "seq", axis=0, tiled=True)
    qkv_ring.step().step()
    gate_piece = join_pieces(
        info, gate_parts, None, fold, (*qkv_ring.sent, hidden_one[1], hidden_one[S - 1]), 0, VW
    )
    gate_ring = Gather(gate_piece).step().step(*qkv_ring.last)
    out_ring = Gather(tie(out_piece, *gate_ring.sent)).step()

    factor = jnp.power(10000.0, -jnp.arange(HALF, dtype=f32) / (HALF - 1))
    angles = jnp.arange(TG, dtype=f32)[:, None] * factor[None, :]
    cosine, sine = jnp.cos(angles), jnp.sin(angles)
    log_all = jnp.log(1.0 - jnp.exp2(-5.0 - jnp.arange(HEADS, dtype=f32)))
    logs = lax.dynamic_slice_in_dim(log_all, me * H, H)
    keep = 1.0 - seq_start[0].astype(f32)

    w_qkv = Weight(qkv_ring)
    qk_pre, values = tokens_times(
        info,
        hidden_one,
        w_qkv,
        [(0, 2 * QW, f32), (2 * QW, VW, bf16)],
        False,
        "project_qkv",
        (*gate_ring.sent, *out_ring.sent, cosine, sine),
    )
    w_qk = Weight(qkv_ring, 1, 0, 2 * QW)
    w_v = Weight(qkv_ring, 1, 2 * QW, VW)
    gate_ring.step(qk_pre)
    out_ring.step(qk_pre)
    gate_ring.step()
    out_ring.step()
    w_g = Weight(gate_ring)
    (gate_pre,) = tokens_times(
        info, hidden_one, w_g, [(0, VW, f32)], False, "project_gate", out_ring.sent
    )
    out_ring.step(gate_pre)
    ffn_ring = Gather(join_pieces(info, gate_parts, ffn_down, fold, out_ring.sent, VW, FW)).step()
    mixed, qk, retained, states, scores = retention_forward(
        info, logs, keep, qk_pre, values, gate_pre, cosine, sine, S, T, H,
        (*out_ring.sent, ffn_ring.got[0]),
    )
    w_out = Weight(out_ring, shards=True)
    odd, even = [g for g in reversed(range(S)) if g & 1], [g for g in reversed(range(S)) if not g & 1]
    ffn_ring.step()
    attn, attn_got = partial_rows(info, [(mixed, w_out, False)], odd, "attn_odd", (ffn_ring.got[0],)), {}
    swap_odd(attn, attn_got)
    attn |= partial_rows(info, [(mixed, w_out, False)], even, "attn_even", (attn[odd[-1]],))
    attn, attn_sent = scatter_seq(attn, attn_got)
    ffn_ring.step()
    middle, normed_two = norm_forward(layer_in, gain_two, shift_two, attn, ffn_ring.sent)
    ffn_ring.step()
    w_up = Weight(ffn_ring, 1, 0, FW)
    w_down = Weight(ffn_ring, fold, FW, 2 * D // S)
    near, far = [1, 0], list(reversed(range(2, S)))
    hidden_two = {0: normed_two, 1: swap_seq(normed_two, 1)}
    active, grad_up, grad_two = feed_forward(info, hidden_two, cot, w_up, w_down, near)
    hidden_two |= far_blocks(normed_two)
    two_got = {}
    swap_odd(grad_two, two_got)
    more = feed_forward(info, hidden_two, cot, w_up, w_down, far, (grad_two[0],))
    swap_odd(more[2], two_got)
    for whole, extra in zip((active, grad_up, grad_two), more):
        whole |= extra

    grad_two, two_sent = scatter_seq(grad_two, two_got)
    order = sorted(active)
    active, grad_up, hidden_two, hidden_one = (
        {gap: x[gap] for gap in order} for x in (active, grad_up, hidden_two, hidden_one)
    )
    ffn_sum = Scatter(
        info,
        [Term(hidden_two, grad_up), Term(active, cot, fold)],
        "ffn_hop",
    ).step(two_sent).step()
    grad_middle, grad_attn, two_sums = norm_backward(
        middle, gain_two, out_grad, grad_two, (f32, bf16), ffn_sum.sent
    )

    down = partial_rows(
        info, [(active, w_down, False)], odd + even, "down", (grad_attn,), True
    )
    grad_attn = gather_seq(grad_attn, down, *ffn_sum.last)
    ffn_sum.step(grad_attn[S // 2])
    (grad_mixed,) = tokens_times(info, grad_attn, w_out, [(0, VW, f32)], True, "grad_mixed", ffn_sum.sent)
    down = lax.psum_scatter(tie(down, *ffn_sum.sent), "seq", scatter_dimension=0, tiled=True)
    grad_qk, grad_v, grad_g = retention_backward(
        info, logs, keep, grad_mixed, gate_pre, retained, qk, values, states, scores, cosine, sine, S, T, H,
        ffn_sum.sent,
    )
    gate_sum = Scatter(
        info, [Term(hidden_one, grad_g), Term(mixed, grad_attn, fold, True)], "gate_hop"
    ).step(grad_g)
    ffn_sum.step(*gate_sum.sent)
    qkv_sum = Scatter(info, [Term(hidden_one, grad_qk), Term(hidden_one, grad_v)], "qkv_hop")
    qkv_sum.step(*ffn_sum.sent)
    terms_one = [(grad_g, w_g, True), (grad_v, w_v, True), (grad_qk, w_qk, True)]
    grad_one, one_got = partial_rows(info, terms_one, odd, "grad_one_odd", qkv_sum.sent), {}
    swap_odd(grad_one, one_got)
    gate_sum.step(grad_one[odd[-1]])
    grad_one |= partial_rows(info, terms_one, even, "grad_one_even", gate_sum.sent)
    grad_one, one_sent = scatter_seq(grad_one, one_got)
    qkv_sum.step(one_sent)
    up_own, down_own = ffn_sum.own((FW, 2 * D // S), (bf16, f32), qkv_sum.sent)
    up_parts = exchange_rows(info, up_own)
    layer_out = add_up([down, middle], bf16, (up_parts[0],))
    gate_sum.step(layer_out)
    in_grad, one_sums = norm_backward(
        layer_in, gain_one, grad_middle, grad_one, (bf16,), gate_sum.sent
    )
    norm_terms = jnp.stack([one_sums[0], one_sums[1], two_sums[0], two_sums[1]])
    down_grad = jnp.concatenate(jnp.split(tie(down_own, in_grad), fold, axis=0), axis=1)
    qkv_sum.step(in_grad)
    gate_sum.step(*qkv_sum.sent)
    up_grad = join_up_columns(info, up_parts, G, gate_sum.sent)
    norm_sum = ScatterAll(norm_terms.reshape(4, G, S, -1).transpose(1, 2, 0, 3))
    for _ in seq_gaps(S):
        norm_sum.step()
    qkv_sum.step(up_grad, norm_sum.held)
    g_own, out_own = gate_sum.own((VW, 2 * D // S), (bf16, bf16), qkv_sum.sent)
    g_parts = exchange_rows(info, g_own)
    out_grad_w = lax.ppermute(out_own, BOTH, [(b, a) for a, b in to_rank])
    (qkv_own,) = qkv_sum.own((2 * QW + VW,), (bf16,), (g_parts[0],))
    qkv_parts = exchange_rows(info, qkv_own)
    norm_sum.held = tie(norm_sum.held, qkv_parts[S // 2], out_grad_w)
    while norm_sum.gaps:
        norm_sum.step()
    norm_grads = norm_sum.held[0, 0]
    in_grad_w = join_in_columns(info, qkv_parts, g_parts, H, QW, VW)
    out_grad_w = jnp.concatenate(jnp.split(out_grad_w, fold, axis=0), axis=1).astype(f32)
    return (
        layer_out,
        in_grad,
        norm_grads[0],
        norm_grads[1],
        in_grad_w,
        out_grad_w,
        norm_grads[2],
        norm_grads[3],
        up_grad,
        down_grad,
    )


def solution(mesh):
    rows, vector = P(BOTH, None), P(BOTH)
    in_specs = (rows, rows, P("dp", None), vector, vector, rows, rows, vector, vector, rows, rows)
    out_specs = (rows, rows, vector, vector, rows, rows, vector, vector, rows, rows)
    return jax.shard_map(local, mesh=mesh, in_specs=in_specs, out_specs=out_specs, check_vma=False)
```

```python
import functools

import jax
import jax.numpy as jnp
from jax import lax
from jax.experimental import pallas as pl
from jax.experimental.pallas import tpu as pltpu
from jax.sharding import PartitionSpec as P

D = 2048
HEADS = 8
VD = 4096
DK = 256
DV = 512
HALF = DK // 2
BOTH = ("dp", "seq")
f32 = jnp.float32
bf16 = jnp.bfloat16
ANY = pl.BlockSpec(memory_space=pl.ANY)
VMEM = pl.BlockSpec(memory_space=pltpu.VMEM)
LIMIT = 58 << 20
DEPTH = 4


def dot(a, b, dims):
    return lax.dot_general(a, b, (dims, ((), ())), preferred_element_type=f32)


def call(body, info, ins, outs, scratch=(), grid=(), in_specs=None, out_specs=None, name=None, cost=None, after=()):
    many = isinstance(outs, (list, tuple))
    n_in, n_after = len(ins), len(after)
    ins, after = list(ins), list(after)

    def inner(at, *refs):
        body(at, *refs[:n_in], *refs[n_in + n_after :])

    spec = pltpu.PrefetchScalarGridSpec(
        num_scalar_prefetch=1,
        grid=grid,
        in_specs=list(in_specs or [ANY] * n_in) + [ANY] * n_after,
        out_specs=out_specs or ([ANY] * len(outs) if many else ANY),
        scratch_shapes=list(scratch),
    )
    moved = sum(x.size * x.dtype.itemsize for x in (*ins, *(outs if many else [outs])))
    return pl.pallas_call(
        inner,
        out_shape=outs,
        grid_spec=spec,
        name=name,
        cost_estimate=pl.CostEstimate(
            flops=cost or 0, bytes_accessed=int(moved), transcendentals=0
        ),
        compiler_params=pltpu.CompilerParams(vmem_limit_bytes=LIMIT),
    )(info, *ins, *after)


def tie(x, *after):
    return pl.pallas_call(
        lambda *refs: None,
        out_shape=like(x.shape, x.dtype),
        in_specs=[ANY] * (1 + len(after)),
        out_specs=ANY,
        input_output_aliases={0: 0},
        name="tie",
    )(x, *after)


def like(shape, dtype):
    return jax.ShapeDtypeStruct(shape, dtype)


def seq_gaps(size):
    return [1 << b for b in range(size.bit_length() - 1)]


def swap_seq(x, gap):
    size = lax.axis_size("seq")
    return lax.ppermute(x, "seq", [(i, i ^ gap) for i in range(size)])


class Loads:
    def __init__(self, sems):
        self.sems, self.count, self.groups = sems, 0, {}

    def add(self, group, source, target):
        copy = pltpu.make_async_copy(source, target, self.sems.at[self.count])
        self.groups.setdefault(group, []).append(copy)
        self.count += 1
        copy.start()

    def wait(self, group):
        for copy in self.groups.pop(group, []):
            copy.wait()


def block_row(at, gap, rows):
    return pl.multiple_of((at[0] ^ gap) * rows, rows)


def gather_seq(x, *after):
    held = {0: x}
    for gap in reversed(seq_gaps(lax.axis_size("seq"))):
        new = {g ^ gap: swap_seq(part, gap) for g, part in list(held.items())}
        if after and gap == lax.axis_size("seq") // 2:
            new = {g: tie(part, *after) for g, part in new.items()}
        held.update(new)
    return held


def far_blocks(x, *after):
    held = {0: x}
    for gap in reversed(seq_gaps(lax.axis_size("seq"))[1:]):
        held.update({g ^ gap: tie(swap_seq(part, gap), *after) for g, part in list(held.items())})
    del held[0]
    return held | {g ^ 1: swap_seq(part, 1) for g, part in held.items()}


ROWS = 128


def plain(body, ins, outs, grid, in_specs, out_specs, name, after=()):
    n_in = len(ins)

    def inner(*refs):
        body(*refs[:n_in], *refs[n_in + len(after) :])

    return pl.pallas_call(
        inner,
        out_shape=outs,
        grid=grid,
        in_specs=[*in_specs, *[ANY] * len(after)],
        out_specs=out_specs,
        name=name,
        compiler_params=pltpu.CompilerParams(vmem_limit_bytes=LIMIT),
    )(*ins, *after)


def tile_of(rows, cols):
    return pl.BlockSpec((rows, cols), lambda i: (i, 0))


def add_up(parts, dtype, after=()):
    T, C = parts[0].shape

    def body(*refs):
        total = refs[0][...].astype(f32)
        for ref in refs[1:-1]:
            total = total + ref[...].astype(f32)
        refs[-1][...] = total.astype(dtype)

    return plain(
        body,
        parts,
        like((T, C), dtype),
        (T // ROWS,),
        [tile_of(ROWS, C)] * len(parts),
        tile_of(ROWS, C),
        "add_up",
        after,
    )


def swap_odd(parts, got):
    for gap in sorted((gap for gap in parts if gap & 1), reverse=True):
        got.setdefault(gap ^ 1, []).append(swap_seq(parts[gap], 1))


def scatter_seq(parts, got, after=()):
    size = lax.axis_size("seq")
    sent = parts[0]
    bit = 2
    while bit < size:
        for gap in [gap for gap in reversed(range(size)) if gap & bit and gap % bit == 0]:
            sent = add_up([parts[gap], *got[gap]], bf16, after)
            got.setdefault(gap ^ bit, []).append(swap_seq(sent, bit))
        bit *= 2
    return [parts[0], *got[0]], sent


def norm_forward(rows, gain, shift, more=(), after=()):
    T, C = rows.shape
    wide = len(more) > 0

    def body(rows_ref, gain_ref, shift_ref, *refs):
        outs = refs[-2:] if wide else refs[-1:]
        total = rows_ref[...].astype(f32)
        for ref in refs[: len(more)]:
            total = total + ref[...].astype(f32)
        if wide:
            outs[0][...] = total
        centred = total - jnp.mean(total, axis=-1, keepdims=True)
        spread = jnp.mean(centred * centred, axis=-1, keepdims=True)
        normed = centred * lax.rsqrt(spread + 1e-05) * gain_ref[...] + shift_ref[...]
        outs[-1][...] = normed.astype(bf16)

    vector = pl.BlockSpec((1, C), lambda i: (0, 0))
    outs = ([like((T, C), f32)] if wide else []) + [like((T, C), bf16)]
    return plain(
        body,
        [rows, gain, shift, *more],
        outs,
        (T // ROWS,),
        [tile_of(ROWS, C), vector, vector] + [tile_of(ROWS, C)] * len(more),
        [tile_of(ROWS, C)] * len(outs),
        "norm_forward",
        after,
    )


def norm_backward(rows, gain, base, parts, dtypes, after=()):
    T, C = rows.shape
    n = len(parts)

    def body(rows_ref, gain_ref, base_ref, *refs):
        grad = refs[0][...].astype(f32)
        for ref in refs[1:n]:
            grad = grad + ref[...].astype(f32)
        total = rows_ref[...].astype(f32)
        centred = total - jnp.mean(total, axis=-1, keepdims=True)
        inverse = lax.rsqrt(jnp.mean(centred * centred, axis=-1, keepdims=True) + 1e-05)
        normed = centred * inverse
        inner = grad * gain_ref[...]
        pull = inner - jnp.mean(inner, axis=-1, keepdims=True)
        pull = pull - normed * jnp.mean(inner * normed, axis=-1, keepdims=True)
        result = base_ref[...].astype(f32) + inverse * pull
        for out in refs[n:-1]:
            out[...] = result.astype(out.dtype)
        sums = refs[-1]

        @pl.when(pl.program_id(0) == 0)
        def _():
            sums[...] = jnp.zeros_like(sums)

        sums[0:1, :] += jnp.sum(grad * normed, axis=0, keepdims=True)
        sums[1:2, :] += jnp.sum(grad, axis=0, keepdims=True)

    vector = pl.BlockSpec((1, C), lambda i: (0, 0))
    outs = [like((T, C), t) for t in dtypes] + [like((8, C), f32)]
    return plain(
        body,
        [rows, gain, base, *parts],
        outs,
        (T // ROWS,),
        [tile_of(ROWS, C), vector, tile_of(ROWS, C)] + [tile_of(ROWS, C)] * n,
        [tile_of(ROWS, C)] * len(dtypes) + [pl.BlockSpec((8, C), lambda i: (0, 0))],
        "norm_backward",
        after,
    )


def swap_all(x, gap):
    size = lax.axis_size("dp") * lax.axis_size("seq")
    return lax.ppermute(x, BOTH, [(i, i ^ gap) for i in range(size)])


def flat_index():
    return lax.axis_index("dp") * lax.axis_size("seq") + lax.axis_index("seq")


class GatherAll:
    def __init__(self, x):
        S, G = lax.axis_size("seq"), lax.axis_size("dp")
        self.held, self.gaps = x[None, None], [S * g for g in seq_gaps(G)] + seq_gaps(S)

    def step(self, *after):
        gap, *self.gaps = self.gaps
        axis = 0 if gap >= lax.axis_size("seq") else 1
        other = swap_all(self.held, gap)
        if after:
            other = tie(other, *after)
        self.held = jnp.where(
            (flat_index() & gap) != 0,
            jnp.concatenate([other, self.held], axis=axis),
            jnp.concatenate([self.held, other], axis=axis),
        )
        return self


class ScatterAll:
    def __init__(self, x):
        S, G = lax.axis_size("seq"), lax.axis_size("dp")
        self.held, self.gaps = x, seq_gaps(S)[::-1] + [S * g for g in seq_gaps(G)[::-1]]

    def step(self):
        gap, *self.gaps = self.gaps
        axis = 0 if gap >= lax.axis_size("seq") else 1
        low, high = jnp.split(self.held, 2, axis=axis)
        upper = (flat_index() & gap) != 0
        self.held = jnp.where(upper, high, low) + swap_all(jnp.where(upper, low, high), gap)
        return self


def cycle(size):
    depth = DEPTH
    width = size // depth
    walk = [(0, x) for x in range(width)]
    for turn, x in enumerate(reversed(range(width))):
        column = [(z, x) for z in range(1, depth)]
        walk += column if turn % 2 == 0 else column[::-1]
    return [z * width + x for z, x in walk]


def ring_moves(size):
    walk = cycle(size)
    ahead = [(walk[i], walk[(i + 1) % size]) for i in range(size)]
    return ahead, [(b, a) for a, b in ahead]


def shard_place(t, size):
    return (t % DEPTH) * (size // DEPTH) + t // DEPTH


def make_info():
    size = lax.axis_size("dp")
    walk = cycle(size)
    table = [[walk[(walk.index(i) - k) % size] for k in range(size)] for i in range(size)]
    shard = {shard_place(t, size): t for t in range(size)}
    table = [row + [shard[i] for i in row] for row in table]
    row = lax.dynamic_index_in_dim(jnp.array(table, jnp.int32), lax.axis_index("dp"), 0, False)
    return jnp.concatenate([lax.axis_index("seq").astype(jnp.int32)[None], row])


class Gather:
    def __init__(self, x):
        self.size = lax.axis_size("dp")
        self.ahead, self.back = ring_moves(self.size)
        self.got = {0: x}
        self.hop = 0

    def step(self, *after):
        size, half = self.size, self.got[0].shape[0] // 2
        self.hop += 1
        k = self.hop
        if after and k > 1:
            for n in {k - 1, (size - k + 1) % size}:
                self.got[n] = tie(self.got[n], *after)
        a, b = self.got[k - 1], self.got[(size - k + 1) % size]
        if k == size // 2:
            a, b = a[:half], b[half:]
        self.sent = (a, b)
        a, b = lax.ppermute(a, "dp", self.ahead), lax.ppermute(b, "dp", self.back)
        if k == size // 2:
            self.halves = (a, b)
        else:
            self.got[k], self.got[size - k] = a, b
        self.last = (a, b)
        return self


def unfold(ref, row, rows, fold, width, start, r0, n):
    views = []
    for c in range(fold):
        lo, hi = max(r0, c * rows), min(r0 + n, (c + 1) * rows)
        if lo < hi:
            views.append((lo - r0, hi - lo, ref.at[pl.ds(row + lo - c * rows, hi - lo), pl.ds(c * width, width)]))
    return views


def piece_views(refs, kinds, places, r0, n, rows):
    out = []
    column = 0
    places = places if isinstance(places, list) else [places] * len(refs)
    for ref, kind, place in zip(refs, kinds, places):
        if kind == 1:
            start = pl.multiple_of(place * rows + r0, n)
            out.append((0, n, column, ref.shape[1], ref.at[pl.ds(start, n)]))
            column += ref.shape[1]
        else:
            width, short = ref.shape[1] // kind, rows // kind
            row = pl.multiple_of(place * short, short)
            for at, count, view in unfold(ref, row, short, kind, width, 0, r0, n):
                out.append((at, count, column, width, view))
            column += width
    return out


class Weight:
    def __init__(self, ring, kind=1, first=0, width=None, shards=False):
        while ring.hop < ring.size // 2:
            ring.step()
        self.kind, self.first, self.shards, self.size = kind, first, shards, ring.size
        self.rows, cols = ring.got[0].shape
        width = width or cols
        half, middle = self.rows // 2, ring.size // 2
        self.parts = [(k, 0, self.rows, x) for k, x in ring.got.items()]
        self.parts += [(middle, 0, half, ring.halves[0]), (middle, half, half, ring.halves[1])]
        self.shape = (self.size * self.rows // kind, width * kind)
        self.arrays = [x for _, _, _, x in self.parts]
        self.copies = len(self.parts) * kind

    def load(self, loads, group, at, refs, target):
        for (k, r0, n, _), ref in zip(self.parts, refs):
            place = at[1 + k + (self.size if self.shards else 0)]
            for row, count, column, width, view in piece_views([target], [self.kind], place, r0, n, self.rows):
                source = ref.at[pl.ds(row, count), pl.ds(self.first + column, width)]
                loads.add(group, source, view)


def tokens_times(info, held, weight, cols, across, name, after=()):
    gaps = list(held)
    S, (T, K) = len(gaps), held[0].shape
    n_w, n_out = len(weight.arrays), len(cols)

    def body(at, *refs):
        pieces, w_refs, outs = refs[:S], refs[S : S + n_w], refs[S + n_w : S + n_w + n_out]
        x, w, *stages, sems = refs[S + n_w + n_out :]
        loads = Loads(sems)
        weight.load(loads, "w", at, w_refs, w)
        for n, piece in enumerate(pieces):
            loads.add(n // 2, piece, x.at[pl.ds(n * T, T)])
        loads.wait("w")
        for n in range(0, S, 2):
            loads.wait(n // 2)
            rows = pl.ds(n * T, 2 * T)
            for (first, width, dtype), out, stage in zip(cols, outs, stages):
                if across:
                    result = dot(x[rows], w[first : first + width, :], ((1,), (1,)))
                else:
                    result = dot(x[rows], w[:, first : first + width], ((1,), (0,)))
                stage[rows] = result.astype(dtype)
                for m in (n, n + 1):
                    target = out.at[pl.ds(block_row(at, gaps[m], T), T)]
                    loads.add("out", stage.at[pl.ds(m * T, T)], target)
        loads.wait("out")

    return call(
        body,
        info,
        [*held.values(), *weight.arrays],
        [like((S * T, width), dtype) for _, width, dtype in cols],
        [pltpu.VMEM((S * T, K), bf16), pltpu.VMEM(weight.shape, bf16)]
        + [pltpu.VMEM((S * T, width), dtype) for _, width, dtype in cols]
        + [pltpu.SemaphoreType.DMA((S + weight.copies + S * n_out,))],
        name=name,
        after=after,
        cost=2 * S * T * K * sum(width for _, width, _ in cols),
    )


def partial_rows(info, terms, gaps, name, after=(), ordered=False):
    arrays, picks = [], []
    for x, weight, _ in terms:
        mine = [x[gap] for gap in gaps] if isinstance(x, dict) else [x]
        picks.append((len(arrays), len(mine), isinstance(x, dict)))
        arrays += [*mine, *weight.arrays]
    first = terms[0][0]
    T = first[gaps[0]].shape[0] if isinstance(first, dict) else first.shape[0] // lax.axis_size("seq")
    widths = [weight.shape[1 if across else 0] for _, weight, across in terms]
    n_term, n_gap = len(terms), len(gaps)

    def body(at, *refs):
        n_out = 1 if ordered else n_gap
        ins, outs = refs[: len(arrays)], refs[len(arrays) : len(arrays) + n_out]
        scratch = refs[len(arrays) + n_out :]
        xs, ws, stages, sems = scratch[:n_term], scratch[n_term : 2 * n_term], scratch[2 * n_term : -1], scratch[-1]
        loads = Loads(sems)
        for (x, weight, across), (start, count, by_gap), x_ref, w_ref in zip(terms, picks, xs, ws):
            for n, gap in enumerate(gaps):
                if by_gap:
                    source = ins[start + n]
                else:
                    source = ins[start].at[pl.ds(block_row(at, gap, T), T)]
                loads.add("x", source, x_ref.at[pl.ds(n * T, T)])
            weight.load(loads, "w", at, ins[start + count : start + count + len(weight.arrays)], w_ref)
        loads.wait("x")
        loads.wait("w")
        for c in range(4):
            cut = slice(c * (D // 4), (c + 1) * (D // 4))
            total = None
            for (_, _, across), x_ref, w_ref in zip(terms, xs, ws):
                if across:
                    part = dot(x_ref[...], w_ref[cut, :], ((1,), (1,)))
                else:
                    part = dot(x_ref[...], w_ref[:, cut], ((1,), (0,)))
                total = part if total is None else total + part
            for n in range(n_gap):
                stages[n][:, cut] = total[n * T : (n + 1) * T].astype(stages[n].dtype)
        for n, gap in enumerate(gaps):
            target = outs[0].at[pl.ds(block_row(at, gap, T), T)] if ordered else outs[n]
            loads.add("out", stages[n], target)
        loads.wait("out")

    dtypes = [bf16 if gap & 1 or ordered else f32 for gap in gaps]
    outs = call(
        body,
        info,
        arrays,
        [like((n_gap * T, D), bf16)] if ordered else [like((T, D), dtype) for dtype in dtypes],
        [pltpu.VMEM((n_gap * T, width), bf16) for width in widths]
        + [pltpu.VMEM(weight.shape, bf16) for _, weight, _ in terms]
        + [pltpu.VMEM((T, D), dtype) for dtype in dtypes]
        + [pltpu.SemaphoreType.DMA((sum(w.copies for _, w, _ in terms) + (n_term + 1) * n_gap,))],
        name=name,
        after=after,
        cost=2 * n_gap * T * D * sum(widths),
    )
    return outs[0] if ordered else dict(zip(gaps, outs))


def feed_forward(info, hidden, cot, up, down, gaps, after=()):
    n_gap = len(gaps)
    T = hidden[0].shape[0]
    FW = up.shape[1]
    n_up, n_down = len(up.arrays), len(down.arrays)
    arrays = [*(hidden[gap] for gap in gaps), cot, *up.arrays, *down.arrays]

    def body(at, *refs):
        ins, outs = refs[: len(arrays)], refs[len(arrays) : len(arrays) + 3 * n_gap]
        x, g, w_up, w_down, acts, grads, *stages, sems = refs[len(arrays) + 3 * n_gap :]
        loads = Loads(sems)
        up.load(loads, "up", at, ins[n_gap + 1 : n_gap + 1 + n_up], w_up)
        for n in range(n_gap):
            loads.add(("x", n // 2), ins[n], x.at[pl.ds(n * T, T)])
        down.load(loads, "down", at, ins[n_gap + 1 + n_up :], w_down)
        for n, gap in enumerate(gaps):
            source = ins[n_gap].at[pl.ds(block_row(at, gap, T), T)]
            loads.add(("g", n // 2), source, g.at[pl.ds(n * T, T)])
        loads.wait("up")
        for n in range(0, n_gap, 2):
            rows = pl.ds(n * T, 2 * T)
            both = [(m, pl.ds(m * T, T)) for m in (n, n + 1)]
            loads.wait(("x", n // 2))
            pre = dot(x[rows], w_up[...], ((1,), (0,)))
            below = 0.5 * (1.0 + lax.erf(pre * 0.5**0.5))
            acts[rows] = (pre * below).astype(bf16)
            for m, part in both:
                loads.add("out", acts.at[part], outs[m])
            slope = below + pre * jnp.exp(-0.5 * pre * pre) * (0.5 / jnp.pi) ** 0.5
            if n == 0:
                loads.wait("down")
            loads.wait(("g", n // 2))
            grads[rows] = (dot(g[rows], w_down[...], ((1,), (1,))) * slope).astype(bf16)
            for m, part in both:
                loads.add("out", grads.at[part], outs[n_gap + m])
            for c in range(4):
                cut = slice(c * (D // 4), (c + 1) * (D // 4))
                result = dot(grads[rows], w_up[cut, :], ((1,), (1,)))
                for m, part in both:
                    value = result[(m - n) * T : (m - n + 1) * T]
                    stages[m][:, cut] = value.astype(stages[m].dtype)
            for m, part in both:
                loads.add("out", stages[m], outs[2 * n_gap + m])
        loads.wait("out")

    dtypes = [bf16 if gap & 1 else f32 for gap in gaps]
    outs = call(
        body,
        info,
        arrays,
        [like((T, FW), bf16)] * (2 * n_gap) + [like((T, D), dtype) for dtype in dtypes],
        [pltpu.VMEM((n_gap * T, D), bf16)] * 2
        + [pltpu.VMEM(up.shape, bf16), pltpu.VMEM(down.shape, bf16)]
        + [pltpu.VMEM((n_gap * T, FW), bf16)] * 2
        + [pltpu.VMEM((T, D), dtype) for dtype in dtypes]
        + [pltpu.SemaphoreType.DMA((up.copies + down.copies + 5 * n_gap,))],
        name="feed_forward",
        after=after,
        cost=6 * n_gap * T * D * FW,
    )
    return [dict(zip(gaps, outs[n * n_gap : (n + 1) * n_gap])) for n in range(3)]


class Term:
    def __init__(self, x, y, kind=1, shards=False, ordered=True):
        self.x, self.y, self.kind, self.shards, self.ordered = x, y, kind, shards, ordered
        some = x[0] if isinstance(x, dict) else x
        other = y[0] if isinstance(y, dict) else y
        self.tokens = some.shape[0] * (len(x) if isinstance(x, dict) else 1)
        self.columns = some.shape[1] // lax.axis_size("dp")
        self.rows, self.width = self.columns * kind, other.shape[1] // kind
        self.wide = other.shape[1]
        self.xs = list(x.values()) if isinstance(x, dict) else [x]
        self.ys = list(y.values()) if isinstance(y, dict) else [y]
        self.whole = self.columns % 128 != 0
        if self.whole:
            product = dot(self.rows_of(x), self.rows_of(y), ((0,), (0,)))
            self.xs, self.ys = [product.astype(bf16)], []

    def rows_of(self, held):
        if not isinstance(held, dict):
            return held
        rows = held[0].shape[0]
        out = jnp.zeros((len(held) * rows, held[0].shape[1]), bf16)
        for gap, part in held.items():
            start = (lax.axis_index("seq") ^ gap if self.ordered else gap) * rows
            out = lax.dynamic_update_slice_in_dim(out, part, start, 0)
        return out

    def spread(self, at, which, refs, target, cols=None):
        held = self.x if which == "x" else self.y
        for gap, ref in zip(held if isinstance(held, dict) else [None], refs):
            source = ref if cols is None else ref.at[:, cols]
            if gap is None:
                yield source, target
                continue
            rows = ref.shape[0]
            start = block_row(at, gap, rows) if self.ordered else gap * rows
            yield source, target.at[pl.ds(start, rows)]


class Scatter:
    def __init__(self, info, terms, name):
        self.info, self.terms, self.name = info, terms, name
        self.size = lax.axis_size("dp")
        self.ahead, self.back = ring_moves(self.size)
        self.rows = terms[0].rows
        self.cols = sum(term.width for term in terms)
        self.hop = 0
        self.last = ()

    def pieces(self, which, got, write, outs, after=()):
        terms, n_got, n_out, n_w = self.terms, len(got), len(outs), len(which)
        arrays = [a for term in terms for a in (*term.xs, *term.ys)]

        def body(at, *refs):
            ins, recvs = refs[: len(arrays)], refs[len(arrays) : len(arrays) + n_got]
            results = refs[len(arrays) + n_got : len(arrays) + n_got + n_out]
            scratch, sems = refs[len(arrays) + n_got + n_out : -1], refs[-1]
            held = scratch[:n_got]
            buffers = scratch[n_got:]
            loads = Loads(sems)
            start = 0
            for i, term in enumerate(terms):
                x_refs = ins[start : start + len(term.xs)]
                y_refs = ins[start + len(term.xs) : start + len(term.xs) + len(term.ys)]
                start += len(term.xs) + len(term.ys)
                y_buf, x_buf = buffers[2 * i : 2 * i + 2]
                for n, k in enumerate(which):
                    mine = pl.ds(n * term.columns, term.columns)
                    x_part = x_buf.at[mine] if term.whole else x_buf.at[:, mine]
                    place = at[1 + k + (self.size if term.shards else 0)]
                    cols = pl.ds(pl.multiple_of(place * term.columns, term.columns), term.columns)
                    if term.whole:
                        loads.add(i, x_refs[0].at[cols], x_part)
                        continue
                    for source, target in term.spread(at, "x", x_refs, x_part, cols):
                        loads.add(i, source, target)
                for source, target in term.spread(at, "y", y_refs, y_buf) if y_refs else ():
                    loads.add(i, source, target)
            for source, target in zip(recvs, held):
                loads.add("got", source, target)
            column = 0
            for i, term in enumerate(terms):
                y_buf, x_buf = buffers[2 * i : 2 * i + 2]
                loads.wait(i)
                for c in range(term.kind):
                    cols = slice(c * term.width, (c + 1) * term.width)
                    if term.whole:
                        values = x_buf[:, cols].astype(f32)
                    else:
                        values = dot(x_buf[...], y_buf[:, cols], ((0,), (0,)))
                    loads.wait("got")
                    for n in range(n_w):
                        piece = values[n * term.columns : (n + 1) * term.columns]
                        write(n, c * term.columns, term.columns, column, piece, held, results)
                column += term.width

        scratch = [pltpu.VMEM(x.shape, x.dtype) for x in got]
        for term in terms:
            scratch += [pltpu.VMEM((8, 128) if term.whole else (term.tokens, term.wide), bf16)]
            many = n_w * term.columns
            scratch += [pltpu.VMEM((many, term.wide) if term.whole else (term.tokens, many), bf16)]
        copies = n_got + sum(n_w * len(t.xs) + len(t.ys) for t in terms)
        return call(
            body,
            self.info,
            [*arrays, *got],
            outs,
            [*scratch, pltpu.SemaphoreType.DMA((copies,))],
            in_specs=[ANY] * (len(arrays) + n_got),
            out_specs=[VMEM] * n_out,
            name=self.name,
            after=after,
            cost=2 * n_w * sum(t.tokens * t.columns * t.wide for t in terms),
        )

    def step(self, *after):
        m, rows, half = self.size // 2, self.rows, self.rows // 2
        k = m - self.hop
        self.hop += 1

        def write(n, row, count, column, values, got, outs):
            width = values.shape[1]
            for side in range(2) if k == m else [n]:
                for lo, hi in ((0, half), (half, rows)):
                    low, high = max(row, lo), min(row + count, hi)
                    if low >= high or (k == m and lo != side * half):
                        continue
                    part = values[low - row : high - row]
                    cols = slice(column, column + width)
                    if k < m - 1:
                        part = part + got[n][low:high, cols].astype(f32)
                    elif k == m - 1 and lo == n * half:
                        part = part + got[n][low - lo : high - lo, cols].astype(f32)
                    at = lo if k == m else 0
                    outs[side][low - at : high - at, cols] = part.astype(bf16)

        shape = like((half if k == m else rows, self.cols), bf16)
        which = [m] if k == m else [k, self.size - k]
        a, b = self.pieces(which, self.last, write, [shape, shape], after)
        self.sent = (a, b)
        self.last = (lax.ppermute(a, "dp", self.back), lax.ppermute(b, "dp", self.ahead))
        return self

    def own(self, widths, dtypes, after=()):
        while self.hop < self.size // 2:
            self.step()

        def write(n, row, count, column, values, got, outs):
            width = values.shape[1]
            total = values
            for ref in got:
                total = total + ref[row : row + count, column : column + width].astype(f32)
            start = 0
            for out, wide in zip(outs, widths):
                low, high = max(start, column), min(start + wide, column + width)
                if low < high:
                    part = total[:, low - column : high - column]
                    out[row : row + count, low - start : high - start] = part.astype(out.dtype)
                start += wide

        outs = [like((self.rows, w), t) for w, t in zip(widths, dtypes)]
        return self.pieces([0], self.last, write, outs, after)


def split_columns(info, proj_in, ffn_up, H, QW, VW, FW):
    size = lax.axis_size("seq")
    rows, G = proj_in.shape[0], lax.axis_size("dp")
    FR = FW // G
    aligned = FR % 128 == 0
    if not aligned:
        ffn_up = ffn_up.reshape(rows, G, size, FR).transpose(0, 2, 1, 3).reshape(rows, size * FW)

    def body(at, w_in, w_up, *outs):
        for gap in range(size):
            who = at[0] ^ gap
            qkv, gate = outs[2 * gap : 2 * gap + 2]
            for h in range(H):
                for n in range(2):
                    src = pl.multiple_of(n * D + (who * H + h) * DK, DK)
                    qkv[:, (2 * h + n) * DK : (2 * h + n + 1) * DK] = w_in[:, pl.ds(src, DK)]
            qkv[:, 2 * QW :] = w_in[:, pl.ds(pl.multiple_of(2 * D + who * VW, VW), VW)]
            gate[:, :VW] = w_in[:, pl.ds(pl.multiple_of(2 * D + VD + who * VW, VW), VW)]
            if not aligned:
                gate[:, VW:] = w_up[:, pl.ds(pl.multiple_of(who * FW, FW), FW)]
                continue
            for i in range(G):
                src = pl.multiple_of((i * size + who) * FR, FR)
                gate[:, VW + i * FR : VW + (i + 1) * FR] = w_up[:, pl.ds(src, FR)]

    outs = [like((rows, 2 * QW + VW), bf16), like((rows, VW + FW), bf16)] * size
    return call(
        body,
        info,
        [proj_in, ffn_up],
        outs,
        in_specs=[VMEM] * 2,
        out_specs=[VMEM] * len(outs),
        name="split_columns",
    )


def join_pieces(info, parts, extra, fold, after=(), first=0, width=None):
    size = len(parts)
    rows, width = parts[0].shape[0], width or parts[0].shape[1]
    wide = 0 if extra is None else extra.shape[1] // fold

    def body(at, *refs):
        out = refs[-1]
        for gap in range(size):
            out[pl.ds(pl.multiple_of((at[0] ^ gap) * rows, rows), rows), :width] = refs[gap][:, first : first + width]
        if extra is not None:
            short = size * rows // fold
            for c in range(fold):
                out[c * short : (c + 1) * short, width:] = refs[size][:, c * wide : (c + 1) * wide]

    ins = parts if extra is None else [*parts, extra]
    return call(
        body,
        info,
        ins,
        like((size * rows, width + wide), bf16),
        in_specs=[VMEM] * len(ins),
        out_specs=VMEM,
        name="join_pieces",
        after=after,
    )


def exchange_rows(info, x):
    size = lax.axis_size("seq")
    rows = x.shape[0] // size

    def body(at, src, *outs):
        for gap in range(size):
            outs[gap][...] = src[pl.ds(pl.multiple_of((at[0] ^ gap) * rows, rows), rows), :]

    outs = [like((rows, x.shape[1]), x.dtype)] * size
    parts = call(
        body, info, [x], outs, in_specs=[VMEM], out_specs=[VMEM] * size, name="exchange_rows"
    )
    return [part if gap == 0 else swap_seq(part, gap) for gap, part in enumerate(parts)]


def join_in_columns(info, qkvs, gates, H, QW, VW, after=()):
    size = len(qkvs)
    rows = qkvs[0].shape[0]

    def body(at, *refs):
        out = refs[-1]
        for gap in range(size):
            who = at[0] ^ gap
            qkv, gate = refs[gap], refs[size + gap]
            for h in range(H):
                for n in range(2):
                    to = pl.multiple_of(n * D + (who * H + h) * DK, DK)
                    part = qkv[:, (2 * h + n) * DK : (2 * h + n + 1) * DK]
                    out[:, pl.ds(to, DK)] = part.astype(f32)
            out[:, pl.ds(pl.multiple_of(2 * D + who * VW, VW), VW)] = qkv[:, 2 * QW :].astype(f32)
            to = pl.multiple_of(2 * D + VD + who * VW, VW)
            out[:, pl.ds(to, VW)] = gate[...].astype(f32)

    ins = [*qkvs, *gates]
    return call(
        body,
        info,
        ins,
        like((rows, 2 * D + 2 * VD), f32),
        in_specs=[VMEM] * len(ins),
        out_specs=VMEM,
        name="join_in_columns",
        after=after,
    )


def join_up_columns(info, ups, G, after=()):
    size = len(ups)
    rows, FW = ups[0].shape
    FR = FW // G
    aligned = FR % 128 == 0

    def body(at, *refs):
        out = refs[-1]
        for gap in range(size):
            who = at[0] ^ gap
            if not aligned:
                to = pl.multiple_of(who * FW, FW)
                out[:, pl.ds(to, FW)] = refs[gap][...].astype(f32)
                continue
            for i in range(G):
                to = pl.multiple_of((i * size + who) * FR, FR)
                out[:, pl.ds(to, FR)] = refs[gap][:, i * FR : (i + 1) * FR].astype(f32)

    out = call(
        body,
        info,
        ups,
        like((rows, size * FW), f32),
        in_specs=[VMEM] * size,
        out_specs=VMEM,
        name="join_up_columns",
        after=after,
    )
    if aligned:
        return out
    return out.reshape(rows, size, G, FR).transpose(0, 2, 1, 3).reshape(rows, size * FW)


def decays(log_decay, T):
    step = lax.broadcasted_iota(jnp.int32, (T, 1), 0).astype(f32)
    decay_query = jnp.exp((step + 1.0) * log_decay)
    decay_key = jnp.exp((T - 1.0 - step) * log_decay)
    row = lax.broadcasted_iota(jnp.int32, (T, T), 0)
    column = lax.broadcasted_iota(jnp.int32, (T, T), 1)
    gap = (row - column).astype(f32)
    lower = row >= column
    mask = jnp.where(lower, jnp.exp(jnp.where(lower, gap, 0.0) * log_decay), 0.0)
    return decay_query, decay_key, mask


def turn(u, cosine, sine):
    a, c = u[:, :HALF], u[:, HALF:]
    return jnp.concatenate([a * cosine - c * sine, a * sine + c * cosine], axis=1)


def centre(retained):
    average = jnp.mean(retained, axis=-1, keepdims=True)
    centred = retained - average
    spread = jnp.mean(centred * centred, axis=-1, keepdims=True)
    inverse = lax.rsqrt(jnp.maximum(spread, 0.25) + 1e-05)
    return centred, spread, inverse


def retention_forward(info, logs, keep, qk, v, gate, cosine, sine, S, T, H, after=()):
    TG = S * T

    def body(_, logs_ref, keep_ref, qk_ref, v_ref, g_ref, cos_ref, sin_ref, *outs):
        mixed, qk_out, retained_out, state_out, scores_out = outs
        log_decay = logs_ref[pl.program_id(0)]
        decay_query, decay_key, mask = decays(log_decay, T)
        block_decay = jnp.exp(jnp.full((1, 1), T * log_decay, f32))
        carry = jnp.zeros((DK, DV), f32)
        for b in range(S):
            rows = pl.ds(b * T, T)
            co, si = cos_ref[rows], sin_ref[rows]
            q = turn(qk_ref[rows, :DK], co, si).astype(bf16)
            k = (turn(qk_ref[rows, DK:], co, si) * DK ** (-0.5)).astype(bf16)
            qk_out[rows, :DK] = q
            qk_out[rows, DK:] = k
            value = v_ref[rows]
            scores = (dot(q, k, ((1,), (1,))) * mask).astype(bf16)
            scores_out[0, b] = scores
            state = keep_ref[b] * carry
            state_in = state.astype(bf16)
            state_out[0, b] = state_in
            query_decay = (q.astype(f32) * decay_query).astype(bf16)
            key_decay = (k.astype(f32) * decay_key).astype(bf16)
            retained = dot(scores, value, ((1,), (0,))) + dot(query_decay, state_in, ((1,), (0,)))
            retained_out[rows] = retained
            carry = block_decay * state + dot(key_decay, value, ((0,), (0,)))
            centred, _, inverse = centre(retained)
            g = g_ref[rows]
            mixed[rows] = (g * jax.nn.sigmoid(g) * (centred * inverse)).astype(bf16)

    smem = pl.BlockSpec(memory_space=pltpu.SMEM)
    once = lambda width: pl.BlockSpec((TG, width), lambda h, _: (0, 0))
    head = lambda width: pl.BlockSpec((TG, width), lambda h, _: (0, h))
    return call(
        body,
        info,
        [logs, keep, qk, v, gate, cosine, sine],
        [
            like((TG, H * DV), bf16),
            like((TG, 2 * H * DK), bf16),
            like((TG, H * DV), f32),
            like((H, S, DK, DV), bf16),
            like((H, S, T, T), bf16),
        ],
        grid=(H,),
        in_specs=[smem, smem, head(2 * DK), head(DV), head(DV), once(HALF), once(HALF)],
        out_specs=[
            head(DV),
            head(2 * DK),
            head(DV),
            pl.BlockSpec((1, S, DK, DV), lambda h, _: (h, 0, 0, 0)),
            pl.BlockSpec((1, S, T, T), lambda h, _: (h, 0, 0, 0)),
        ],
        name="retention_forward",
        after=after,
        cost=2 * H * S * T * T * (DK + DV) + 4 * H * S * T * DK * DV,
    )


def retention_backward(info, logs, keep, grad_mixed, gate, retained, qk, v, states, scores, cosine, sine, S, T, H, after=()):
    TG = S * T

    def body(_, logs_ref, keep_ref, gm_ref, g_ref, r_ref, qk_ref, v_ref, state_ref, scores_ref, cos_ref, sin_ref, *outs):
        qk_grad, v_grad, g_grad = outs
        log_decay = logs_ref[pl.program_id(0)]
        decay_query, decay_key, mask = decays(log_decay, T)
        block_decay = jnp.exp(jnp.full((1, 1), T * log_decay, f32))
        later = jnp.zeros((DK, DV), f32)
        for b in reversed(range(S)):
            rows = pl.ds(b * T, T)
            gm, g = gm_ref[rows], g_ref[rows]
            centred, spread, inverse = centre(r_ref[rows])
            sig = jax.nn.sigmoid(g)
            swish = g * sig
            normed = centred * inverse
            g_grad[rows] = (gm * normed * (sig + swish * (1.0 - sig))).astype(bf16)
            grad_normed = gm * swish
            passes = jnp.where(spread > 0.25, 1.0, jnp.where(spread == 0.25, 0.5, 0.0))
            pull = jnp.sum(grad_normed * centred, axis=-1, keepdims=True)
            pull = pull * (-inverse * inverse * inverse / DV) * passes
            grad_centred = grad_normed * inverse + pull * centred
            grad_ret = grad_centred - jnp.mean(grad_centred, axis=-1, keepdims=True)
            grad_ret = grad_ret.astype(bf16)
            q, k, value = qk_ref[rows, :DK], qk_ref[rows, DK:], v_ref[rows]
            query_decay = (q.astype(f32) * decay_query).astype(bf16)
            key_decay = (k.astype(f32) * decay_key).astype(bf16)
            grad_raw = (dot(grad_ret, value, ((1,), (1,))) * mask).astype(bf16)
            local = later.astype(bf16)
            grad_q = dot(grad_raw, k, ((1,), (0,)))
            grad_q = grad_q + decay_query * dot(grad_ret, state_ref[0, b], ((1,), (1,)))
            grad_k = dot(grad_raw, q, ((0,), (0,)))
            grad_k = grad_k + decay_key * dot(value, local, ((1,), (1,)))
            grad_v = dot(scores_ref[0, b], grad_ret, ((0,), (0,)))
            grad_v = grad_v + dot(key_decay, local, ((1,), (0,)))
            co, si = cos_ref[rows], -sin_ref[rows]
            qk_grad[rows, :DK] = turn(grad_q, co, si).astype(bf16)
            qk_grad[rows, DK:] = turn(grad_k * DK ** (-0.5), co, si).astype(bf16)
            v_grad[rows] = grad_v.astype(bf16)
            if b > 0:
                here = dot(query_decay, grad_ret, ((0,), (0,)))
                later = keep_ref[b] * (here + block_decay * later)

    smem = pl.BlockSpec(memory_space=pltpu.SMEM)
    once = lambda width: pl.BlockSpec((TG, width), lambda h, _: (0, 0))
    head = lambda width: pl.BlockSpec((TG, width), lambda h, _: (0, h))
    return call(
        body,
        info,
        [logs, keep, grad_mixed, gate, retained, qk, v, states, scores, cosine, sine],
        [like((TG, 2 * H * DK), bf16), like((TG, H * DV), bf16), like((TG, H * DV), bf16)],
        grid=(H,),
        in_specs=[
            smem,
            smem,
            head(DV),
            head(DV),
            head(DV),
            head(2 * DK),
            head(DV),
            pl.BlockSpec((1, S, DK, DV), lambda h, _: (h, 0, 0, 0)),
            pl.BlockSpec((1, S, T, T), lambda h, _: (h, 0, 0, 0)),
            once(HALF),
            once(HALF),
        ],
        out_specs=[head(2 * DK), head(DV), head(DV)],
        name="retention_backward",
        after=after,
        cost=4 * H * S * T * T * (DK + DV) + 8 * H * S * T * DK * DV,
    )


def local(
    layer_in,
    out_grad,
    seq_start,
    norm1_gain,
    norm1_shift,
    proj_in,
    proj_out,
    norm2_gain,
    norm2_shift,
    ffn_up,
    ffn_down,
):
    S, G = lax.axis_size("seq"), lax.axis_size("dp")
    me = lax.axis_index("seq")
    T = layer_in.shape[0]
    TG = S * T
    H = HEADS // S
    QW, VW = H * DK, H * DV
    FW = G * ffn_down.shape[0]
    fold = S // 2
    info = make_info()

    to_rank = [(j * G + t, shard_place(t, G) * S + j) for j in range(S) for t in range(G)]
    parts = split_columns(info, proj_in, ffn_up, H, QW, VW, FW)

    vectors = jnp.stack([norm1_gain, norm1_shift, norm2_gain, norm2_shift])
    norms = GatherAll(tie(vectors, parts[0]))
    while norms.gaps:
        norms.step()
    norms = norms.held.transpose(2, 0, 1, 3).reshape(4, 1, D).astype(f32)
    gain_one, shift_one, gain_two, shift_two = norms

    out_piece = lax.ppermute(tie(proj_out, norms), BOTH, to_rank)

    def exchanged(own, *after):
        return [own[0]] + [
            swap_seq(tie(x, *after) if after else x, gap) for gap, x in enumerate(own) if gap
        ]

    qkv_parts = exchanged(parts[0::2])
    qkv_ring = Gather(join_pieces(info, qkv_parts, None, fold, (norms,))).step()
    (normed_one,) = norm_forward(layer_in, gain_one, shift_one, (), (qkv_ring.got[0],))
    hidden_one = gather_seq(normed_one)
    early = (*qkv_ring.last, hidden_one[S // 2])
    qkv_ring.step()
    gate_parts = exchanged(parts[1::2], *early)
    cot = lax.all_gather(tie(out_grad, *early), "seq", axis=0, tiled=True)
    qkv_ring.step().step()
    gate_piece = join_pieces(
        info, gate_parts, None, fold, (*qkv_ring.sent, hidden_one[1], hidden_one[S - 1]), 0, VW
    )
    gate_ring = Gather(gate_piece).step().step(*qkv_ring.last)
    out_ring = Gather(tie(out_piece, *gate_ring.sent)).step()

    factor = jnp.power(10000.0, -jnp.arange(HALF, dtype=f32) / (HALF - 1))
    angles = jnp.arange(TG, dtype=f32)[:, None] * factor[None, :]
    cosine, sine = jnp.cos(angles), jnp.sin(angles)
    log_all = jnp.log(1.0 - jnp.exp2(-5.0 - jnp.arange(HEADS, dtype=f32)))
    logs = lax.dynamic_slice_in_dim(log_all, me * H, H)
    keep = 1.0 - seq_start[0].astype(f32)

    w_qkv = Weight(qkv_ring)
    qk_pre, values = tokens_times(
        info,
        hidden_one,
        w_qkv,
        [(0, 2 * QW, f32), (2 * QW, VW, bf16)],
        False,
        "project_qkv",
        (*gate_ring.sent, *out_ring.sent, cosine, sine),
    )
    w_qk = Weight(qkv_ring, 1, 0, 2 * QW)
    w_v = Weight(qkv_ring, 1, 2 * QW, VW)
    gate_ring.step(qk_pre)
    out_ring.step(qk_pre)
    gate_ring.step()
    out_ring.step()
    w_g = Weight(gate_ring)
    (gate_pre,) = tokens_times(
        info, hidden_one, w_g, [(0, VW, f32)], False, "project_gate", out_ring.sent
    )
    out_ring.step(gate_pre)
    ffn_ring = Gather(join_pieces(info, gate_parts, ffn_down, fold, out_ring.sent, VW, FW)).step()
    mixed, qk, retained, states, scores = retention_forward(
        info, logs, keep, qk_pre, values, gate_pre, cosine, sine, S, T, H,
        (*out_ring.sent, ffn_ring.got[0]),
    )
    w_out = Weight(out_ring, shards=True)
    odd, even = [g for g in reversed(range(S)) if g & 1], [g for g in reversed(range(S)) if not g & 1]
    ffn_ring.step()
    attn, attn_got = partial_rows(info, [(mixed, w_out, False)], odd, "attn_odd", (ffn_ring.got[0],)), {}
    swap_odd(attn, attn_got)
    attn |= partial_rows(info, [(mixed, w_out, False)], even, "attn_even", (attn[odd[-1]],))
    attn, attn_sent = scatter_seq(attn, attn_got)
    ffn_ring.step()
    middle, normed_two = norm_forward(layer_in, gain_two, shift_two, attn, ffn_ring.sent)
    ffn_ring.step()
    w_up = Weight(ffn_ring, 1, 0, FW)
    w_down = Weight(ffn_ring, fold, FW, 2 * D // S)
    near, far = [1, 0], list(reversed(range(2, S)))
    hidden_two = {0: normed_two, 1: swap_seq(normed_two, 1)}
    active, grad_up, grad_two = feed_forward(info, hidden_two, cot, w_up, w_down, near)
    hidden_two |= far_blocks(normed_two)
    two_got = {}
    swap_odd(grad_two, two_got)
    more = feed_forward(info, hidden_two, cot, w_up, w_down, far, (grad_two[0],))
    swap_odd(more[2], two_got)
    for whole, extra in zip((active, grad_up, grad_two), more):
        whole |= extra

    grad_two, two_sent = scatter_seq(grad_two, two_got)
    order = sorted(active)
    active, grad_up, hidden_two, hidden_one = (
        {gap: x[gap] for gap in order} for x in (active, grad_up, hidden_two, hidden_one)
    )
    ffn_sum = Scatter(
        info,
        [Term(hidden_two, grad_up), Term(active, cot, fold)],
        "ffn_hop",
    ).step(two_sent).step()
    grad_middle, grad_attn, two_sums = norm_backward(
        middle, gain_two, out_grad, grad_two, (f32, bf16), ffn_sum.sent
    )

    down = partial_rows(
        info, [(active, w_down, False)], odd + even, "down", (grad_attn,), True
    )
    grad_attn = gather_seq(grad_attn, down, *ffn_sum.last)
    ffn_sum.step(grad_attn[S // 2])
    (grad_mixed,) = tokens_times(info, grad_attn, w_out, [(0, VW, f32)], True, "grad_mixed", ffn_sum.sent)
    down = lax.psum_scatter(tie(down, *ffn_sum.sent), "seq", scatter_dimension=0, tiled=True)
    grad_qk, grad_v, grad_g = retention_backward(
        info, logs, keep, grad_mixed, gate_pre, retained, qk, values, states, scores, cosine, sine, S, T, H,
        ffn_sum.sent,
    )
    gate_sum = Scatter(
        info, [Term(hidden_one, grad_g), Term(mixed, grad_attn, fold, True)], "gate_hop"
    ).step(grad_g)
    ffn_sum.step(*gate_sum.sent)
    qkv_sum = Scatter(info, [Term(hidden_one, grad_qk), Term(hidden_one, grad_v)], "qkv_hop")
    qkv_sum.step(*ffn_sum.sent)
    terms_one = [(grad_g, w_g, True), (grad_v, w_v, True), (grad_qk, w_qk, True)]
    grad_one, one_got = partial_rows(info, terms_one, odd, "grad_one_odd", qkv_sum.sent), {}
    swap_odd(grad_one, one_got)
    gate_sum.step(grad_one[odd[-1]])
    grad_one |= partial_rows(info, terms_one, even, "grad_one_even", gate_sum.sent)
    grad_one, one_sent = scatter_seq(grad_one, one_got)
    qkv_sum.step(one_sent)
    up_own, down_own = ffn_sum.own((FW, 2 * D // S), (bf16, f32), qkv_sum.sent)
    up_parts = exchange_rows(info, up_own)
    layer_out = add_up([down, middle], bf16, (up_parts[0],))
    gate_sum.step(layer_out)
    in_grad, one_sums = norm_backward(
        layer_in, gain_one, grad_middle, grad_one, (bf16,), gate_sum.sent
    )
    norm_terms = jnp.stack([one_sums[0], one_sums[1], two_sums[0], two_sums[1]])
    down_grad = jnp.concatenate(jnp.split(tie(down_own, in_grad), fold, axis=0), axis=1)
    qkv_sum.step(in_grad)
    gate_sum.step(*qkv_sum.sent)
    up_grad = join_up_columns(info, up_parts, G, gate_sum.sent)
    norm_sum = ScatterAll(norm_terms.reshape(4, G, S, -1).transpose(1, 2, 0, 3))
    for _ in seq_gaps(S):
        norm_sum.step()
    qkv_sum.step(up_grad, norm_sum.held)
    g_own, out_own = gate_sum.own((VW, 2 * D // S), (bf16, bf16), qkv_sum.sent)
    g_parts = exchange_rows(info, g_own)
    out_grad_w = lax.ppermute(out_own, BOTH, [(b, a) for a, b in to_rank])
    (qkv_own,) = qkv_sum.own((2 * QW + VW,), (bf16,), (g_parts[0],))
    qkv_parts = exchange_rows(info, qkv_own)
    norm_sum.held = tie(norm_sum.held, qkv_parts[S // 2], out_grad_w)
    while norm_sum.gaps:
        norm_sum.step()
    norm_grads = norm_sum.held[0, 0]
    in_grad_w = join_in_columns(info, qkv_parts, g_parts, H, QW, VW)
    out_grad_w = jnp.concatenate(jnp.split(out_grad_w, fold, axis=0), axis=1).astype(f32)
    return (
        layer_out,
        in_grad,
        norm_grads[0],
        norm_grads[1],
        in_grad_w,
        out_grad_w,
        norm_grads[2],
        norm_grads[3],
        up_grad,
        down_grad,
    )


def solution(mesh):
    rows, vector = P(BOTH, None), P(BOTH)
    in_specs = (rows, rows, P("dp", None), vector, vector, rows, rows, vector, vector, rows, rows)
    out_specs = (rows, rows, vector, vector, rows, rows, vector, vector, rows, rows)
    return jax.shard_map(local, mesh=mesh, in_specs=in_specs, out_specs=out_specs, check_vma=False)
```
